1024 devices in a mesh: elem: 128 (over z, x), grp: 8 (over y, core).
Axes of the slice: x: 4, y: 4, z: 32, core: 2. Of those that a mesh axis runs over, the one named last changes fastest.
Arguments:
- state: float32 [8192, 6, 512], P(('elem', 'grp')), may hold values from -6 to 20, as said below
- material: int32 [8192], P(('elem', 'grp')), may hold values from 0 to 1
- metric: float32 [8192], P(('elem', 'grp')), may hold values from 1 to 4
- mortar_proj: float32 [4, 64, 64], replicated, may hold values from 0 to 1, as said below
- mortar_map: int32 [1024, 4, 128], P(('elem', 'grp')), may hold values from 0 to 7, as said below
- mortar_count: int32 [1024, 10], P(('elem', 'grp')), may hold values from 0 to 32, as said below
- neighbours: int32 [8192, 6], P(('elem', 'grp')), may hold values from -1 to 7, as said below
Outputs:
- new_state: float32 [8192, 6, 512], P(('elem', 'grp'))
The draws below stay inside these ranges and needn't reach their ends.
Inputs may be any that keep to these rules, and one draw needn't show every extreme that they name: `state`: density and pressure, with either heat ratio, are positive at every node. `mortar_proj`: entries are nonnegative and every row sums to one. `mortar_map`: Rows: local element, face (0 to 5), subface (0 conforming, 1 to 4 a quadrant of a coarse face), orientation (0 to 7). Slot s below 64 pairs with slot (own grp index) * 8 + s % 8 of the device with the same elem index and grp index s // 8; the next 32 slots pair, position by position, with the last 32 slots of the device one elem index higher, the last 32 with the middle 32 of the device one elem index lower, same grp index. Paired faces lie along one dimension with opposite normals; at most one side of a pair has a nonzero subface. `mortar_count`: entry g below 8 counts the live slots toward grp peer g, 0 for the device itself, equal to the peer's entry for this device, at most 8 and reaching it on some devices; entry 8 toward the next elem index equals that device's entry 9; the top elem index has 0 in entry 8, the bottom one 0 in entry 9. Slots at positions below the count are live. `neighbours`: local element across the face, meeting its opposite face, or -1.
All inputs are finite; a program needn't handle non-finite values.
Results may differ from the reference program's by a relative error of at most 0.0003.
Values sent between devices are 32-bit elements; how exact they have to be, the bound alone decides.
No kernel may reach another device: no remote copies, remote signals or barrier semaphores. Data moves between devices by JAX's collectives and lax.ppermute only.
A program may use at most 64 MiB of HBM per device.

```python
import math
import jax
import jax.numpy as jnp
import numpy as np
from jax import lax

NV = 6
NP = 8
FN = 64
VN = 512
SUBS = 4
EL_DEV = 8
CAPG = 8
CAPS = 32
SLOTS = 128
ELEMS = 8192
N_ELEM = 128
N_GRP = 8
DEVICES = 1024


def draw_state(key, part):
    keys = jax.random.split(key, 4)
    density = jnp.exp(jax.random.uniform(keys[0], (ELEMS, VN), jnp.float32, math.log(0.5), math.log(2.0)))
    velocity = jnp.clip(0.5 * jax.random.normal(keys[1], (ELEMS, 3, VN), jnp.float32), -2.0, 2.0)
    pressure = jnp.exp(jax.random.uniform(keys[2], (ELEMS, VN), jnp.float32, math.log(0.5), math.log(2.0)))
    scalar = jax.random.uniform(keys[3], (ELEMS, VN), jnp.float32)
    energy = pressure / 0.4 + 0.5 * density * jnp.sum(velocity * velocity, axis=1)
    return jnp.concatenate([density[:, None], density[:, None] * velocity, energy[:, None], (density * scalar)[:, None]], axis=1)


def draw_mortar_proj(key, part):
    spread = jax.random.uniform(key, (SUBS, FN, FN), jnp.float32)
    spread = spread / jnp.sum(spread, axis=2, keepdims=True)
    return 0.6 * jnp.eye(FN, dtype=jnp.float32)[None] + 0.4 * spread


def link_tables(key):
    base = jax.random.fold_in(key, 7331)
    keys = jax.random.split(base, 8)
    grp_shape = (N_ELEM, N_GRP, N_GRP, CAPG)
    up_shape = (N_ELEM, N_GRP, CAPS)
    grp_code = jax.random.randint(keys[0], grp_shape, 0, 6, jnp.int32)
    grp_kind = jax.random.randint(keys[1], grp_shape, 0, 3, jnp.int32)
    grp_sub = jax.random.randint(keys[2], grp_shape, 1, 5, jnp.int32)
    grp_level = jax.random.randint(keys[3], (N_ELEM, N_GRP, N_GRP), 0, 4, jnp.int32)
    up_code = jax.random.randint(keys[4], up_shape, 0, 6, jnp.int32)
    up_kind = jax.random.randint(keys[5], up_shape, 0, 3, jnp.int32)
    up_sub = jax.random.randint(keys[6], up_shape, 1, 5, jnp.int32)
    up_level = jax.random.randint(keys[7], (N_ELEM, N_GRP), 0, 4, jnp.int32)
    return (grp_code, grp_kind, grp_sub, grp_level, up_code, up_kind, up_sub, up_level)


def draw_mortar_count(key, part):
    grp_code, grp_kind, grp_sub, grp_level, up_code, up_kind, up_sub, up_level = link_tables(key)
    order = jnp.arange(N_GRP, dtype=jnp.int32)
    low_index = jnp.minimum(order[:, None], order[None, :])
    high_index = jnp.maximum(order[:, None], order[None, :])
    level = grp_level[:, low_index, high_index]
    pinned = (low_index == 0) & (high_index == 1)
    level = jnp.where(pinned[None], 0, level)
    grp_count = CAPG * jnp.right_shift(jnp.int32(8), level) // 8
    grp_count = jnp.where((order[:, None] == order[None, :])[None], 0, grp_count)
    elem_order = jnp.arange(N_ELEM, dtype=jnp.int32)
    first = (elem_order[:, None] == 0) & (order[None, :] == 0)
    link_level = jnp.where(first, 0, up_level)
    link = CAPS * jnp.right_shift(jnp.int32(8), link_level) // 8
    link = jnp.where((elem_order == N_ELEM - 1)[:, None], 0, link)
    below = jnp.concatenate([jnp.zeros((1, N_GRP), jnp.int32), link[:-1]], axis=0)
    table = jnp.concatenate([grp_count, link[:, :, None], below[:, :, None]], axis=2)
    return table.reshape(DEVICES, N_GRP + 2).astype(jnp.int32)


def draw_mortar_map(key, part):
    grp_code, grp_kind, grp_sub, grp_level, up_code, up_kind, up_sub, up_level = link_tables(key)
    order = jnp.arange(N_GRP, dtype=jnp.int32)
    low_index = jnp.minimum(order[:, None], order[None, :])
    high_index = jnp.maximum(order[:, None], order[None, :])
    code = grp_code[:, low_index, high_index]
    kind = grp_kind[:, low_index, high_index]
    quadrant = grp_sub[:, low_index, high_index]
    is_lower = (order[:, None] < order[None, :])[None, :, :, None]
    grp_face = jnp.where(is_lower, code, jnp.bitwise_xor(code, 1)).reshape(N_ELEM, N_GRP, N_GRP * CAPG)
    grp_subs = jnp.where(is_lower & (kind == 1) | jnp.logical_not(is_lower) & (kind == 2), quadrant, 0).reshape(N_ELEM, N_GRP, N_GRP * CAPG)
    up_face = up_code
    up_subs = jnp.where(up_kind == 1, up_sub, 0)
    code_below = jnp.concatenate([jnp.zeros_like(up_code[:1]), up_code[:-1]], axis=0)
    kind_below = jnp.concatenate([jnp.zeros_like(up_kind[:1]), up_kind[:-1]], axis=0)
    sub_below = jnp.concatenate([jnp.zeros_like(up_sub[:1]), up_sub[:-1]], axis=0)
    down_face = jnp.bitwise_xor(code_below, 1)
    down_subs = jnp.where(kind_below == 2, sub_below, 0)
    face = jnp.concatenate([grp_face, up_face, down_face], axis=2)
    subface = jnp.concatenate([grp_subs, up_subs, down_subs], axis=2)
    element = jax.random.randint(jax.random.fold_in(key, 11), (N_ELEM, N_GRP, SLOTS), 0, EL_DEV, jnp.int32)
    orient = jax.random.randint(jax.random.fold_in(key, 13), (N_ELEM, N_GRP, SLOTS), 0, 8, jnp.int32)
    stacked = jnp.stack([element, face, subface, orient], axis=2)
    return stacked.reshape(DEVICES, 4, SLOTS).astype(jnp.int32)


def draw_neighbours(key, part):
    keys = jax.random.split(jax.random.fold_in(key, 17), 2)
    target = jax.random.randint(keys[0], (ELEMS, 6), 0, EL_DEV, jnp.int32)
    keep = jax.random.randint(keys[1], (ELEMS, 6), 0, 2, jnp.int32)
    return jnp.where(keep == 1, target, -1).astype(jnp.int32)


def plant(values, key, smallest, top_value):
    index_at = [jax.random.randint(jax.random.fold_in(key, axis), (), 0, length) for axis, length in enumerate(values.shape)]
    main_axis = values.shape.index(max(values.shape))
    neighbour = index_at[:main_axis] + [(index_at[main_axis] + 1) % values.shape[main_axis]] + index_at[main_axis + 1:]
    return values.at[tuple(index_at)].set(smallest).at[tuple(neighbour)].set(top_value)


def levels(own_key, dims, cuts, smallest, top_value):
    def one(axis_at, blocks):
        steps = jax.random.uniform(jax.random.fold_in(jax.random.fold_in(own_key, 6), axis_at), (blocks,), jnp.float32, smallest / len(cuts), top_value / len(cuts))
        return jnp.repeat(jnp.exp(steps), dims[axis_at] // blocks).reshape((-1,) + (1,) * (len(dims) - axis_at - 1))

    level = one(*cuts[0])
    for cut in cuts[1:]:
        level = level * one(*cut)
    return level


def setup_inputs(seed: int = 0) -> dict:
    splits = jax.random.split(jax.random.key(seed), 8)
    return {
        "state": draw_state(jax.random.fold_in(splits[7], 71), 0),
        "material": plant(jax.random.randint(splits[1], (ELEMS,), 0, 2), jax.random.fold_in(splits[1], 1), 0, 1).astype(jnp.int32),
        "metric": jnp.clip(jnp.exp(math.log(4.0) - 1.3862944 * jax.random.uniform(splits[2], (ELEMS,), jnp.float32) ** levels(splits[2], (ELEMS,), ((0, 1024),), -0.2, 0.2)), 1.0, 4.0),
        "mortar_proj": draw_mortar_proj(jax.random.fold_in(splits[7], 71), 0),
        "mortar_map": draw_mortar_map(jax.random.fold_in(splits[7], 71), 0),
        "mortar_count": draw_mortar_count(jax.random.fold_in(splits[7], 71), 0),
        "neighbours": draw_neighbours(jax.random.fold_in(splits[7], 71), 0),
    }


highest = lax.Precision.HIGHEST
step_size = 0.002
lift_weight = 49.0

def cheb_matrix():
    points = -np.cos(np.pi * np.arange(8) / 7.0)
    factor = np.array([2.0, 1.0, 1.0, 1.0, 1.0, 1.0, 1.0, 2.0])
    alternating = np.where(np.arange(8) % 2 == 0, 1.0, -1.0)
    scaled = factor * alternating
    differ = points[:, None] - points[None, :] + np.eye(8)
    matrix = scaled[:, None] / scaled[None, :] / differ
    matrix = matrix * (1.0 - np.eye(8))
    return matrix - np.eye(8) * matrix.sum(axis=1)[:, None]

def face_plane(node_grid, face):
    index = 0 if face % 2 == 0 else 7
    if face // 2 == 0:
        return node_grid[index]
    if face // 2 == 1:
        return node_grid[:, index]
    return node_grid[:, :, index]

def face_select():
    node_grid = np.arange(512).reshape(8, 8, 8)
    layers = []
    for face in range(6):
        layers.append(face_plane(node_grid, face).reshape(64))
    nodes = np.concatenate(layers)
    return (nodes[:, None] == np.arange(512)[None, :]).astype(np.float32)

def orient_matrices():
    first, second = np.meshgrid(np.arange(8), np.arange(8), indexing='ij')
    result = []
    for orient in range(8):
        row_p, row_r = (second, first) if orient & 4 else (first, second)
        if orient & 1:
            row_p = 7 - row_p
        if orient & 2:
            row_r = 7 - row_r
        source = (8 * row_p + row_r).reshape(64)
        result.append((source[:, None] == np.arange(64)[None, :]).astype(np.float32))
    return np.stack(result)

def state_parts(cons, heat_ratio, normal):
    density = cons[:, 0]
    momentum = cons[:, 1:4]
    energy = cons[:, 4]
    scalar = cons[:, 5]
    velocity = momentum / density[:, None]
    pressure = (heat_ratio[:, None] - 1.0) * (energy - 0.5 * lax.optimization_barrier(jnp.sum(momentum * velocity, axis=1)))
    direction = normal[:, :, None]
    speed_n = lax.optimization_barrier(jnp.sum(direction * velocity, axis=1))
    sound_speed = jnp.sqrt(heat_ratio[:, None] * pressure / density)
    phys_flux = jnp.concatenate([(density * speed_n)[:, None], momentum * speed_n[:, None] + pressure[:, None] * direction, ((energy + pressure) * speed_n)[:, None], (scalar * speed_n)[:, None]], axis=1)
    return (density, velocity, pressure, speed_n, sound_speed, energy, scalar, phys_flux)

def star_state(parts, wave_speed, middle, normal):
    density, velocity, pressure, speed_n, sound_speed, energy, scalar, phys_flux = parts
    relative = wave_speed - speed_n
    factor = density * relative / (wave_speed - middle)
    shifted = middle - speed_n
    momentum = factor[:, None] * (velocity + shifted[:, None] * normal[:, :, None])
    energy_star = factor * (energy / density + shifted * (middle + pressure / (density * relative)))
    return jnp.concatenate([factor[:, None], momentum, energy_star[:, None], (factor * scalar / density)[:, None]], axis=1)

def hllc_flux(left, right, heat_left, heat_right, normal):
    left_parts = state_parts(left, heat_left, normal)
    right_parts = state_parts(right, heat_right, normal)
    left_wave = jnp.minimum(left_parts[3] - left_parts[4], right_parts[3] - right_parts[4])
    right_wave = jnp.maximum(left_parts[3] + left_parts[4], right_parts[3] + right_parts[4])
    left_mass = left_parts[0] * (left_wave - left_parts[3])
    right_mass = right_parts[0] * (right_wave - right_parts[3])
    middle = (right_parts[2] - left_parts[2] + left_mass * left_parts[3] - right_mass * right_parts[3]) / (left_mass - right_mass)
    left_star = left_parts[7] + left_wave[:, None] * (star_state(left_parts, left_wave, middle, normal) - left)
    right_star = right_parts[7] + right_wave[:, None] * (star_state(right_parts, right_wave, middle, normal) - right)
    return jnp.where((left_wave >= 0.0)[:, None], left_parts[7], jnp.where((middle >= 0.0)[:, None], left_star, jnp.where((right_wave > 0.0)[:, None], right_star, right_parts[7])))

def normals_of(face):
    axis_id = face // 2
    orient_sign = jnp.where(face % 2 == 1, 1.0, -1.0).astype(jnp.float32)
    return orient_sign[:, None] * (axis_id[:, None] == jnp.arange(3, dtype=jnp.int32)[None, :]).astype(jnp.float32)

def face_traces(elements, select):
    count_el = elements.shape[0]
    flat_state = elements.reshape(count_el * NV, VN)
    traces = jnp.dot(flat_state, select.T, precision=highest, preferred_element_type=jnp.float32)
    return traces.reshape(count_el, NV, 6, FN).transpose(0, 2, 1, 3).reshape(count_el * 6, NV, FN)

def slot_operators(mortar_proj, mortar_info):
    identity = jnp.eye(FN, dtype=jnp.float32)
    proj_table = jnp.concatenate([identity[None], mortar_proj], axis=0)
    orients = jnp.asarray(orient_matrices(), jnp.float32)
    combos = jnp.einsum('spq,oqr->sopr', proj_table, orients, precision=highest).reshape((SUBS + 1) * 8, FN, FN)
    return combos[mortar_info[2] * 8 + mortar_info[3]]

def mortar_traces(face_rows, operators, heat_ratio, mortar_info):
    picked = face_rows[mortar_info[0] * 6 + mortar_info[1]]
    native = jnp.einsum('spq,svq->svp', operators, picked, precision=highest)
    return (native, heat_ratio[mortar_info[0]])

def slot_layout(groups, grp_index, counts):
    grp_slots = groups * CAPG
    slot_index = jnp.arange(grp_slots + 2 * CAPS, dtype=jnp.int32)
    peer_index = slot_index // CAPG
    in_grp = slot_index < grp_slots
    in_up = (slot_index >= grp_slots) & (slot_index < grp_slots + CAPS)
    group_id = jnp.where(in_grp, peer_index, jnp.where(in_up, groups, groups + 1))
    position = jnp.where(in_grp, slot_index % CAPG, (slot_index - grp_slots) % CAPS)
    slot_limit = lax.optimization_barrier(jnp.sum(jnp.where(group_id[:, None] == jnp.arange(groups + 2, dtype=jnp.int32)[None, :], counts[None, :], 0), axis=1))
    is_live = position < slot_limit
    is_lower = jnp.where(in_grp, grp_index < peer_index, in_up)
    return (is_lower, is_live)

def mortar_flux(native, partner, native_heat, partner_heat, normal, is_lower, is_live):
    live_mask = is_live[:, None, None]
    partner = jnp.where(live_mask, partner, native)
    partner_heat = jnp.where(is_live, partner_heat, native_heat)
    lower_mask = is_lower[:, None, None]
    low_side = jnp.where(lower_mask, native, partner)
    high_side = jnp.where(lower_mask, partner, native)
    low_heat = jnp.where(is_lower, native_heat, partner_heat)
    high_heat = jnp.where(is_lower, partner_heat, native_heat)
    low_normal = jnp.where(is_lower[:, None], normal, -normal)
    return hllc_flux(low_side, high_side, low_heat, high_heat, low_normal)

def volume_fluxes(elements, heat_ratio):
    fluxes = []
    for axis_id in range(3):
        direction = jnp.eye(3, dtype=jnp.float32)[axis_id][None, :]
        fluxes.append(state_parts(elements, heat_ratio, direction)[7])
    return fluxes

def volume_term(elements, heat_ratio):
    count_el = elements.shape[0]
    deriv = jnp.asarray(cheb_matrix(), jnp.float32)
    flux_x, flux_y, flux_z = [item.reshape(count_el, NV, NP, NP, NP) for item in volume_fluxes(elements, heat_ratio)]
    total = jnp.einsum('ia,evabc->evibc', deriv, flux_x, precision=highest)
    total = total + jnp.einsum('jb,evabc->evajc', deriv, flux_y, precision=highest)
    total = total + jnp.einsum('kc,evabc->evabk', deriv, flux_z, precision=highest)
    return -total.reshape(count_el, NV, VN)

def section_update(elements, heat_ratio, metric, mortar_info, neighbours, face_rows, operators, native, native_heat, flux_own, is_live, select, volume):
    count_el = elements.shape[0]
    normal = normals_of(mortar_info[1])
    correction = state_parts(native, native_heat, normal)[7] - flux_own
    correction = jnp.where(is_live[:, None, None], correction, 0.0)
    back_weight = jnp.where(mortar_info[2] == 0, 1.0, 0.25).astype(jnp.float32)
    projected = back_weight[:, None, None] * jnp.einsum('spq,svp->svq', operators, correction, precision=highest)
    face_id = jnp.tile(jnp.arange(6, dtype=jnp.int32), count_el)
    face_owner = jnp.repeat(jnp.arange(count_el, dtype=jnp.int32), 6)
    face_normal = normals_of(face_id)
    across = neighbours.reshape(count_el * 6)
    has_across = across >= 0
    safe_across = jnp.where(has_across, across, face_owner)
    source = jnp.where(has_across, across * 6 + jnp.bitwise_xor(face_id, 1), jnp.arange(count_el * 6, dtype=jnp.int32))
    partner = face_rows[source]
    row_heat = heat_ratio[face_owner]
    local_term = state_parts(face_rows, row_heat, face_normal)[7] - hllc_flux(face_rows, partner, row_heat, heat_ratio[safe_across], face_normal)
    local_term = jnp.where(has_across[:, None, None], local_term, 0.0)
    face_sum = local_term + jax.ops.segment_sum(projected, mortar_info[0] * 6 + mortar_info[1], num_segments=count_el * 6)
    placed = face_sum.reshape(count_el, 6, NV, FN).transpose(0, 2, 1, 3).reshape(count_el * NV, 6 * FN)
    surface = jnp.dot(placed, select, precision=highest, preferred_element_type=jnp.float32).reshape(count_el, NV, VN)
    return elements + step_size * metric[:, None, None] * (volume + lift_weight * surface)

def partner_slots(values):
    rest = values.shape[2:]
    grid = values.reshape((N_ELEM, N_GRP, SLOTS) + rest)
    grp_slots = N_GRP * CAPG
    grouped = grid[:, :, :grp_slots].reshape((N_ELEM, N_GRP, N_GRP, CAPG) + rest)
    swapped = jnp.swapaxes(grouped, 1, 2).reshape((N_ELEM, N_GRP, grp_slots) + rest)
    upward = grid[:, :, grp_slots:grp_slots + CAPS]
    downward = grid[:, :, grp_slots + CAPS:]
    above = jnp.concatenate([downward[1:], jnp.zeros_like(downward[:1])], axis=0)
    below = jnp.concatenate([jnp.zeros_like(upward[:1]), upward[:-1]], axis=0)
    return jnp.concatenate([swapped, above, below], axis=2).reshape((DEVICES, SLOTS) + rest)

def reference(state, material, metric, mortar_proj, mortar_map, mortar_count, neighbours):
    select = jnp.asarray(face_select(), jnp.float32)
    blocks = state.reshape(DEVICES, EL_DEV, NV, VN)
    materials = material.reshape(DEVICES, EL_DEV)
    metrics = metric.reshape(DEVICES, EL_DEV)
    across_all = neighbours.reshape(DEVICES, EL_DEV, 6)

    def first_pass(inputs):
        elements, kinds, mortar_info = inputs
        heat_ratio = 1.4 + 0.27 * kinds.astype(jnp.float32)
        face_rows = face_traces(elements, select)
        operators = slot_operators(mortar_proj, mortar_info)
        return mortar_traces(face_rows, operators, heat_ratio, mortar_info)
    natives, native_heats = lax.map(first_pass, (blocks, materials, mortar_map))
    partners = partner_slots(natives)
    partner_heats = partner_slots(native_heats)

    def second_pass(inputs):
        elements, kinds, scale, mortar_info, counts, across, native, native_heat, partner, partner_heat, device = inputs
        heat_ratio = 1.4 + 0.27 * kinds.astype(jnp.float32)
        face_rows = face_traces(elements, select)
        operators = slot_operators(mortar_proj, mortar_info)
        is_lower, is_live = slot_layout(N_GRP, device % N_GRP, counts)
        normal = normals_of(mortar_info[1])
        star_flux = mortar_flux(native, partner, native_heat, partner_heat, normal, is_lower, is_live)
        flux_own = jnp.where(is_lower[:, None, None], star_flux, -star_flux)
        volume = volume_term(elements, heat_ratio)
        return section_update(elements, heat_ratio, scale, mortar_info, across, face_rows, operators, native, native_heat, flux_own, is_live, select, volume)
    result = lax.map(second_pass, (blocks, materials, metrics, mortar_map, mortar_count, across_all, natives, native_heats, partners, partner_heats, jnp.arange(DEVICES, dtype=jnp.int32)))
    return result.reshape(ELEMS, NV, VN)
```

```python
import functools

import jax
import jax.numpy as jnp
import numpy as np
from jax import lax
from jax.experimental import pallas as pl
from jax.experimental.pallas import tpu as pltpu
from jax.sharding import PartitionSpec as P

CAPG = 8
CAPS = 32
SLOTS = 128
STEP = 0.002
LIFT = 49.0

f32 = jnp.float32
bf16 = jnp.bfloat16


def cheb_matrix():
    points = -np.cos(np.pi * np.arange(8) / 7.0)
    factor = np.array([2.0, 1.0, 1.0, 1.0, 1.0, 1.0, 1.0, 2.0])
    alternating = np.where(np.arange(8) % 2 == 0, 1.0, -1.0)
    scaled = factor * alternating
    differ = points[:, None] - points[None, :] + np.eye(8)
    matrix = scaled[:, None] / scaled[None, :] / differ
    matrix = matrix * (1.0 - np.eye(8))
    return (matrix - np.eye(8) * matrix.sum(axis=1)[:, None]).astype(np.float32)


def face_select():
    grid = np.arange(512).reshape(8, 8, 8)
    planes = [grid[:, 0], grid[:, 7], grid[:, :, 0], grid[:, :, 7]]
    nodes = np.concatenate([p.reshape(64) for p in planes])
    return (np.arange(512)[:, None] == nodes[None, :]).astype(np.float32)


def orient_table():
    first, second = np.meshgrid(np.arange(8), np.arange(8), indexing="ij")
    out = np.zeros((128, 1024), np.float32)
    for orient in range(8):
        p, r = (second, first) if orient & 4 else (first, second)
        p = 7 - p if orient & 1 else p
        r = 7 - r if orient & 2 else r
        source = (8 * p + r).reshape(64)
        for half in range(2):
            out[half * 64 + source, orient * 128 + half * 64 + np.arange(64)] = 1.0
    return out


def deriv_table():
    d = cheb_matrix()
    along_b = np.kron(np.eye(2), np.kron(d, np.eye(8))).T
    along_c = np.kron(np.eye(16), d).T
    return np.concatenate([along_b, along_c], axis=0).astype(np.float32)


def code_table(rows):
    out = np.zeros((16, 128 * len(rows)), np.float32)
    for block, weights in enumerate(rows):
        for row, weight in weights.items():
            out[row, block * 128 : (block + 1) * 128] = weight
    return out


def dot(a, b, ca=1, cb=0):
    return lax.dot_general(a, b, (((ca,), (cb,)), ((), ())), preferred_element_type=f32)


def split2(x):
    hi = x.astype(bf16)
    return hi, (x - hi.astype(f32)).astype(bf16)


def split3(x):
    hi = x.astype(bf16)
    rest = x - hi.astype(f32)
    mid = rest.astype(bf16)
    return hi, mid, (rest - mid.astype(f32)).astype(bf16)


def lane_low(shape):
    return lax.broadcasted_iota(jnp.int32, shape, len(shape) - 1) % 128 < 64


def swap(x):
    return pltpu.roll(x, 64, 1)


def join_pair(low, a, b):
    return jnp.where(low, a, swap(b))


def by_element(ref, shape):
    row = lax.broadcasted_iota(jnp.int32, shape, 0)
    out = jnp.full(shape, ref[0], f32) if ref.dtype == f32 else jnp.full(shape, ref[0].astype(f32), f32)
    for e in range(1, 8):
        out = jnp.where(row == e, ref[e].astype(f32), out)
    return out


def project_blocks(proj_ref):
    zero = jnp.zeros((64, 64), f32)
    blocks = []
    for s in range(4):
        p = proj_ref[s]
        top = jnp.concatenate([p, zero], axis=1)
        bottom = jnp.concatenate([zero, p], axis=1)
        blocks.append(jnp.concatenate([top, bottom], axis=0))
    return blocks


def slot_material(mat_ref, element):
    out = jnp.zeros(element.shape, f32)
    for e in range(8):
        out = jnp.where(element == e, mat_ref[e].astype(f32), out)
    return out


def code_rows(rows):
    pad = [jnp.zeros((1, SLOTS), f32)] * (16 - len(rows))
    return jnp.concatenate(rows + pad, axis=0).astype(bf16)


def trace_kernel(state_ref, mat_ref, map_ref, proj_ref, sel_ref, orient_ref, code_ref, out_ref, face_ref):
    low = lane_low((8, 128))
    flat = state_ref[...].reshape(48, 512)
    picked = dot(jnp.concatenate(split3(flat), axis=0), sel_ref[...])
    picked = picked[0:48] + picked[48:96] + picked[96:144]
    pairs = []
    for v in range(6):
        x = state_ref[v]
        pairs.append(
            [
                jnp.where(low, x[:, 0:128], x[:, 384:512]),
                picked[8 * v : 8 * v + 8, 0:128],
                picked[8 * v : 8 * v + 8, 128:256],
            ]
        )
    rows = []
    for j in range(3):
        for d in range(3):
            first, second = pairs[2 * j][d], pairs[2 * j + 1][d]
            rows.append(jnp.where(low, first, swap(second)))
            rows.append(jnp.where(low, swap(first), second))
    faces = jnp.concatenate(rows, axis=0)
    face_ref[...] = faces
    hi, lo = split2(faces)
    table = dot(jnp.concatenate([hi, lo], axis=0), orient_ref[...]).astype(bf16)
    info = map_ref[...]
    element, face, sub, orient = (info[i : i + 1] for i in range(4))
    material = slot_material(mat_ref, element)
    codes = code_rows([element.astype(f32), face.astype(f32), sub.astype(f32), orient.astype(f32), material])
    spread = dot(codes, code_ref[...], 0, 0)
    index = spread[:, 0:128].astype(jnp.int32)
    sub_of = spread[:, 128:256].astype(jnp.int32)
    lane = lax.broadcasted_iota(jnp.int32, (SLOTS, 128), 1)
    one_hot = jnp.concatenate(
        [jnp.where(index == lane + 128 * t, 1.0, 0.0).astype(bf16) for t in range(3)], axis=1
    )
    columns = []
    for part in range(6):
        block = table[48 * part : 48 * part + 48]
        columns.append(jnp.concatenate([block[:, 128 * o : 128 * o + 128] for o in range(8)], axis=0))
    gathered = dot(one_hot, jnp.concatenate(columns, axis=1))
    x_hi = jnp.concatenate([gathered[:, 128 * j : 128 * j + 128] for j in range(3)], axis=0)
    x_lo = jnp.concatenate([gathered[:, 384 + 128 * j : 512 + 128 * j] for j in range(3)], axis=0)
    b_hi, b_lo = split2(jnp.concatenate(project_blocks(proj_ref), axis=0))
    h = x_hi.astype(bf16)
    wide = dot(
        jnp.concatenate([h, x_lo.astype(bf16)], axis=1), jnp.concatenate([b_hi, b_hi], axis=1), 1, 1
    ) + dot(h, b_lo, 1, 1)
    for j in range(3):
        r = slice(128 * j, 128 * j + 128)
        w = x_hi[r] + x_lo[r]
        for s in range(4):
            w = jnp.where(sub_of == s + 1, wide[r, 128 * s : 128 * s + 128], w)
        out_ref[:, 128 * j : 128 * j + 128] = w
    out_ref[:, 384:512] = 1.4 + 0.27 * spread[:, 256:384]


def hllc_correction(u, g, normal, own):
    inv = 1.0 / u[0]
    vel = [u[1] * inv, u[2] * inv, u[3] * inv]
    p = (g - 1.0) * (u[4] - 0.5 * (u[1] * vel[0] + u[2] * vel[1] + u[3] * vel[2]))
    s = normal[0] * vel[0] + normal[1] * vel[1] + normal[2] * vel[2]
    c = jnp.sqrt(g * p * inv)
    lower, upper = s - c, s + c
    left = jnp.minimum(lower, swap(lower))
    right = jnp.maximum(upper, swap(upper))
    wave = jnp.where(own, left, right)
    relative = wave - s
    mass = u[0] * relative
    part = mass * s - p
    middle = (part - swap(part)) / (mass - swap(mass))
    chi = mass / (wave - middle)
    shift = middle - s
    star = [
        chi,
        chi * (vel[0] + shift * normal[0]),
        chi * (vel[1] + shift * normal[1]),
        chi * (vel[2] + shift * normal[2]),
        chi * (u[4] * inv + shift * (middle + p / mass)),
        chi * (u[5] * inv),
    ]
    flux = [
        u[0] * s,
        u[1] * s + p * normal[0],
        u[2] * s + p * normal[1],
        u[3] * s + p * normal[2],
        (u[4] + p) * s,
        u[5] * s,
    ]
    use_star = jnp.where(own, -wave, wave) > 0.0
    take_own = (left >= 0.0) | (middle >= 0.0)
    out = []
    for v in range(6):
        side = jnp.where(use_star, wave * (star[v] - u[v]), 0.0)
        out.append(jnp.where(take_own, -side, flux[v] - swap(flux[v] + side)))
    return out


def paired(own, mine, theirs):
    return jnp.where(own, mine, swap(theirs)), jnp.where(own, swap(mine), theirs)


def local_kernel(state_ref, mat_ref, metric_ref, near_ref, face_ref, deriv_ref, base_ref, local_ref):
    heat = 1.4 + 0.27 * by_element(mat_ref, (8, 512))
    u = [state_ref[v] for v in range(6)]
    inv = 1.0 / u[0]
    vel = [u[1] * inv, u[2] * inv, u[3] * inv]
    p = (heat - 1.0) * (u[4] - 0.5 * (u[1] * vel[0] + u[2] * vel[1] + u[3] * vel[2]))
    fluxes = []
    for d in range(3):
        s = vel[d]
        f = [u[0] * s, u[1] * s, u[2] * s, u[3] * s, (u[4] + p) * s, u[5] * s]
        f[1 + d] = f[1 + d] + p
        fluxes.append(f)
    rows = []
    for v in range(6):
        for t in range(4):
            r = slice(128 * t, 128 * t + 128)
            rows.append(jnp.concatenate([fluxes[1][v][:, r], fluxes[2][v][:, r]], axis=1))
    hi, lo = split2(jnp.concatenate(rows, axis=0))
    d_hi, d_lo = deriv_ref[:, 0:128], deriv_ref[:, 128:256]
    main = dot(jnp.concatenate([hi, lo], axis=0), d_hi)
    bc = main[0:192] + main[192:384] + dot(hi, d_lo)
    low = lane_low((8, 128))
    deriv = cheb_matrix()
    scale = STEP * by_element(metric_ref, (8, 128))
    for v in range(6):
        x = [fluxes[0][v][:, 128 * t : 128 * t + 128] for t in range(4)]
        xs = [swap(a) for a in x]
        for t in range(4):
            acc = bc[32 * v + 8 * t : 32 * v + 8 * t + 8]
            for k in range(4):
                same = jnp.where(low, float(deriv[2 * t, 2 * k]), float(deriv[2 * t + 1, 2 * k + 1]))
                cross = jnp.where(low, float(deriv[2 * t, 2 * k + 1]), float(deriv[2 * t + 1, 2 * k]))
                acc = acc + same * x[k] + cross * xs[k]
            r = slice(128 * t, 128 * t + 128)
            base_ref[v, :, r] = u[v][:, r] - scale * acc
    faces = face_ref[...]
    lane = lax.broadcasted_iota(jnp.int32, (8, 256), 1)
    hot, live = [], []
    for k in range(6):
        near = jnp.broadcast_to(near_ref[:, k : k + 1], (8, 256))
        live.append((near >= 0)[:, 0:128])
        target = 8 * (k ^ 1) + near
        hit = (jnp.bitwise_and(lane, 63) == target) & (near >= 0) & (lane < 192)
        hot.append(jnp.where(hit, 1.0, 0.0))
    hot = jnp.concatenate(hot, axis=0).astype(bf16)
    heat_rows = jnp.concatenate([heat[:, 0:128]] * 6, axis=0)
    table = jnp.concatenate([faces[0:48], faces[48:96], faces[96:144], heat_rows], axis=1)
    gap = jnp.zeros((16, 512), bf16)
    terms = []
    for term in split3(table):
        terms += [term, gap]
    terms.append(jnp.zeros((64, 512), bf16))
    theirs = dot(hot, jnp.concatenate(terms, axis=0))
    own = lane_low((48, 128))
    row = lax.broadcasted_iota(jnp.int32, (48, 128), 0)
    sign = jnp.where(jnp.bitwise_and(row, 8) != 0, 1.0, -1.0)
    normal = [jnp.where(lax.shift_right_logical(row, 4) == d, sign, 0.0) for d in range(3)]
    states = []
    for j in range(3):
        states += paired(own, faces[48 * j : 48 * j + 48], theirs[:, 128 * j : 128 * j + 128])
    g = jnp.where(own, heat_rows, theirs[:, 384:512])
    corr = hllc_correction(states, g, normal, own)
    for j in range(3):
        packed = join_pair(own, corr[2 * j], corr[2 * j + 1])
        for k in range(6):
            local_ref[48 * j + 8 * k : 48 * j + 8 * k + 8, :] = jnp.where(
                live[k], packed[8 * k : 8 * k + 8], 0.0
            )


def mortar_kernel(
    mine_ref, grp_ref, above_ref, below_ref, mat_ref, metric_ref, count_ref, map_ref, proj_ref,
    sel_ref, orient_ref, code_ref, base_ref, local_ref, out_ref,
):
    info = map_ref[...]
    element, face, sub, orient = (info[i : i + 1] for i in range(4))
    slot = lax.broadcasted_iota(jnp.int32, (1, SLOTS), 1)
    group = jnp.where(
        slot < 64, lax.shift_right_logical(slot, 3), 6 + lax.shift_right_logical(slot, 5)
    )
    position = jnp.where(slot < 64, jnp.bitwise_and(slot, 7), jnp.bitwise_and(slot, 31))
    limit = jnp.zeros((1, SLOTS), jnp.int32)
    for n in range(10):
        limit = jnp.where(group == n, count_ref[n], limit)
    alive = jnp.where(position < limit, 1.0, 0.0)
    sign = jnp.where(jnp.bitwise_and(face, 1) == 1, 1.0, -1.0)
    axis = lax.shift_right_logical(face, 1)
    codes = code_rows(
        [sub.astype(f32), alive] + [jnp.where(axis == d, sign, 0.0) for d in range(3)]
    )
    spread = dot(codes, code_ref[...], 0, 0)
    chunk = 32
    own = lane_low((chunk, 128))
    packed = [[], [], []]
    for start in range(0, SLOTS, chunk):
        r = slice(start, start + chunk)
        if start < 64:
            theirs_ref, at = grp_ref, start
        elif start < 96:
            theirs_ref, at = above_ref, start - 64
        else:
            theirs_ref, at = below_ref, start - 96
        q = slice(at, at + chunk)
        states = []
        for j in range(3):
            lanes = slice(128 * j, 128 * j + 128)
            states += paired(own, mine_ref[r, lanes], theirs_ref[q, lanes])
        g = jnp.where(own, mine_ref[r, 384:512], theirs_ref[q, 384:512])
        live = spread[r, 128:256] > 0.5
        normal = [spread[r, 256 + 128 * d : 384 + 128 * d] for d in range(3)]
        corr = hllc_correction(states, g, normal, own)
        for j in range(3):
            packed[j].append(jnp.where(live, join_pair(own, corr[2 * j], corr[2 * j + 1]), 0.0))
    corr = jnp.concatenate(packed[0] + packed[1] + packed[2], axis=0)
    b_hi, b_lo = split2(jnp.concatenate(project_blocks(proj_ref), axis=1))
    hi, lo = split2(corr)
    wide = dot(jnp.concatenate([hi, lo], axis=1), jnp.concatenate([b_hi, b_hi], axis=0)) + dot(hi, b_lo)
    sub_of = spread[:, 0:128].astype(jnp.int32)
    back = []
    for j in range(3):
        r = slice(128 * j, 128 * j + 128)
        y = corr[r]
        for s in range(4):
            y = jnp.where(sub_of == s + 1, wide[r, 128 * s : 128 * s + 128], y)
        back.append(y)
    hi, lo = split2(jnp.concatenate(back, axis=1))
    index = 48 * orient + 8 * face + element
    row = lax.broadcasted_iota(jnp.int32, (384, SLOTS), 0)
    beta = jnp.where(sub == 0, 1.0, 0.25)
    hot = jnp.where(row == index, beta, 0.0).astype(bf16)
    summed = dot(jnp.concatenate([hot, hot], axis=1), jnp.concatenate([hi, lo], axis=0))
    rows = []
    for j in range(3):
        lanes = slice(128 * j, 128 * j + 128)
        rows.append(jnp.concatenate([summed[48 * o : 48 * o + 48, lanes] for o in range(8)], axis=1))
    hi, lo = split2(jnp.concatenate(rows, axis=0))
    turned = dot(jnp.concatenate([hi, lo], axis=0), orient_ref[...], 1, 1)
    total = turned[0:144] + turned[144:288] + local_ref[...]
    low = lane_low((8, 128))
    lift = []
    for v in range(6):
        at = 48 * (v // 2)
        parts = []
        for d in range(3):
            first = total[at + 16 * d : at + 16 * d + 8]
            second = total[at + 16 * d + 8 : at + 16 * d + 16]
            if v % 2 == 0:
                parts.append(jnp.where(low, first, swap(second)))
            else:
                parts.append(jnp.where(low, swap(first), second))
        lift.append(parts)
    side = jnp.concatenate(
        [jnp.concatenate([lift[v][1] for v in range(6)], axis=0), jnp.concatenate([lift[v][2] for v in range(6)], axis=0)],
        axis=1,
    )
    hi, lo = split2(side)
    placed = dot(jnp.concatenate([hi, lo], axis=0), sel_ref[...], 1, 1)
    placed = placed[0:48] + placed[48:96]
    scale = (STEP * LIFT) * by_element(metric_ref, (8, 128))
    for v in range(6):
        for t in range(4):
            lanes = slice(128 * t, 128 * t + 128)
            value = placed[8 * v : 8 * v + 8, lanes]
            if t == 0:
                value = value + jnp.where(low, lift[v][0], 0.0)
            if t == 3:
                value = value + jnp.where(low, 0.0, lift[v][0])
            out_ref[v, :, lanes] = base_ref[v, :, lanes] + scale * value


SM = pl.BlockSpec(memory_space=pltpu.SMEM)
VM = pl.BlockSpec(memory_space=pltpu.VMEM)


def call(kernel, outs, specs, name):
    return pl.pallas_call(
        kernel,
        out_shape=[jax.ShapeDtypeStruct(s, f32) for s in outs],
        in_specs=specs,
        out_specs=[VM] * len(outs),
        name=name,
    )


def shards(state, material, metric, mortar_proj, mortar_map, mortar_count, neighbours):
    groups = lax.axis_size("grp")
    n_elem = lax.axis_size("elem")
    elements = jnp.transpose(state, (1, 0, 2))
    info = mortar_map[0]
    counts = mortar_count[0]
    select = jnp.asarray(face_select(), bf16)
    orients = jnp.asarray(orient_table(), bf16)
    deriv = deriv_table()
    d_hi = deriv.astype(bf16)
    d_lo = (deriv - d_hi.astype(np.float32)).astype(bf16)
    derivs = jnp.asarray(np.concatenate([d_hi, d_lo], axis=1))
    codes_a = jnp.asarray(code_table([{0: 1, 1: 8, 3: 48}, {2: 1}, {4: 1}]), bf16)
    codes_c = jnp.asarray(code_table([{n: 1} for n in range(5)]), bf16)

    mine, faces = call(
        trace_kernel, [(SLOTS, 512), (144, 128)], [VM, SM, VM, VM, VM, VM, VM], "traces"
    )(elements, material, info, mortar_proj, select, orients, codes_a)
    split = groups * CAPG
    arrived = lax.all_to_all(
        mine[:split].reshape(groups, CAPG, 512), "grp", split_axis=0, concat_axis=0, tiled=True
    ).reshape(split, 512)
    up = [(i, i + 1) for i in range(n_elem - 1)]
    down = [(i + 1, i) for i in range(n_elem - 1)]
    from_above = lax.ppermute(mine[split + CAPS :], "elem", down)
    from_below = lax.ppermute(mine[split : split + CAPS], "elem", up)
    base, local = call(
        local_kernel, [(6, 8, 512), (144, 128)], [VM, SM, SM, VM, VM, VM], "local"
    )(elements, material, metric, neighbours, faces, derivs)
    (new,) = call(
        mortar_kernel,
        [(6, 8, 512)],
        [VM, VM, VM, VM, SM, SM, SM, VM, VM, VM, VM, VM, VM, VM],
        "mortar",
    )(
        mine, arrived, from_above, from_below, material, metric, counts, info, mortar_proj,
        select, orients, codes_c, base, local,
    )
    return jnp.transpose(new, (1, 0, 2))


def solution(mesh):
    return jax.shard_map(
        shards,
        mesh=mesh,
        in_specs=(
            P(("elem", "grp"), None, None),
            P(("elem", "grp")),
            P(("elem", "grp")),
            P(),
            P(("elem", "grp"), None, None),
            P(("elem", "grp"), None),
            P(("elem", "grp"), None),
        ),
        out_specs=P(("elem", "grp"), None, None),
        check_vma=False,
    )
```

```python
import functools

import jax
import jax.numpy as jnp
import numpy as np
from jax import lax
from jax.experimental import pallas as pl
from jax.experimental.pallas import tpu as pltpu
from jax.sharding import PartitionSpec as P


CAPG = 8
CAPS = 32
SLOTS = 128
STEP = 0.002
LIFT = 49.0

f32 = jnp.float32
bf16 = jnp.bfloat16


def cheb_matrix():
    points = -np.cos(np.pi * np.arange(8) / 7.0)
    factor = np.array([2.0, 1.0, 1.0, 1.0, 1.0, 1.0, 1.0, 2.0])
    alternating = np.where(np.arange(8) % 2 == 0, 1.0, -1.0)
    scaled = factor * alternating
    differ = points[:, None] - points[None, :] + np.eye(8)
    matrix = scaled[:, None] / scaled[None, :] / differ
    matrix = matrix * (1.0 - np.eye(8))
    return (matrix - np.eye(8) * matrix.sum(axis=1)[:, None]).astype(np.float32)


def face_select():
    grid = np.arange(512).reshape(8, 8, 8)
    planes = [grid[:, 0], grid[:, 7], grid[:, :, 0], grid[:, :, 7]]
    nodes = np.concatenate([p.reshape(64) for p in planes])
    return (np.arange(512)[:, None] == nodes[None, :]).astype(np.float32)


def orient_table():
    first, second = np.meshgrid(np.arange(8), np.arange(8), indexing="ij")
    out = np.zeros((128, 1024), np.float32)
    for orient in range(8):
        p, r = (second, first) if orient & 4 else (first, second)
        p = 7 - p if orient & 1 else p
        r = 7 - r if orient & 2 else r
        source = (8 * p + r).reshape(64)
        for half in range(2):
            out[half * 64 + source, orient * 128 + half * 64 + np.arange(64)] = 1.0
    return out


def deriv_table():
    d = cheb_matrix()
    along_b = np.kron(np.eye(2), np.kron(d, np.eye(8))).T
    along_c = np.kron(np.eye(16), d).T
    return np.concatenate([along_b, along_c], axis=0).astype(np.float32)


def code_table(rows):
    out = np.zeros((16, 128 * len(rows)), np.float32)
    for block, weights in enumerate(rows):
        for row, weight in weights.items():
            out[row, block * 128 : (block + 1) * 128] = weight
    return out


def dot(a, b, ca=1, cb=0):
    return lax.dot_general(a, b, (((ca,), (cb,)), ((), ())), preferred_element_type=f32)


def split2(x):
    hi = x.astype(bf16)
    return hi, (x - hi.astype(f32)).astype(bf16)


def split3(x):
    hi = x.astype(bf16)
    rest = x - hi.astype(f32)
    mid = rest.astype(bf16)
    return hi, mid, (rest - mid.astype(f32)).astype(bf16)


def lane_low(shape):
    return lax.broadcasted_iota(jnp.int32, shape, len(shape) - 1) % 128 < 64


def swap(x):
    return pltpu.roll(x, 64, 1)


def join_pair(low, a, b):
    return jnp.where(low, a, swap(b))


def by_element(ref, shape):
    row = lax.broadcasted_iota(jnp.int32, shape, 0)
    out = jnp.full(shape, ref[0], f32) if ref.dtype == f32 else jnp.full(shape, ref[0].astype(f32), f32)
    for e in range(1, 8):
        out = jnp.where(row == e, ref[e].astype(f32), out)
    return out


def project_blocks(proj_ref):
    zero = jnp.zeros((64, 64), f32)
    blocks = []
    for s in range(4):
        p = proj_ref[s]
        top = jnp.concatenate([p, zero], axis=1)
        bottom = jnp.concatenate([zero, p], axis=1)
        blocks.append(jnp.concatenate([top, bottom], axis=0))
    return blocks


def slot_material(mat_ref, element):
    out = jnp.zeros(element.shape, f32)
    for e in range(8):
        out = jnp.where(element == e, mat_ref[e].astype(f32), out)
    return out


def code_rows(rows):
    pad = [jnp.zeros((1, SLOTS), f32)] * (16 - len(rows))
    return jnp.concatenate(rows + pad, axis=0).astype(bf16)


def trace_kernel(
    state_ref, mat_ref, map_ref, proj_ref, sel_ref, orient_ref, code_ref, grp_ref, up_ref, down_ref, face_ref, mine_ref, info_ref,
):
    low = lane_low((8, 128))
    flat = state_ref[...].reshape(48, 512)
    picked = dot(jnp.concatenate(split3(flat), axis=0), sel_ref[...])
    picked = picked[0:48] + picked[48:96] + picked[96:144]
    pairs = []
    for v in range(6):
        x = state_ref[v]
        pairs.append(
            [
                jnp.where(low, x[:, 0:128], x[:, 384:512]),
                picked[8 * v : 8 * v + 8, 0:128],
                picked[8 * v : 8 * v + 8, 128:256],
            ]
        )
    rows = []
    for j in range(3):
        for d in range(3):
            first, second = pairs[2 * j][d], pairs[2 * j + 1][d]
            rows.append(jnp.where(low, first, swap(second)))
            rows.append(jnp.where(low, swap(first), second))
    faces = jnp.concatenate(rows, axis=0)
    face_ref[...] = faces
    hi, lo = split2(faces)
    table = dot(jnp.concatenate([hi, lo], axis=0), orient_ref[...]).astype(bf16)
    info = map_ref[...]
    info_ref[...] = jnp.concatenate([info, info], axis=0)
    element, face, sub, orient = (info[i : i + 1] for i in range(4))
    material = slot_material(mat_ref, element)
    codes = code_rows([element.astype(f32), face.astype(f32), sub.astype(f32), orient.astype(f32), material])
    spread = dot(codes, code_ref[...], 0, 0)
    index = spread[:, 0:128].astype(jnp.int32)
    sub_of = spread[:, 128:256].astype(jnp.int32)
    lane = lax.broadcasted_iota(jnp.int32, (SLOTS, 128), 1)
    one_hot = jnp.concatenate(
        [jnp.where(index == lane + 128 * t, 1.0, 0.0).astype(bf16) for t in range(3)], axis=1
    )
    columns = []
    for part in range(6):
        block = table[48 * part : 48 * part + 48]
        columns.append(jnp.concatenate([block[:, 128 * o : 128 * o + 128] for o in range(8)], axis=0))
    gathered = dot(one_hot, jnp.concatenate(columns, axis=1))
    x_hi = jnp.concatenate([gathered[:, 128 * j : 128 * j + 128] for j in range(3)], axis=0)
    x_lo = jnp.concatenate([gathered[:, 384 + 128 * j : 512 + 128 * j] for j in range(3)], axis=0)
    b_hi, b_lo = split2(jnp.concatenate(project_blocks(proj_ref), axis=0))
    h = x_hi.astype(bf16)
    wide = dot(
        jnp.concatenate([h, x_lo.astype(bf16)], axis=1), jnp.concatenate([b_hi, b_hi], axis=1), 1, 1
    ) + dot(h, b_lo, 1, 1)

    def put(at, value):
        lanes = slice(at, at + 128)
        for g in range(8):
            grp_ref[g, :, lanes] = value[8 * g : 8 * g + 8]
            mine_ref[g, :, lanes] = value[8 * g : 8 * g + 8]
        up_ref[:, lanes] = value[64:96]
        down_ref[:, lanes] = value[96:128]

    for j in range(3):
        r = slice(128 * j, 128 * j + 128)
        w = x_hi[r] + x_lo[r]
        for s in range(4):
            w = jnp.where(sub_of == s + 1, wide[r, 128 * s : 128 * s + 128], w)
        put(128 * j, w)
    put(384, 1.4 + 0.27 * spread[:, 256:384])


def hllc_correction(u, g, normal, own):
    inv = 1.0 / u[0]
    vel = [u[1] * inv, u[2] * inv, u[3] * inv]
    p = (g - 1.0) * (u[4] - 0.5 * (u[1] * vel[0] + u[2] * vel[1] + u[3] * vel[2]))
    s = normal[0] * vel[0] + normal[1] * vel[1] + normal[2] * vel[2]
    c = jnp.sqrt(g * p * inv)
    lower, upper = s - c, s + c
    left = jnp.minimum(lower, swap(lower))
    right = jnp.maximum(upper, swap(upper))
    wave = jnp.where(own, left, right)
    relative = wave - s
    mass = u[0] * relative
    part = mass * s - p
    middle = (part - swap(part)) / (mass - swap(mass))
    chi = mass / (wave - middle)
    shift = middle - s
    star = [
        chi,
        chi * (vel[0] + shift * normal[0]),
        chi * (vel[1] + shift * normal[1]),
        chi * (vel[2] + shift * normal[2]),
        chi * (u[4] * inv + shift * (middle + p / mass)),
        chi * (u[5] * inv),
    ]
    flux = [
        u[0] * s,
        u[1] * s + p * normal[0],
        u[2] * s + p * normal[1],
        u[3] * s + p * normal[2],
        (u[4] + p) * s,
        u[5] * s,
    ]
    use_star = jnp.where(own, -wave, wave) > 0.0
    take_own = (left >= 0.0) | (middle >= 0.0)
    out = []
    for v in range(6):
        side = jnp.where(use_star, wave * (star[v] - u[v]), 0.0)
        out.append(jnp.where(take_own, -side, flux[v] - swap(flux[v] + side)))
    return out


def paired(own, mine, theirs):
    return jnp.where(own, mine, swap(theirs)), jnp.where(own, swap(mine), theirs)


def local_kernel(
    state_ref, mat_ref, metric_ref, count_ref, near_ref, face_ref, deriv_ref, info_ref, proj_ref, code_ref,
    base_ref, local_ref, spread_ref, hot_ref, back_ref,
):
    info = info_ref[...]
    element, face, sub, orient = (info[i : i + 1] for i in range(4))
    slot = lax.broadcasted_iota(jnp.int32, (1, SLOTS), 1)
    group = jnp.where(
        slot < 64, lax.shift_right_logical(slot, 3), 6 + lax.shift_right_logical(slot, 5)
    )
    position = jnp.where(slot < 64, jnp.bitwise_and(slot, 7), jnp.bitwise_and(slot, 31))
    limit = jnp.zeros((1, SLOTS), jnp.int32)
    for n in range(10):
        limit = jnp.where(group == n, count_ref[n], limit)
    alive = jnp.where(position < limit, 1.0, 0.0)
    sign = jnp.where(jnp.bitwise_and(face, 1) == 1, 1.0, -1.0)
    axis = lax.shift_right_logical(face, 1)
    codes = code_rows(
        [sub.astype(f32), alive] + [jnp.where(axis == d, sign, 0.0) for d in range(3)]
    )
    spread_ref[...] = dot(codes, code_ref[...], 0, 0)
    index = 48 * orient + 8 * face + element
    row = lax.broadcasted_iota(jnp.int32, (384, SLOTS), 0)
    beta = jnp.where(sub == 0, 1.0, 0.25)
    hot = jnp.where(row == index, beta, 0.0).astype(bf16)
    hot_ref[:, 0:128] = hot
    hot_ref[:, 128:256] = hot
    b_hi, b_lo = split2(jnp.concatenate(project_blocks(proj_ref), axis=1))
    back_ref[0:128, :] = b_hi
    back_ref[128:256, :] = b_hi
    back_ref[256:384, :] = b_lo
    heat = 1.4 + 0.27 * by_element(mat_ref, (8, 512))
    u = [state_ref[v] for v in range(6)]
    inv = 1.0 / u[0]
    vel = [u[1] * inv, u[2] * inv, u[3] * inv]
    p = (heat - 1.0) * (u[4] - 0.5 * (u[1] * vel[0] + u[2] * vel[1] + u[3] * vel[2]))
    fluxes = []
    for d in range(3):
        s = vel[d]
        f = [u[0] * s, u[1] * s, u[2] * s, u[3] * s, (u[4] + p) * s, u[5] * s]
        f[1 + d] = f[1 + d] + p
        fluxes.append(f)
    rows = []
    for v in range(6):
        for t in range(4):
            r = slice(128 * t, 128 * t + 128)
            rows.append(jnp.concatenate([fluxes[1][v][:, r], fluxes[2][v][:, r]], axis=1))
    hi, lo = split2(jnp.concatenate(rows, axis=0))
    d_hi, d_lo = deriv_ref[:, 0:128], deriv_ref[:, 128:256]
    main = dot(jnp.concatenate([hi, lo], axis=0), d_hi)
    bc = main[0:192] + main[192:384] + dot(hi, d_lo)
    low = lane_low((8, 128))
    deriv = cheb_matrix()
    scale = STEP * by_element(metric_ref, (8, 128))
    for v in range(6):
        x = [fluxes[0][v][:, 128 * t : 128 * t + 128] for t in range(4)]
        xs = [swap(a) for a in x]
        for t in range(4):
            acc = bc[32 * v + 8 * t : 32 * v + 8 * t + 8]
            for k in range(4):
                same = jnp.where(low, float(deriv[2 * t, 2 * k]), float(deriv[2 * t + 1, 2 * k + 1]))
                cross = jnp.where(low, float(deriv[2 * t, 2 * k + 1]), float(deriv[2 * t + 1, 2 * k]))
                acc = acc + same * x[k] + cross * xs[k]
            r = slice(128 * t, 128 * t + 128)
            base_ref[v, :, r] = u[v][:, r] - scale * acc
    faces = face_ref[...]
    lane = lax.broadcasted_iota(jnp.int32, (8, 256), 1)
    hot, live = [], []
    for k in range(6):
        near = jnp.broadcast_to(near_ref[:, k : k + 1], (8, 256))
        live.append((near >= 0)[:, 0:128])
        target = 8 * (k ^ 1) + near
        hit = (jnp.bitwise_and(lane, 63) == target) & (near >= 0) & (lane < 192)
        hot.append(jnp.where(hit, 1.0, 0.0))
    hot = jnp.concatenate(hot, axis=0).astype(bf16)
    heat_rows = jnp.concatenate([heat[:, 0:128]] * 6, axis=0)
    table = jnp.concatenate([faces[0:48], faces[48:96], faces[96:144], heat_rows], axis=1)
    gap = jnp.zeros((16, 512), bf16)
    terms = []
    for term in split3(table):
        terms += [term, gap]
    terms.append(jnp.zeros((64, 512), bf16))
    theirs = dot(hot, jnp.concatenate(terms, axis=0))
    own = lane_low((48, 128))
    row = lax.broadcasted_iota(jnp.int32, (48, 128), 0)
    sign = jnp.where(jnp.bitwise_and(row, 8) != 0, 1.0, -1.0)
    normal = [jnp.where(lax.shift_right_logical(row, 4) == d, sign, 0.0) for d in range(3)]
    states = []
    for j in range(3):
        states += paired(own, faces[48 * j : 48 * j + 48], theirs[:, 128 * j : 128 * j + 128])
    g = jnp.where(own, heat_rows, theirs[:, 384:512])
    corr = hllc_correction(states, g, normal, own)
    for j in range(3):
        packed = join_pair(own, corr[2 * j], corr[2 * j + 1])
        for k in range(6):
            local_ref[48 * j + 8 * k : 48 * j + 8 * k + 8, :] = jnp.where(
                live[k], packed[8 * k : 8 * k + 8], 0.0
            )


def mortar_kernel(
    grp_ref, up_ref, down_ref, from_grp_ref, above_ref, below_ref, metric_ref,
    sel_ref, orient_ref, base_ref, local_ref, spread_ref, hot_ref, back_ref, out_ref,
):
    chunk = 32
    own = lane_low((chunk, 128))
    packed = [[], [], []]
    for start in range(0, SLOTS, chunk):
        r = slice(start, start + chunk)

        def rows(grp, up, down, at):
            lanes = slice(at, at + 128)
            if start < 64:
                return jnp.concatenate([grp[start // 8 + n, :, lanes] for n in range(chunk // 8)], axis=0)
            return (up if start < 96 else down)[:, lanes]

        mine = functools.partial(rows, grp_ref, up_ref, down_ref)
        theirs = functools.partial(rows, from_grp_ref, above_ref, below_ref)
        states = []
        for j in range(3):
            states += paired(own, mine(128 * j), theirs(128 * j))
        g = jnp.where(own, mine(384), theirs(384))
        live = spread_ref[r, 128:256] > 0.5
        normal = [spread_ref[r, 256 + 128 * d : 384 + 128 * d] for d in range(3)]
        corr = hllc_correction(states, g, normal, own)
        for j in range(3):
            packed[j].append(jnp.where(live, join_pair(own, corr[2 * j], corr[2 * j + 1]), 0.0))
    corr = jnp.concatenate(packed[0] + packed[1] + packed[2], axis=0)
    hi, lo = split2(corr)
    wide = dot(jnp.concatenate([hi, lo, hi], axis=1), back_ref[...])
    sub_of = spread_ref[:, 0:128].astype(jnp.int32)
    back = []
    for j in range(3):
        r = slice(128 * j, 128 * j + 128)
        y = corr[r]
        for s in range(4):
            y = jnp.where(sub_of == s + 1, wide[r, 128 * s : 128 * s + 128], y)
        back.append(y)
    hi, lo = split2(jnp.concatenate(back, axis=1))
    summed = dot(hot_ref[...], jnp.concatenate([hi, lo], axis=0))
    rows = []
    for j in range(3):
        lanes = slice(128 * j, 128 * j + 128)
        rows.append(jnp.concatenate([summed[48 * o : 48 * o + 48, lanes] for o in range(8)], axis=1))
    hi, lo = split2(jnp.concatenate(rows, axis=0))
    turned = dot(jnp.concatenate([hi, lo], axis=0), orient_ref[...], 1, 1)
    total = turned[0:144] + turned[144:288] + local_ref[...]
    low = lane_low((8, 128))
    lift = []
    for v in range(6):
        at = 48 * (v // 2)
        parts = []
        for d in range(3):
            first = total[at + 16 * d : at + 16 * d + 8]
            second = total[at + 16 * d + 8 : at + 16 * d + 16]
            if v % 2 == 0:
                parts.append(jnp.where(low, first, swap(second)))
            else:
                parts.append(jnp.where(low, swap(first), second))
        lift.append(parts)
    side = jnp.concatenate(
        [jnp.concatenate([lift[v][1] for v in range(6)], axis=0), jnp.concatenate([lift[v][2] for v in range(6)], axis=0)],
        axis=1,
    )
    hi, lo = split2(side)
    placed = dot(jnp.concatenate([hi, lo], axis=0), sel_ref[...], 1, 1)
    placed = placed[0:48] + placed[48:96]
    scale = (STEP * LIFT) * by_element(metric_ref, (8, 128))
    for v in range(6):
        for t in range(4):
            lanes = slice(128 * t, 128 * t + 128)
            value = placed[8 * v : 8 * v + 8, lanes]
            if t == 0:
                value = value + jnp.where(low, lift[v][0], 0.0)
            if t == 3:
                value = value + jnp.where(low, 0.0, lift[v][0])
            out_ref[v, :, lanes] = base_ref[v, :, lanes] + scale * value


SM = pl.BlockSpec(memory_space=pltpu.SMEM)
VM = pl.BlockSpec(memory_space=pltpu.VMEM)


def call(kernel, outs, scalars, args, first=False, free=()):
    outs = [s if isinstance(s[0], tuple) else (s, f32) for s in outs]
    held = [
        a if first or n in scalars else pltpu.with_memory_space_constraint(a, pltpu.VMEM)
        for n, a in enumerate(args)
    ]
    return pl.pallas_call(
        kernel,
        out_shape=[jax.ShapeDtypeStruct(*s) if n in free else pltpu.VMEM(*s) for n, s in enumerate(outs)],
        in_specs=[SM if n in scalars else VM for n in range(len(args))],
        out_specs=[VM] * len(outs),
    )(*held)


def section(state, material, metric, mortar_proj, mortar_map, mortar_count, neighbours):
    groups = lax.axis_size("grp")
    n_elem = lax.axis_size("elem")
    elements = jnp.transpose(state, (1, 0, 2))
    info = mortar_map[0]
    counts = mortar_count[0]
    select = jnp.asarray(face_select(), bf16)
    orients = jnp.asarray(orient_table(), bf16)
    deriv = deriv_table()
    d_hi = deriv.astype(bf16)
    d_lo = (deriv - d_hi.astype(np.float32)).astype(bf16)
    derivs = jnp.asarray(np.concatenate([d_hi, d_lo], axis=1))
    codes_a = jnp.asarray(code_table([{0: 1, 1: 8, 3: 48}, {2: 1}, {4: 1}]), bf16)
    codes_c = jnp.asarray(code_table([{n: 1} for n in range(5)]), bf16)

    grp, up, down, faces, mine, kept = call(
        trace_kernel,
        [(groups, CAPG, 512), (CAPS, 512), (CAPS, 512), (144, 128), (groups, CAPG, 512), ((8, SLOTS), jnp.int32)],
        {1},
        (elements, material, info, mortar_proj, select, orients, codes_a),
        first=True,
        free=(0,),
    )
    above = lax.ppermute(down, "elem", [(i + 1, i) for i in range(n_elem - 1)])
    below = lax.ppermute(up, "elem", [(i, i + 1) for i in range(n_elem - 1)])
    held = call(
        local_kernel,
        [(6, 8, 512), (144, 128), (SLOTS, 640), ((384, 256), bf16), ((384, 512), bf16)],
        {1, 2, 3},
        (elements, material, metric, counts, neighbours, faces, derivs, kept, mortar_proj, codes_c),
    )
    arrived = lax.all_to_all(grp, "grp", split_axis=0, concat_axis=0, tiled=True)
    (new,) = call(
        mortar_kernel,
        [(6, 8, 512)],
        {6},
        (mine, up, down, arrived, above, below, metric, select, orients, *held),
        free=(0,),
    )
    return jnp.transpose(new, (1, 0, 2))


def solution(mesh):
    return jax.shard_map(
        section,
        mesh=mesh,
        in_specs=(
            P(("elem", "grp"), None, None),
            P(("elem", "grp")),
            P(("elem", "grp")),
            P(),
            P(("elem", "grp"), None, None),
            P(("elem", "grp"), None),
            P(("elem", "grp"), None),
        ),
        out_specs=P(("elem", "grp"), None, None),
        check_vma=False,
    )
```

```python
import functools

import jax
import jax.numpy as jnp
import numpy as np
from jax import lax
from jax.experimental import pallas as pl
from jax.experimental.pallas import tpu as pltpu
from jax.sharding import PartitionSpec as P


CAPG = 8
CAPS = 32
SLOTS = 128
STEP = 0.002
LIFT = 49.0

f32 = jnp.float32
bf16 = jnp.bfloat16


def cheb_matrix():
    points = -np.cos(np.pi * np.arange(8) / 7.0)
    factor = np.array([2.0, 1.0, 1.0, 1.0, 1.0, 1.0, 1.0, 2.0])
    alternating = np.where(np.arange(8) % 2 == 0, 1.0, -1.0)
    scaled = factor * alternating
    differ = points[:, None] - points[None, :] + np.eye(8)
    matrix = scaled[:, None] / scaled[None, :] / differ
    matrix = matrix * (1.0 - np.eye(8))
    return (matrix - np.eye(8) * matrix.sum(axis=1)[:, None]).astype(np.float32)


def face_select():
    grid = np.arange(512).reshape(8, 8, 8)
    planes = [grid[:, 0], grid[:, 7], grid[:, :, 0], grid[:, :, 7]]
    nodes = np.concatenate([p.reshape(64) for p in planes])
    return (np.arange(512)[:, None] == nodes[None, :]).astype(np.float32)


def orient_table():
    first, second = np.meshgrid(np.arange(8), np.arange(8), indexing="ij")
    out = np.zeros((128, 1024), np.float32)
    for orient in range(8):
        p, r = (second, first) if orient & 4 else (first, second)
        p = 7 - p if orient & 1 else p
        r = 7 - r if orient & 2 else r
        source = (8 * p + r).reshape(64)
        for half in range(2):
            out[half * 64 + source, orient * 128 + half * 64 + np.arange(64)] = 1.0
    return out


def deriv_table():
    d = cheb_matrix()
    along_b = np.kron(np.eye(2), np.kron(d, np.eye(8))).T
    along_c = np.kron(np.eye(16), d).T
    return np.concatenate([along_b, along_c], axis=0).astype(np.float32)


def code_table(rows):
    out = np.zeros((16, 128 * len(rows)), np.float32)
    for block, weights in enumerate(rows):
        for row, weight in weights.items():
            out[row, block * 128 : (block + 1) * 128] = weight
    return out


def dot(a, b, ca=1, cb=0):
    return lax.dot_general(a, b, (((ca,), (cb,)), ((), ())), preferred_element_type=f32)


def split2(x):
    hi = x.astype(bf16)
    return hi, (x - hi.astype(f32)).astype(bf16)


def split3(x):
    hi = x.astype(bf16)
    rest = x - hi.astype(f32)
    mid = rest.astype(bf16)
    return hi, mid, (rest - mid.astype(f32)).astype(bf16)


def lane_low(shape):
    return lax.broadcasted_iota(jnp.int32, shape, len(shape) - 1) % 128 < 64


def swap(x):
    return pltpu.roll(x, 64, 1)


def join_pair(low, a, b):
    return jnp.where(low, a, swap(b))


def by_element(ref, shape):
    row = lax.broadcasted_iota(jnp.int32, shape, 0)
    out = jnp.full(shape, ref[0], f32) if ref.dtype == f32 else jnp.full(shape, ref[0].astype(f32), f32)
    for e in range(1, 8):
        out = jnp.where(row == e, ref[e].astype(f32), out)
    return out


def project_blocks(proj_ref):
    zero = jnp.zeros((64, 64), f32)
    blocks = []
    for s in range(4):
        p = proj_ref[s]
        top = jnp.concatenate([p, zero], axis=1)
        bottom = jnp.concatenate([zero, p], axis=1)
        blocks.append(jnp.concatenate([top, bottom], axis=0))
    return blocks


def slot_material(mat_ref, element):
    out = jnp.zeros(element.shape, f32)
    for e in range(8):
        out = jnp.where(element == e, mat_ref[e].astype(f32), out)
    return out


def code_rows(rows):
    pad = [jnp.zeros((1, SLOTS), f32)] * (16 - len(rows))
    return jnp.concatenate(rows + pad, axis=0).astype(bf16)


def trace_kernel(
    state_ref, mat_ref, map_ref, proj_ref, sel_ref, orient_ref, code_ref, grp_ref, even_ref, odd_ref, face_ref, mine_ref, info_ref,
):
    low = lane_low((8, 128))
    flat = state_ref[...].reshape(48, 512)
    picked = dot(jnp.concatenate(split3(flat), axis=0), sel_ref[...])
    picked = picked[0:48] + picked[48:96] + picked[96:144]
    pairs = []
    for v in range(6):
        x = state_ref[v]
        pairs.append(
            [
                jnp.where(low, x[:, 0:128], x[:, 384:512]),
                picked[8 * v : 8 * v + 8, 0:128],
                picked[8 * v : 8 * v + 8, 128:256],
            ]
        )
    rows = []
    for j in range(3):
        for d in range(3):
            first, second = pairs[2 * j][d], pairs[2 * j + 1][d]
            rows.append(jnp.where(low, first, swap(second)))
            rows.append(jnp.where(low, swap(first), second))
    faces = jnp.concatenate(rows, axis=0)
    face_ref[...] = faces
    hi, lo = split2(faces)
    table = dot(jnp.concatenate([hi, lo], axis=0), orient_ref[...]).astype(bf16)
    info = jnp.concatenate([map_ref[...]] * 2, axis=0)
    slot = lax.broadcasted_iota(jnp.int32, (8, SLOTS), 1)
    turned = jnp.where(slot < 96, pltpu.roll(info, 96, 1), pltpu.roll(info, 32, 1))
    odd = jnp.bitwise_and(lax.axis_index("elem"), 1) == 1
    info = jnp.where((slot >= 64) & odd, turned, info)
    info_ref[...] = info
    element, face, sub, orient = (info[i : i + 1] for i in range(4))
    material = slot_material(mat_ref, element)
    codes = code_rows([element.astype(f32), face.astype(f32), sub.astype(f32), orient.astype(f32), material])
    spread = dot(codes, code_ref[...], 0, 0)
    index = spread[:, 0:128].astype(jnp.int32)
    sub_of = spread[:, 128:256].astype(jnp.int32)
    lane = lax.broadcasted_iota(jnp.int32, (SLOTS, 128), 1)
    one_hot = jnp.concatenate(
        [jnp.where(index == lane + 128 * t, 1.0, 0.0).astype(bf16) for t in range(3)], axis=1
    )
    columns = []
    for part in range(6):
        block = table[48 * part : 48 * part + 48]
        columns.append(jnp.concatenate([block[:, 128 * o : 128 * o + 128] for o in range(8)], axis=0))
    gathered = dot(one_hot, jnp.concatenate(columns, axis=1))
    x_hi = jnp.concatenate([gathered[:, 128 * j : 128 * j + 128] for j in range(3)], axis=0)
    x_lo = jnp.concatenate([gathered[:, 384 + 128 * j : 512 + 128 * j] for j in range(3)], axis=0)
    b_hi, b_lo = split2(jnp.concatenate(project_blocks(proj_ref), axis=0))
    h = x_hi.astype(bf16)
    wide = dot(
        jnp.concatenate([h, x_lo.astype(bf16)], axis=1), jnp.concatenate([b_hi, b_hi], axis=1), 1, 1
    ) + dot(h, b_lo, 1, 1)

    def put(at, value):
        lanes = slice(at, at + 128)
        for g in range(8):
            grp_ref[g, :, lanes] = value[8 * g : 8 * g + 8]
            mine_ref[g, :, lanes] = value[8 * g : 8 * g + 8]
        even_ref[:, lanes] = value[64:96]
        odd_ref[:, lanes] = value[96:128]

    for j in range(3):
        r = slice(128 * j, 128 * j + 128)
        w = x_hi[r] + x_lo[r]
        for s in range(4):
            w = jnp.where(sub_of == s + 1, wide[r, 128 * s : 128 * s + 128], w)
        put(128 * j, w)
    put(384, 1.4 + 0.27 * spread[:, 256:384])


def hllc_correction(u, g, normal, own):
    inv = 1.0 / u[0]
    vel = [u[1] * inv, u[2] * inv, u[3] * inv]
    p = (g - 1.0) * (u[4] - 0.5 * (u[1] * vel[0] + u[2] * vel[1] + u[3] * vel[2]))
    s = normal[0] * vel[0] + normal[1] * vel[1] + normal[2] * vel[2]
    c = jnp.sqrt(g * p * inv)
    lower, upper = s - c, s + c
    left = jnp.minimum(lower, swap(lower))
    right = jnp.maximum(upper, swap(upper))
    wave = jnp.where(own, left, right)
    relative = wave - s
    mass = u[0] * relative
    part = mass * s - p
    middle = (part - swap(part)) / (mass - swap(mass))
    chi = mass / (wave - middle)
    shift = middle - s
    star = [
        chi,
        chi * (vel[0] + shift * normal[0]),
        chi * (vel[1] + shift * normal[1]),
        chi * (vel[2] + shift * normal[2]),
        chi * (u[4] * inv + shift * (middle + p / mass)),
        chi * (u[5] * inv),
    ]
    flux = [
        u[0] * s,
        u[1] * s + p * normal[0],
        u[2] * s + p * normal[1],
        u[3] * s + p * normal[2],
        (u[4] + p) * s,
        u[5] * s,
    ]
    use_star = jnp.where(own, -wave, wave) > 0.0
    take_own = (left >= 0.0) | (middle >= 0.0)
    out = []
    for v in range(6):
        side = jnp.where(use_star, wave * (star[v] - u[v]), 0.0)
        out.append(jnp.where(take_own, -side, flux[v] - swap(flux[v] + side)))
    return out


def paired(own, mine, theirs):
    return jnp.where(own, mine, swap(theirs)), jnp.where(own, swap(mine), theirs)


def local_kernel(
    state_ref, mat_ref, metric_ref, count_ref, near_ref, face_ref, deriv_ref, info_ref, proj_ref, code_ref,
    base_ref, local_ref, spread_ref, hot_ref, back_ref,
):
    info = info_ref[...]
    element, face, sub, orient = (info[i : i + 1] for i in range(4))
    slot = lax.broadcasted_iota(jnp.int32, (1, SLOTS), 1)
    odd = jnp.bitwise_and(lax.axis_index("elem"), 1)
    side = jnp.bitwise_xor(jnp.bitwise_and(lax.shift_right_logical(slot, 5), 1), odd)
    group = jnp.where(slot < 64, lax.shift_right_logical(slot, 3), 8 + side)
    position = jnp.where(slot < 64, jnp.bitwise_and(slot, 7), jnp.bitwise_and(slot, 31))
    limit = jnp.zeros((1, SLOTS), jnp.int32)
    for n in range(10):
        limit = jnp.where(group == n, count_ref[n], limit)
    alive = jnp.where(position < limit, 1.0, 0.0)
    sign = jnp.where(jnp.bitwise_and(face, 1) == 1, 1.0, -1.0)
    axis = lax.shift_right_logical(face, 1)
    codes = code_rows(
        [sub.astype(f32), alive] + [jnp.where(axis == d, sign, 0.0) for d in range(3)]
    )
    spread_ref[...] = dot(codes, code_ref[...], 0, 0)
    index = 48 * orient + 8 * face + element
    row = lax.broadcasted_iota(jnp.int32, (384, SLOTS), 0)
    beta = jnp.where(sub == 0, 1.0, 0.25)
    hot = jnp.where(row == index, beta, 0.0).astype(bf16)
    hot_ref[:, 0:128] = hot
    hot_ref[:, 128:256] = hot
    b_hi, b_lo = split2(jnp.concatenate(project_blocks(proj_ref), axis=1))
    back_ref[0:128, :] = b_hi
    back_ref[128:256, :] = b_hi
    back_ref[256:384, :] = b_lo
    heat = 1.4 + 0.27 * by_element(mat_ref, (8, 512))
    u = [state_ref[v] for v in range(6)]
    inv = 1.0 / u[0]
    vel = [u[1] * inv, u[2] * inv, u[3] * inv]
    p = (heat - 1.0) * (u[4] - 0.5 * (u[1] * vel[0] + u[2] * vel[1] + u[3] * vel[2]))
    fluxes = []
    for d in range(3):
        s = vel[d]
        f = [u[0] * s, u[1] * s, u[2] * s, u[3] * s, (u[4] + p) * s, u[5] * s]
        f[1 + d] = f[1 + d] + p
        fluxes.append(f)
    rows = []
    for v in range(6):
        for t in range(4):
            r = slice(128 * t, 128 * t + 128)
            rows.append(jnp.concatenate([fluxes[1][v][:, r], fluxes[2][v][:, r]], axis=1))
    hi, lo = split2(jnp.concatenate(rows, axis=0))
    d_hi, d_lo = deriv_ref[:, 0:128], deriv_ref[:, 128:256]
    main = dot(jnp.concatenate([hi, lo], axis=0), d_hi)
    bc = main[0:192] + main[192:384] + dot(hi, d_lo)
    low = lane_low((8, 128))
    deriv = cheb_matrix()
    scale = STEP * by_element(metric_ref, (8, 128))
    for v in range(6):
        x = [fluxes[0][v][:, 128 * t : 128 * t + 128] for t in range(4)]
        xs = [swap(a) for a in x]
        for t in range(4):
            acc = bc[32 * v + 8 * t : 32 * v + 8 * t + 8]
            for k in range(4):
                same = jnp.where(low, float(deriv[2 * t, 2 * k]), float(deriv[2 * t + 1, 2 * k + 1]))
                cross = jnp.where(low, float(deriv[2 * t, 2 * k + 1]), float(deriv[2 * t + 1, 2 * k]))
                acc = acc + same * x[k] + cross * xs[k]
            r = slice(128 * t, 128 * t + 128)
            base_ref[v, :, r] = u[v][:, r] - scale * acc
    faces = face_ref[...]
    lane = lax.broadcasted_iota(jnp.int32, (8, 256), 1)
    hot, live = [], []
    for k in range(6):
        near = jnp.broadcast_to(near_ref[:, k : k + 1], (8, 256))
        live.append((near >= 0)[:, 0:128])
        target = 8 * (k ^ 1) + near
        hit = (jnp.bitwise_and(lane, 63) == target) & (near >= 0) & (lane < 192)
        hot.append(jnp.where(hit, 1.0, 0.0))
    hot = jnp.concatenate(hot, axis=0).astype(bf16)
    heat_rows = jnp.concatenate([heat[:, 0:128]] * 6, axis=0)
    table = jnp.concatenate([faces[0:48], faces[48:96], faces[96:144], heat_rows], axis=1)
    gap = jnp.zeros((16, 512), bf16)
    terms = []
    for term in split3(table):
        terms += [term, gap]
    terms.append(jnp.zeros((64, 512), bf16))
    theirs = dot(hot, jnp.concatenate(terms, axis=0))
    own = lane_low((48, 128))
    row = lax.broadcasted_iota(jnp.int32, (48, 128), 0)
    sign = jnp.where(jnp.bitwise_and(row, 8) != 0, 1.0, -1.0)
    normal = [jnp.where(lax.shift_right_logical(row, 4) == d, sign, 0.0) for d in range(3)]
    states = []
    for j in range(3):
        states += paired(own, faces[48 * j : 48 * j + 48], theirs[:, 128 * j : 128 * j + 128])
    g = jnp.where(own, heat_rows, theirs[:, 384:512])
    corr = hllc_correction(states, g, normal, own)
    for j in range(3):
        packed = join_pair(own, corr[2 * j], corr[2 * j + 1])
        for k in range(6):
            local_ref[48 * j + 8 * k : 48 * j + 8 * k + 8, :] = jnp.where(
                live[k], packed[8 * k : 8 * k + 8], 0.0
            )


def mortar_kernel(
    grp_ref, even_ref, odd_ref, from_grp_ref, from_even_ref, from_odd_ref, metric_ref,
    sel_ref, orient_ref, base_ref, local_ref, spread_ref, hot_ref, back_ref, out_ref,
):
    chunk = 32
    own = lane_low((chunk, 128))
    packed = [[], [], []]
    for start in range(0, SLOTS, chunk):
        r = slice(start, start + chunk)

        def rows(grp, even, odd, at):
            lanes = slice(at, at + 128)
            if start < 64:
                return jnp.concatenate([grp[start // 8 + n, :, lanes] for n in range(chunk // 8)], axis=0)
            return (even if start < 96 else odd)[:, lanes]

        mine = functools.partial(rows, grp_ref, even_ref, odd_ref)
        theirs = functools.partial(rows, from_grp_ref, from_even_ref, from_odd_ref)
        states = []
        for j in range(3):
            states += paired(own, mine(128 * j), theirs(128 * j))
        g = jnp.where(own, mine(384), theirs(384))
        live = spread_ref[r, 128:256] > 0.5
        normal = [spread_ref[r, 256 + 128 * d : 384 + 128 * d] for d in range(3)]
        corr = hllc_correction(states, g, normal, own)
        for j in range(3):
            packed[j].append(jnp.where(live, join_pair(own, corr[2 * j], corr[2 * j + 1]), 0.0))
    corr = jnp.concatenate(packed[0] + packed[1] + packed[2], axis=0)
    hi, lo = split2(corr)
    wide = dot(jnp.concatenate([hi, lo, hi], axis=1), back_ref[...])
    sub_of = spread_ref[:, 0:128].astype(jnp.int32)
    back = []
    for j in range(3):
        r = slice(128 * j, 128 * j + 128)
        y = corr[r]
        for s in range(4):
            y = jnp.where(sub_of == s + 1, wide[r, 128 * s : 128 * s + 128], y)
        back.append(y)
    hi, lo = split2(jnp.concatenate(back, axis=1))
    summed = dot(hot_ref[...], jnp.concatenate([hi, lo], axis=0))
    rows = []
    for j in range(3):
        lanes = slice(128 * j, 128 * j + 128)
        rows.append(jnp.concatenate([summed[48 * o : 48 * o + 48, lanes] for o in range(8)], axis=1))
    hi, lo = split2(jnp.concatenate(rows, axis=0))
    turned = dot(jnp.concatenate([hi, lo], axis=0), orient_ref[...], 1, 1)
    total = turned[0:144] + turned[144:288] + local_ref[...]
    low = lane_low((8, 128))
    lift = []
    for v in range(6):
        at = 48 * (v // 2)
        parts = []
        for d in range(3):
            first = total[at + 16 * d : at + 16 * d + 8]
            second = total[at + 16 * d + 8 : at + 16 * d + 16]
            if v % 2 == 0:
                parts.append(jnp.where(low, first, swap(second)))
            else:
                parts.append(jnp.where(low, swap(first), second))
        lift.append(parts)
    side = jnp.concatenate(
        [jnp.concatenate([lift[v][1] for v in range(6)], axis=0), jnp.concatenate([lift[v][2] for v in range(6)], axis=0)],
        axis=1,
    )
    hi, lo = split2(side)
    placed = dot(jnp.concatenate([hi, lo], axis=0), sel_ref[...], 1, 1)
    placed = placed[0:48] + placed[48:96]
    scale = (STEP * LIFT) * by_element(metric_ref, (8, 128))
    for v in range(6):
        for t in range(4):
            lanes = slice(128 * t, 128 * t + 128)
            value = placed[8 * v : 8 * v + 8, lanes]
            if t == 0:
                value = value + jnp.where(low, lift[v][0], 0.0)
            if t == 3:
                value = value + jnp.where(low, 0.0, lift[v][0])
            out_ref[v, :, lanes] = base_ref[v, :, lanes] + scale * value


SM = pl.BlockSpec(memory_space=pltpu.SMEM)
VM = pl.BlockSpec(memory_space=pltpu.VMEM)


def call(kernel, outs, scalars, args, first=False, free=()):
    outs = [s if isinstance(s[0], tuple) else (s, f32) for s in outs]
    held = [
        a if first or n in scalars else pltpu.with_memory_space_constraint(a, pltpu.VMEM)
        for n, a in enumerate(args)
    ]
    return pl.pallas_call(
        kernel,
        out_shape=[jax.ShapeDtypeStruct(*s) if n in free else pltpu.VMEM(*s) for n, s in enumerate(outs)],
        in_specs=[SM if n in scalars else VM for n in range(len(args))],
        out_specs=[VM] * len(outs),
    )(*held)


def section(state, material, metric, mortar_proj, mortar_map, mortar_count, neighbours):
    groups = lax.axis_size("grp")
    n_elem = lax.axis_size("elem")
    elements = jnp.transpose(state, (1, 0, 2))
    info = mortar_map[0]
    counts = mortar_count[0]
    select = jnp.asarray(face_select(), bf16)
    orients = jnp.asarray(orient_table(), bf16)
    deriv = deriv_table()
    d_hi = deriv.astype(bf16)
    d_lo = (deriv - d_hi.astype(np.float32)).astype(bf16)
    derivs = jnp.asarray(np.concatenate([d_hi, d_lo], axis=1))
    codes_a = jnp.asarray(code_table([{0: 1, 1: 8, 3: 48}, {2: 1}, {4: 1}]), bf16)
    codes_c = jnp.asarray(code_table([{n: 1} for n in range(5)]), bf16)

    grp, even, odd, faces, mine, kept = call(
        trace_kernel,
        [(groups, CAPG, 512), (CAPS, 512), (CAPS, 512), (144, 128), (groups, CAPG, 512), ((8, SLOTS), jnp.int32)],
        {1},
        (elements, material, info, mortar_proj, select, orients, codes_a),
        first=True,
        free=(0,),
    )
    pairs = [[(i + n, i + 1 - n) for i in range(first, n_elem - 1, 2) for n in range(2)] for first in range(2)]
    from_odd = lax.ppermute(odd, "elem", pairs[1])
    arrived = lax.all_to_all(grp, "grp", split_axis=0, concat_axis=0, tiled=True)
    from_even = lax.ppermute(even, "elem", pairs[0])
    held = call(
        local_kernel,
        [(6, 8, 512), (144, 128), (SLOTS, 640), ((384, 256), bf16), ((384, 512), bf16)],
        {1, 2, 3},
        (elements, material, metric, counts, neighbours, faces, derivs, kept, mortar_proj, codes_c),
    )
    (new,) = call(
        mortar_kernel,
        [(6, 8, 512)],
        {6},
        (mine, even, odd, arrived, from_even, from_odd, metric, select, orients, *held),
        free=(0,),
    )
    return jnp.transpose(new, (1, 0, 2))


def solution(mesh):
    return jax.shard_map(
        section,
        mesh=mesh,
        in_specs=(
            P(("elem", "grp"), None, None),
            P(("elem", "grp")),
            P(("elem", "grp")),
            P(),
            P(("elem", "grp"), None, None),
            P(("elem", "grp"), None),
            P(("elem", "grp"), None),
        ),
        out_specs=P(("elem", "grp"), None, None),
        check_vma=False,
    )
```

```python
import jax
import jax.numpy as jnp
import numpy as np
from jax import lax
from jax.experimental import pallas as pl
from jax.experimental.pallas import tpu as pltpu
from jax.sharding import PartitionSpec as P


CAPG = 8
CAPS = 32
SLOTS = 128
STEP = 0.002
LIFT = 49.0

f32 = jnp.float32
bf16 = jnp.bfloat16


def cheb_matrix():
    points = -np.cos(np.pi * np.arange(8) / 7.0)
    factor = np.array([2.0, 1.0, 1.0, 1.0, 1.0, 1.0, 1.0, 2.0])
    alternating = np.where(np.arange(8) % 2 == 0, 1.0, -1.0)
    scaled = factor * alternating
    differ = points[:, None] - points[None, :] + np.eye(8)
    matrix = scaled[:, None] / scaled[None, :] / differ
    matrix = matrix * (1.0 - np.eye(8))
    return (matrix - np.eye(8) * matrix.sum(axis=1)[:, None]).astype(np.float32)


def face_select():
    grid = np.arange(512).reshape(8, 8, 8)
    planes = [grid[:, 0], grid[:, 7], grid[:, :, 0], grid[:, :, 7]]
    nodes = np.concatenate([p.reshape(64) for p in planes])
    return (np.arange(512)[:, None] == nodes[None, :]).astype(np.float32)


def orient_table():
    first, second = np.meshgrid(np.arange(8), np.arange(8), indexing="ij")
    out = np.zeros((128, 1024), np.float32)
    for orient in range(8):
        p, r = (second, first) if orient & 4 else (first, second)
        p = 7 - p if orient & 1 else p
        r = 7 - r if orient & 2 else r
        source = (8 * p + r).reshape(64)
        for half in range(2):
            out[half * 64 + source, orient * 128 + half * 64 + np.arange(64)] = 1.0
    return out


def deriv_table():
    d = cheb_matrix()
    along_b = np.kron(np.eye(2), np.kron(d, np.eye(8))).T
    along_c = np.kron(np.eye(16), d).T
    return np.concatenate([along_b, along_c], axis=0).astype(np.float32)


def code_table(rows):
    out = np.zeros((16, 128 * len(rows)), np.float32)
    for block, weights in enumerate(rows):
        for row, weight in weights.items():
            out[row, block * 128 : (block + 1) * 128] = weight
    return out


def dot(a, b, ca=1, cb=0):
    return lax.dot_general(a, b, (((ca,), (cb,)), ((), ())), preferred_element_type=f32)


def split2(x):
    hi = x.astype(bf16)
    return hi, (x - hi.astype(f32)).astype(bf16)


def split3(x):
    hi = x.astype(bf16)
    rest = x - hi.astype(f32)
    mid = rest.astype(bf16)
    return hi, mid, (rest - mid.astype(f32)).astype(bf16)


def lane_low(shape):
    return lax.broadcasted_iota(jnp.int32, shape, len(shape) - 1) % 128 < 64


def swap(x):
    return pltpu.roll(x, 64, 1)


def join_pair(low, a, b):
    return jnp.where(low, a, swap(b))


def by_element(ref, shape):
    row = lax.broadcasted_iota(jnp.int32, shape, 0)
    out = jnp.full(shape, ref[0], f32) if ref.dtype == f32 else jnp.full(shape, ref[0].astype(f32), f32)
    for e in range(1, 8):
        out = jnp.where(row == e, ref[e].astype(f32), out)
    return out


def project_blocks(proj_ref):
    zero = jnp.zeros((64, 64), f32)
    blocks = []
    for s in range(4):
        p = proj_ref[s]
        top = jnp.concatenate([p, zero], axis=1)
        bottom = jnp.concatenate([zero, p], axis=1)
        blocks.append(jnp.concatenate([top, bottom], axis=0))
    return blocks


def slot_material(mat_ref, element):
    out = jnp.zeros(element.shape, f32)
    for e in range(8):
        out = jnp.where(element == e, mat_ref[e].astype(f32), out)
    return out


def code_rows(rows):
    pad = [jnp.zeros((1, SLOTS), f32)] * (16 - len(rows))
    return jnp.concatenate(rows + pad, axis=0).astype(bf16)


def selection():
    lane = lax.broadcasted_iota(jnp.int32, (1, 256), 1)
    far = jnp.bitwise_and(lax.shift_right_logical(lane, 6), 1)
    p = jnp.bitwise_and(lax.shift_right_logical(lane, 3), 7)
    r = jnp.bitwise_and(lane, 7)
    node = 64 * p + jnp.where(lane < 128, r + 56 * far, 8 * r + 7 * far)
    row = lax.broadcasted_iota(jnp.int32, (512, 256), 0)
    return jnp.where(row == node, 1.0, 0.0).astype(bf16)


def orientations():
    lane = lax.broadcasted_iota(jnp.int32, (1, 1024), 1)
    half = jnp.bitwise_and(lane, 64)
    p = jnp.bitwise_and(lax.shift_right_logical(lane, 3), 7)
    r = jnp.bitwise_and(lane, 7)
    turn = jnp.bitwise_and(lane, 512) != 0
    p, r = jnp.where(turn, r, p), jnp.where(turn, p, r)
    p = jnp.where(jnp.bitwise_and(lane, 128) != 0, 7 - p, p)
    r = jnp.where(jnp.bitwise_and(lane, 256) != 0, 7 - r, r)
    row = lax.broadcasted_iota(jnp.int32, (128, 1024), 0)
    return jnp.where(row == half + 8 * p + r, 1.0, 0.0).astype(bf16)


def trace_kernel(
    state_hbm, mat_hbm, map_hbm, proj_hbm, grp_hbm, even_ref, odd_ref, face_ref, mine_ref, info_ref,
    state_ref, mat_ref, map_ref, proj_ref, sel_ref, orient_ref, in_sem, out_sem,
):
    loads = [
        pltpu.make_async_copy(src, dst, in_sem.at[n])
        for n, (src, dst) in enumerate(
            [(state_hbm, state_ref), (mat_hbm, mat_ref), (map_hbm, map_ref), (proj_hbm, proj_ref)]
        )
    ]
    for load in loads:
        load.start()
    sel_ref[...] = selection()
    orient_ref[...] = orientations()
    code_row = lax.broadcasted_iota(jnp.int32, (16, 128), 0)
    weights = jnp.where(code_row == 0, 1.0, jnp.where(code_row == 1, 8.0, jnp.where(code_row == 3, 48.0, 0.0)))
    spreads = jnp.concatenate(
        [weights, jnp.where(code_row == 2, 1.0, 0.0), jnp.where(code_row == 4, 1.0, 0.0)], axis=1
    ).astype(bf16)
    for load in loads:
        load.wait()
    low = lane_low((8, 128))
    flat = state_ref[...].reshape(48, 512)
    picked = dot(jnp.concatenate(split3(flat), axis=0), sel_ref[...])
    picked = picked[0:48] + picked[48:96] + picked[96:144]
    pairs = []
    for v in range(6):
        x = state_ref[v]
        pairs.append(
            [
                jnp.where(low, x[:, 0:128], x[:, 384:512]),
                picked[8 * v : 8 * v + 8, 0:128],
                picked[8 * v : 8 * v + 8, 128:256],
            ]
        )
    rows = []
    for j in range(3):
        for d in range(3):
            first, second = pairs[2 * j][d], pairs[2 * j + 1][d]
            rows.append(jnp.where(low, first, swap(second)))
            rows.append(jnp.where(low, swap(first), second))
    faces = jnp.concatenate(rows, axis=0)
    face_ref[...] = faces
    hi, lo = split2(faces)
    table = dot(jnp.concatenate([hi, lo], axis=0), orient_ref[...]).astype(bf16)
    info = jnp.concatenate([map_ref[...]] * 2, axis=0)
    slot = lax.broadcasted_iota(jnp.int32, (8, SLOTS), 1)
    turned = jnp.where(slot < 96, pltpu.roll(info, 96, 1), pltpu.roll(info, 32, 1))
    odd = jnp.bitwise_and(lax.axis_index("elem"), 1) == 1
    info = jnp.where((slot >= 64) & odd, turned, info)
    info_ref[...] = info
    element, face, sub, orient = (info[i : i + 1] for i in range(4))
    material = slot_material(mat_ref, element)
    codes = code_rows([element.astype(f32), face.astype(f32), sub.astype(f32), orient.astype(f32), material])
    spread = dot(codes, spreads, 0, 0)
    index = spread[:, 0:128].astype(jnp.int32)
    sub_of = spread[:, 128:256].astype(jnp.int32)
    lane = lax.broadcasted_iota(jnp.int32, (SLOTS, 128), 1)
    one_hot = jnp.concatenate(
        [jnp.where(index == lane + 128 * t, 1.0, 0.0).astype(bf16) for t in range(3)], axis=1
    )
    columns = []
    for part in range(6):
        block = table[48 * part : 48 * part + 48]
        columns.append(jnp.concatenate([block[:, 128 * o : 128 * o + 128] for o in range(8)], axis=0))
    gathered = dot(one_hot, jnp.concatenate(columns, axis=1))
    x_hi = jnp.concatenate([gathered[:, 128 * j : 128 * j + 128] for j in range(3)], axis=0)
    x_lo = jnp.concatenate([gathered[:, 384 + 128 * j : 512 + 128 * j] for j in range(3)], axis=0)
    b_hi, b_lo = split2(jnp.concatenate(project_blocks(proj_ref), axis=0))
    h = x_hi.astype(bf16)
    wide = dot(
        jnp.concatenate([h, x_lo.astype(bf16)], axis=1), jnp.concatenate([b_hi, b_hi], axis=1), 1, 1
    ) + dot(h, b_lo, 1, 1)
    stores = []

    def put(at, value):
        lanes = slice(at, at + 128)
        for g in range(8):
            mine_ref[g, :, lanes] = value[8 * g : 8 * g + 8]
        even_ref[:, lanes] = value[64:96]
        odd_ref[:, lanes] = value[96:128]
        store = pltpu.make_async_copy(mine_ref.at[:, :, lanes], grp_hbm.at[:, :, lanes], out_sem.at[at // 128])
        store.start()
        stores.append(store)

    put(384, 1.4 + 0.27 * spread[:, 256:384])
    for j in range(3):
        r = slice(128 * j, 128 * j + 128)
        w = x_hi[r] + x_lo[r]
        for s in range(4):
            w = jnp.where(sub_of == s + 1, wide[r, 128 * s : 128 * s + 128], w)
        put(128 * j, w)
    for store in stores:
        store.wait()


def primitives(u, g, n):
    inv = 1.0 / u[0]
    p = (g - 1.0) * (u[4] - 0.5 * inv * (u[1] * u[1] + u[2] * u[2] + u[3] * u[3]))
    s = (n[0] * u[1] + n[1] * u[2] + n[2] * u[3]) * inv
    return p, s, jnp.sqrt(g * p * inv)


def flux_of(u, p, s, n):
    return [u[0] * s, u[1] * s + p * n[0], u[2] * s + p * n[1], u[3] * s + p * n[2], (u[4] + p) * s, u[5] * s]


def hllc(u_l, u_r, prim_l, prim_r, n):
    (p_l, s_l, c_l), (p_r, s_r, c_r) = prim_l, prim_r
    left = jnp.minimum(s_l - c_l, s_r - c_r)
    right = jnp.maximum(s_l + c_l, s_r + c_r)
    mass_l = u_l[0] * (left - s_l)
    mass_r = u_r[0] * (right - s_r)
    middle = (p_r - p_l + mass_l * s_l - mass_r * s_r) / (mass_l - mass_r)
    take = (left >= 0.0) | (middle >= 0.0)
    u = [jnp.where(take, x, y) for x, y in zip(u_l, u_r)]
    p = jnp.where(take, p_l, p_r)
    s = jnp.where(take, s_l, s_r)
    mass = jnp.where(take, mass_l, mass_r)
    wave = jnp.where(take, left, right)
    use_star = jnp.where(take, -left, right) > 0.0
    a = jnp.where(use_star, wave * (middle - s) / (wave - middle), 0.0)
    speed = s + a
    push = a * mass
    lift = p + push
    return [
        u[0] * speed,
        u[1] * speed + lift * n[0],
        u[2] * speed + lift * n[1],
        u[3] * speed + lift * n[2],
        (u[4] + p) * speed + push * middle,
        u[5] * speed,
    ]


def two_halves(low, first, second):
    return jnp.where(low, first, swap(second)), jnp.where(low, swap(first), second)


def local_kernel(
    state_ref, mat_ref, metric_ref, count_ref, near_ref, face_ref, deriv_ref, info_ref, proj_ref, code_ref,
    mine_ref, even_ref, odd_ref, base_ref, local_ref, sub_ref, own_ref, scale_ref, hot_ref, back_ref,
):
    info = info_ref[...]
    element, face, sub, orient = (info[i : i + 1] for i in range(4))
    slot = lax.broadcasted_iota(jnp.int32, (1, SLOTS), 1)
    odd = jnp.bitwise_and(lax.axis_index("elem"), 1)
    side = jnp.bitwise_xor(jnp.bitwise_and(lax.shift_right_logical(slot, 5), 1), odd)
    group = jnp.where(slot < 64, lax.shift_right_logical(slot, 3), 8 + side)
    position = jnp.where(slot < 64, jnp.bitwise_and(slot, 7), jnp.bitwise_and(slot, 31))
    limit = jnp.zeros((1, SLOTS), jnp.int32)
    for n in range(10):
        limit = jnp.where(group == n, count_ref[n], limit)
    alive = jnp.where(position < limit, 1.0, 0.0)
    sign = jnp.where(jnp.bitwise_and(face, 1) == 1, 1.0, -1.0)
    axis = lax.shift_right_logical(face, 1)
    codes = code_rows(
        [sub.astype(f32), alive] + [jnp.where(axis == d, sign, 0.0) for d in range(3)]
    )
    spread = dot(codes, code_ref[...], 0, 0)
    sub_ref[...] = spread[:, 0:128]
    index = 48 * orient + 8 * face + element
    row = lax.broadcasted_iota(jnp.int32, (384, SLOTS), 0)
    beta = jnp.where(sub == 0, 1.0, 0.25)
    hot = jnp.where(row == index, beta, 0.0).astype(bf16)
    hot_ref[:, 0:128] = hot
    hot_ref[:, 128:256] = hot
    b_hi, b_lo = split2(jnp.concatenate(project_blocks(proj_ref), axis=1))
    back_ref[0:128, :] = b_hi
    back_ref[128:256, :] = b_hi
    back_ref[256:384, :] = b_lo
    heat = 1.4 + 0.27 * by_element(mat_ref, (8, 512))
    u = [state_ref[v] for v in range(6)]
    inv = 1.0 / u[0]
    vel = [u[1] * inv, u[2] * inv, u[3] * inv]
    p = (heat - 1.0) * (u[4] - 0.5 * (u[1] * vel[0] + u[2] * vel[1] + u[3] * vel[2]))
    fluxes = []
    for d in range(3):
        s = vel[d]
        f = [u[0] * s, u[1] * s, u[2] * s, u[3] * s, (u[4] + p) * s, u[5] * s]
        f[1 + d] = f[1 + d] + p
        fluxes.append(f)
    rows = []
    for v in range(6):
        for t in range(4):
            r = slice(128 * t, 128 * t + 128)
            rows.append(jnp.concatenate([fluxes[1][v][:, r], fluxes[2][v][:, r]], axis=1))
    hi, lo = split2(jnp.concatenate(rows, axis=0))
    d_hi, d_lo = deriv_ref[:, 0:128], deriv_ref[:, 128:256]
    main = dot(jnp.concatenate([hi, lo], axis=0), d_hi)
    bc = main[0:192] + main[192:384] + dot(hi, d_lo)
    low = lane_low((8, 128))
    deriv = cheb_matrix()
    scale = STEP * by_element(metric_ref, (8, 128))
    for v in range(6):
        x = [fluxes[0][v][:, 128 * t : 128 * t + 128] for t in range(4)]
        xs = [swap(a) for a in x]
        for t in range(4):
            acc = bc[32 * v + 8 * t : 32 * v + 8 * t + 8]
            for k in range(4):
                same = jnp.where(low, float(deriv[2 * t, 2 * k]), float(deriv[2 * t + 1, 2 * k + 1]))
                cross = jnp.where(low, float(deriv[2 * t, 2 * k + 1]), float(deriv[2 * t + 1, 2 * k]))
                acc = acc + same * x[k] + cross * xs[k]
            r = slice(128 * t, 128 * t + 128)
            base_ref[v, :, r] = u[v][:, r] - scale * acc
    faces = face_ref[...]
    lane = lax.broadcasted_iota(jnp.int32, (8, 256), 1)
    hot, live = [], []
    for k in range(6):
        near = jnp.broadcast_to(near_ref[:, k : k + 1], (8, 256))
        live.append((near >= 0)[:, 0:128])
        target = 8 * (k ^ 1) + near
        hit = (jnp.bitwise_and(lane, 63) == target) & (near >= 0) & (lane < 192)
        hot.append(jnp.where(hit, 1.0, 0.0))
    hot = jnp.concatenate(hot, axis=0).astype(bf16)
    heat_rows = jnp.concatenate([heat[:, 0:128]] * 6, axis=0)
    table = jnp.concatenate([faces[0:48], faces[48:96], faces[96:144], heat_rows], axis=1)
    gap = jnp.zeros((16, 512), bf16)
    terms = []
    for term in split3(table):
        terms += [term, gap]
    terms.append(jnp.zeros((64, 512), bf16))
    theirs = dot(hot, jnp.concatenate(terms, axis=0))
    low = lane_low((48, 128))
    row = lax.broadcasted_iota(jnp.int32, (48, 128), 0)
    sign = jnp.where(jnp.bitwise_and(row, 8) != 0, 1.0, -1.0)
    normal = [jnp.where(lax.shift_right_logical(row, 4) == d, sign, 0.0) for d in range(3)]
    mine, other = [], []
    for j in range(3):
        x, y = faces[48 * j : 48 * j + 48], theirs[:, 128 * j : 128 * j + 128]
        mine += [x, swap(x)]
        other += [y, swap(y)]
    prim = primitives(mine, heat_rows, normal)
    flux = flux_of(mine, prim[0], prim[1], normal)
    through = hllc(mine, other, prim, primitives(other, theirs[:, 384:512], normal), normal)
    corr = [f - h for f, h in zip(flux, through)]
    for j in range(3):
        packed = join_pair(low, corr[2 * j], corr[2 * j + 1])
        for k in range(6):
            local_ref[48 * j + 8 * k : 48 * j + 8 * k + 8, :] = jnp.where(
                live[k], packed[8 * k : 8 * k + 8], 0.0
            )
    low = lane_low((64, 128))

    def rows(at):
        lanes = slice(at, at + 128)
        return (
            jnp.concatenate([mine_ref[g, :, lanes] for g in range(8)], axis=0),
            jnp.concatenate([even_ref[:, lanes], odd_ref[:, lanes]], axis=0),
        )

    states = []
    for j in range(3):
        states += two_halves(low, *rows(128 * j))
    g = jnp.where(low, *rows(384))
    slots = [
        jnp.where(low, spread[0:64, 128 * n : 128 * n + 128], spread[64:128, 128 * n : 128 * n + 128])
        for n in range(1, 5)
    ]
    prim = primitives(states, g, slots[1:])
    kept = [*states, *prim, *flux_of(states, prim[0], prim[1], slots[1:]), *slots]
    for n, x in enumerate(kept):
        own_ref[n] = x
    scale_ref[...] = (STEP * LIFT) * by_element(metric_ref, (8, 128))


def mortar_kernel(
    from_grp_ref, from_even_ref, from_odd_ref, sel_ref, orient_ref,
    base_ref, local_ref, sub_ref, own_ref, scale_ref, hot_ref, back_ref, out_ref,
):
    chunk = 16
    low = lane_low((chunk, 128))
    first, second = [[], [], []], [[], [], []]
    for at in range(0, 64, chunk):
        r = slice(at, at + chunk)

        def rows(lane):
            lanes = slice(lane, lane + 128)
            elem_ref, start = (from_even_ref, at) if at < 32 else (from_odd_ref, at - 32)
            grp = [from_grp_ref[at // 8 + n, :, lanes] for n in range(chunk // 8)]
            return jnp.concatenate(grp, axis=0), elem_ref[start : start + chunk, lanes]

        theirs = []
        for j in range(3):
            theirs += two_halves(low, *rows(128 * j))
        g = jnp.where(low, *rows(384))
        mine = [own_ref[n, r] for n in range(6)]
        normal = [own_ref[n, r] for n in range(16, 19)]
        live = own_ref[15, r] > 0.5
        prim = tuple(own_ref[n, r] for n in range(6, 9))
        through = hllc(mine, theirs, prim, primitives(theirs, g, normal), normal)
        corr = [jnp.where(live, own_ref[9 + n, r] - through[n], 0.0) for n in range(6)]
        for j in range(3):
            x, y = two_halves(low, corr[2 * j], corr[2 * j + 1])
            first[j].append(x)
            second[j].append(y)
    corr = jnp.concatenate([x for j in range(3) for x in first[j] + second[j]], axis=0)
    hi, lo = split2(corr)
    wide = dot(jnp.concatenate([hi, lo, hi], axis=1), back_ref[...])
    sub_of = sub_ref[...].astype(jnp.int32)
    back = []
    for j in range(3):
        r = slice(128 * j, 128 * j + 128)
        y = corr[r]
        for s in range(4):
            y = jnp.where(sub_of == s + 1, wide[r, 128 * s : 128 * s + 128], y)
        back.append(y)
    hi, lo = split2(jnp.concatenate(back, axis=1))
    summed = dot(hot_ref[...], jnp.concatenate([hi, lo], axis=0))
    rows = []
    for j in range(3):
        lanes = slice(128 * j, 128 * j + 128)
        rows.append(jnp.concatenate([summed[48 * o : 48 * o + 48, lanes] for o in range(8)], axis=1))
    hi, lo = split2(jnp.concatenate(rows, axis=0))
    turned = dot(jnp.concatenate([hi, lo], axis=0), orient_ref[...], 1, 1)
    total = turned[0:144] + turned[144:288] + local_ref[...]
    low = lane_low((8, 128))
    lift = []
    for v in range(6):
        at = 48 * (v // 2)
        parts = []
        for d in range(3):
            first = total[at + 16 * d : at + 16 * d + 8]
            second = total[at + 16 * d + 8 : at + 16 * d + 16]
            if v % 2 == 0:
                parts.append(jnp.where(low, first, swap(second)))
            else:
                parts.append(jnp.where(low, swap(first), second))
        lift.append(parts)
    side = jnp.concatenate(
        [jnp.concatenate([lift[v][1] for v in range(6)], axis=0), jnp.concatenate([lift[v][2] for v in range(6)], axis=0)],
        axis=1,
    )
    hi, lo = split2(side)
    placed = dot(jnp.concatenate([hi, lo], axis=0), sel_ref[...], 1, 1)
    placed = placed[0:48] + placed[48:96]
    scale = scale_ref[...]
    for v in range(6):
        for t in range(4):
            lanes = slice(128 * t, 128 * t + 128)
            value = placed[8 * v : 8 * v + 8, lanes]
            if t == 0:
                value = value + jnp.where(low, lift[v][0], 0.0)
            if t == 3:
                value = value + jnp.where(low, 0.0, lift[v][0])
            out_ref[v, :, lanes] = base_ref[v, :, lanes] + scale * value


SM = pl.BlockSpec(memory_space=pltpu.SMEM)
VM = pl.BlockSpec(memory_space=pltpu.VMEM)


def call(kernel, outs, scalars, args, free=()):
    outs = [s if isinstance(s[0], tuple) else (s, f32) for s in outs]
    held = [
        a if n in scalars else pltpu.with_memory_space_constraint(a, pltpu.VMEM)
        for n, a in enumerate(args)
    ]
    return pl.pallas_call(
        kernel,
        out_shape=[jax.ShapeDtypeStruct(*s) if n in free else pltpu.VMEM(*s) for n, s in enumerate(outs)],
        in_specs=[SM if n in scalars else VM for n in range(len(args))],
        out_specs=[VM] * len(outs),
        compiler_params=pltpu.CompilerParams(vmem_limit_bytes=16 << 20),
    )(*held)


def section(state, material, metric, mortar_proj, mortar_map, mortar_count, neighbours):
    groups = lax.axis_size("grp")
    n_elem = lax.axis_size("elem")
    elements = jnp.transpose(state, (1, 0, 2))
    info = mortar_map[0]
    counts = mortar_count[0]
    select = jnp.asarray(face_select(), bf16)
    orients = jnp.asarray(orient_table(), bf16)
    deriv = deriv_table()
    d_hi = deriv.astype(bf16)
    d_lo = (deriv - d_hi.astype(np.float32)).astype(bf16)
    derivs = jnp.asarray(np.concatenate([d_hi, d_lo], axis=1))
    codes_c = jnp.asarray(code_table([{n: 1} for n in range(5)]), bf16)

    far = pl.BlockSpec(memory_space=pl.ANY)
    grp, even, odd, faces, mine, kept = pl.pallas_call(
        trace_kernel,
        out_shape=[
            jax.ShapeDtypeStruct((groups, CAPG, 512), f32),
            pltpu.VMEM((CAPS, 512), f32),
            pltpu.VMEM((CAPS, 512), f32),
            pltpu.VMEM((144, 128), f32),
            pltpu.VMEM((groups, CAPG, 512), f32),
            pltpu.VMEM((8, SLOTS), jnp.int32),
        ],
        in_specs=[far] * 4,
        out_specs=[far] + [VM] * 5,
        scratch_shapes=[
            pltpu.VMEM((6, 8, 512), f32),
            pltpu.SMEM((8,), jnp.int32),
            pltpu.VMEM((4, SLOTS), jnp.int32),
            pltpu.VMEM((4, 64, 64), f32),
            pltpu.VMEM((512, 256), bf16),
            pltpu.VMEM((128, 1024), bf16),
            pltpu.SemaphoreType.DMA((4,)),
            pltpu.SemaphoreType.DMA((4,)),
        ],
        name="traces",
        compiler_params=pltpu.CompilerParams(vmem_limit_bytes=16 << 20),
    )(*(pltpu.with_memory_space_constraint(a, pltpu.HBM) for a in (elements, material, info, mortar_proj)))
    pairs = [[(i + n, i + 1 - n) for i in range(first, n_elem - 1, 2) for n in range(2)] for first in range(2)]
    from_odd = lax.ppermute(odd, "elem", pairs[1])
    arrived = lax.all_to_all(grp, "grp", split_axis=0, concat_axis=0, tiled=True)
    from_even = lax.ppermute(even, "elem", pairs[0])
    held = call(
        local_kernel,
        [
            (6, 8, 512), (144, 128), (SLOTS, 128), (19, 64, 128), (8, 128),
            ((384, 256), bf16), ((384, 512), bf16),
        ],
        {1, 2, 3},
        (
            elements, material, metric, counts, neighbours, faces, derivs, kept, mortar_proj, codes_c,
            mine, even, odd,
        ),
    )
    (new,) = call(
        mortar_kernel, [(6, 8, 512)], set(), (arrived, from_even, from_odd, select, orients, *held), free=(0,)
    )
    return jnp.transpose(new, (1, 0, 2))


def solution(mesh):
    return jax.shard_map(
        section,
        mesh=mesh,
        in_specs=(
            P(("elem", "grp"), None, None),
            P(("elem", "grp")),
            P(("elem", "grp")),
            P(),
            P(("elem", "grp"), None, None),
            P(("elem", "grp"), None),
            P(("elem", "grp"), None),
        ),
        out_specs=P(("elem", "grp"), None, None),
        check_vma=False,
    )
```

```python
import jax
import jax.numpy as jnp
import numpy as np
from jax import lax
from jax.experimental import pallas as pl
from jax.experimental.pallas import tpu as pltpu
from jax.sharding import PartitionSpec as P


CAPG = 8
CAPS = 32
SLOTS = 128
STEP = 0.002
LIFT = 49.0

f32 = jnp.float32
bf16 = jnp.bfloat16


def cheb_matrix():
    points = -np.cos(np.pi * np.arange(8) / 7.0)
    factor = np.array([2.0, 1.0, 1.0, 1.0, 1.0, 1.0, 1.0, 2.0])
    alternating = np.where(np.arange(8) % 2 == 0, 1.0, -1.0)
    scaled = factor * alternating
    differ = points[:, None] - points[None, :] + np.eye(8)
    matrix = scaled[:, None] / scaled[None, :] / differ
    matrix = matrix * (1.0 - np.eye(8))
    return (matrix - np.eye(8) * matrix.sum(axis=1)[:, None]).astype(np.float32)


def face_select():
    grid = np.arange(512).reshape(8, 8, 8)
    planes = [grid[:, 0], grid[:, 7], grid[:, :, 0], grid[:, :, 7]]
    nodes = np.concatenate([p.reshape(64) for p in planes])
    return (np.arange(512)[:, None] == nodes[None, :]).astype(np.float32)


def orient_table():
    first, second = np.meshgrid(np.arange(8), np.arange(8), indexing="ij")
    out = np.zeros((128, 1024), np.float32)
    for orient in range(8):
        p, r = (second, first) if orient & 4 else (first, second)
        p = 7 - p if orient & 1 else p
        r = 7 - r if orient & 2 else r
        source = (8 * p + r).reshape(64)
        for half in range(2):
            out[half * 64 + source, orient * 128 + half * 64 + np.arange(64)] = 1.0
    return out


def deriv_table():
    d = cheb_matrix()
    along_b = np.kron(np.eye(2), np.kron(d, np.eye(8))).T
    along_c = np.kron(np.eye(16), d).T
    return np.concatenate([along_b, along_c], axis=0).astype(np.float32)


def code_table(rows):
    out = np.zeros((16, 128 * len(rows)), np.float32)
    for block, weights in enumerate(rows):
        for row, weight in weights.items():
            out[row, block * 128 : (block + 1) * 128] = weight
    return out


def dot(a, b, ca=1, cb=0):
    return lax.dot_general(a, b, (((ca,), (cb,)), ((), ())), preferred_element_type=f32)


def split2(x):
    hi = x.astype(bf16)
    return hi, (x - hi.astype(f32)).astype(bf16)


def split3(x):
    hi = x.astype(bf16)
    rest = x - hi.astype(f32)
    mid = rest.astype(bf16)
    return hi, mid, (rest - mid.astype(f32)).astype(bf16)


def lane_low(shape):
    return lax.broadcasted_iota(jnp.int32, shape, len(shape) - 1) % 128 < 64


def swap(x):
    return pltpu.roll(x, 64, 1)


def join_pair(low, a, b):
    return jnp.where(low, a, swap(b))


def by_element(ref, shape):
    row = lax.broadcasted_iota(jnp.int32, shape, 0)
    out = jnp.full(shape, ref[0], f32) if ref.dtype == f32 else jnp.full(shape, ref[0].astype(f32), f32)
    for e in range(1, 8):
        out = jnp.where(row == e, ref[e].astype(f32), out)
    return out


def project_blocks(proj_ref):
    zero = jnp.zeros((64, 64), f32)
    blocks = []
    for s in range(4):
        p = proj_ref[s]
        top = jnp.concatenate([p, zero], axis=1)
        bottom = jnp.concatenate([zero, p], axis=1)
        blocks.append(jnp.concatenate([top, bottom], axis=0))
    return blocks


def slot_material(mat_ref, element):
    out = jnp.zeros(element.shape, f32)
    for e in range(8):
        out = jnp.where(element == e, mat_ref[e].astype(f32), out)
    return out


def code_rows(rows):
    pad = [jnp.zeros((1, SLOTS), f32)] * (16 - len(rows))
    return jnp.concatenate(rows + pad, axis=0).astype(bf16)


def selection():
    lane = lax.broadcasted_iota(jnp.int32, (1, 256), 1)
    far = jnp.bitwise_and(lax.shift_right_logical(lane, 6), 1)
    p = jnp.bitwise_and(lax.shift_right_logical(lane, 3), 7)
    r = jnp.bitwise_and(lane, 7)
    node = 64 * p + jnp.where(lane < 128, r + 56 * far, 8 * r + 7 * far)
    row = lax.broadcasted_iota(jnp.int32, (512, 256), 0)
    return jnp.where(row == node, 1.0, 0.0).astype(bf16)


def orientations():
    lane = lax.broadcasted_iota(jnp.int32, (1, 1024), 1)
    half = jnp.bitwise_and(lane, 64)
    p = jnp.bitwise_and(lax.shift_right_logical(lane, 3), 7)
    r = jnp.bitwise_and(lane, 7)
    turn = jnp.bitwise_and(lane, 512) != 0
    p, r = jnp.where(turn, r, p), jnp.where(turn, p, r)
    p = jnp.where(jnp.bitwise_and(lane, 128) != 0, 7 - p, p)
    r = jnp.where(jnp.bitwise_and(lane, 256) != 0, 7 - r, r)
    row = lax.broadcasted_iota(jnp.int32, (128, 1024), 0)
    return jnp.where(row == half + 8 * p + r, 1.0, 0.0).astype(bf16)


def trace_kernel(
    state_hbm, mat_hbm, map_hbm, proj_hbm, grp_hbm, even_ref, odd_ref, face_ref, mine_ref, info_ref,
    state_ref, mat_ref, map_ref, proj_ref, sel_ref, orient_ref, in_sem, out_sem,
):
    def load(src, dst, n):
        copy = pltpu.make_async_copy(src, dst, in_sem.at[n])
        copy.start()
        return copy

    map_load = load(map_hbm, map_ref, 0)
    mat_load = load(mat_hbm, mat_ref, 1)
    state_load = load(state_hbm, state_ref, 2)
    proj_load = load(proj_hbm, proj_ref, 3)
    sel_ref[...] = selection()
    orient_ref[...] = orientations()
    code_row = lax.broadcasted_iota(jnp.int32, (16, 128), 0)
    weights = jnp.where(code_row == 0, 1.0, jnp.where(code_row == 1, 8.0, jnp.where(code_row == 3, 48.0, 0.0)))
    spreads = jnp.concatenate(
        [weights, jnp.where(code_row == 2, 1.0, 0.0), jnp.where(code_row == 4, 1.0, 0.0)], axis=1
    ).astype(bf16)
    map_load.wait()
    mat_load.wait()
    info = jnp.concatenate([map_ref[...]] * 2, axis=0)
    slot = lax.broadcasted_iota(jnp.int32, (8, SLOTS), 1)
    turned = jnp.where(slot < 96, pltpu.roll(info, 96, 1), pltpu.roll(info, 32, 1))
    odd = jnp.bitwise_and(lax.axis_index("elem"), 1) == 1
    info = jnp.where((slot >= 64) & odd, turned, info)
    info_ref[...] = info
    element, face, sub, orient = (info[i : i + 1] for i in range(4))
    material = slot_material(mat_ref, element)
    codes = code_rows([element.astype(f32), face.astype(f32), sub.astype(f32), orient.astype(f32), material])
    spread = dot(codes, spreads, 0, 0)
    index = spread[:, 0:128].astype(jnp.int32)
    sub_of = spread[:, 128:256].astype(jnp.int32)
    lane = lax.broadcasted_iota(jnp.int32, (SLOTS, 128), 1)
    one_hot = jnp.concatenate(
        [jnp.where(index == lane + 128 * t, 1.0, 0.0).astype(bf16) for t in range(3)], axis=1
    )
    heat = 1.4 + 0.27 * spread[:, 256:384]
    state_load.wait()
    low = lane_low((8, 128))
    flat = state_ref[...].reshape(48, 512)
    picked = dot(jnp.concatenate(split3(flat), axis=0), sel_ref[...])
    picked = picked[0:48] + picked[48:96] + picked[96:144]
    pairs = []
    for v in range(6):
        x = state_ref[v]
        pairs.append(
            [
                jnp.where(low, x[:, 0:128], x[:, 384:512]),
                picked[8 * v : 8 * v + 8, 0:128],
                picked[8 * v : 8 * v + 8, 128:256],
            ]
        )
    rows = []
    for j in range(3):
        for d in range(3):
            first, second = pairs[2 * j][d], pairs[2 * j + 1][d]
            rows.append(jnp.where(low, first, swap(second)))
            rows.append(jnp.where(low, swap(first), second))
    faces = jnp.concatenate(rows, axis=0)
    face_ref[...] = faces
    hi, lo = split2(faces)
    table = dot(jnp.concatenate([hi, lo], axis=0), orient_ref[...]).astype(bf16)
    columns = []
    for part in range(6):
        block = table[48 * part : 48 * part + 48]
        columns.append(jnp.concatenate([block[:, 128 * o : 128 * o + 128] for o in range(8)], axis=0))
    gathered = dot(one_hot, jnp.concatenate(columns, axis=1))
    proj_load.wait()
    b_hi, b_lo = split2(jnp.concatenate(project_blocks(proj_ref), axis=0))
    b_twice = jnp.concatenate([b_hi, b_hi], axis=1)

    def project(at):
        q = slice(at, at + 64)
        x_hi = jnp.concatenate([gathered[q, 128 * j : 128 * j + 128] for j in range(3)], axis=0)
        x_lo = jnp.concatenate([gathered[q, 384 + 128 * j : 512 + 128 * j] for j in range(3)], axis=0)
        h = x_hi.astype(bf16)
        wide = dot(jnp.concatenate([h, x_lo.astype(bf16)], axis=1), b_twice, 1, 1) + dot(h, b_lo, 1, 1)
        for j in range(3):
            r = slice(64 * j, 64 * j + 64)
            w = x_hi[r] + x_lo[r]
            for s in range(4):
                w = jnp.where(sub_of[q] == s + 1, wide[r, 128 * s : 128 * s + 128], w)
            yield slice(128 * j, 128 * j + 128), w
        yield slice(384, 512), heat[q]

    stores = []
    for n, (lanes, w) in enumerate(project(0)):
        for g in range(8):
            mine_ref[g, :, lanes] = w[8 * g : 8 * g + 8]
        stores.append(pltpu.make_async_copy(mine_ref.at[:, :, lanes], grp_hbm.at[:, :, lanes], out_sem.at[n]))
        stores[-1].start()
    for lanes, w in project(64):
        even_ref[:, lanes] = w[0:32]
        odd_ref[:, lanes] = w[32:64]
    for store in stores:
        store.wait()


def primitives(u, g, n):
    inv = 1.0 / u[0]
    p = (g - 1.0) * (u[4] - 0.5 * inv * (u[1] * u[1] + u[2] * u[2] + u[3] * u[3]))
    s = (n[0] * u[1] + n[1] * u[2] + n[2] * u[3]) * inv
    return p, s, jnp.sqrt(g * p * inv)


def flux_of(u, p, s, n):
    return [u[0] * s, u[1] * s + p * n[0], u[2] * s + p * n[1], u[3] * s + p * n[2], (u[4] + p) * s, u[5] * s]


def hllc(u_l, u_r, prim_l, prim_r, n):
    (p_l, s_l, c_l), (p_r, s_r, c_r) = prim_l, prim_r
    left = jnp.minimum(s_l - c_l, s_r - c_r)
    right = jnp.maximum(s_l + c_l, s_r + c_r)
    mass_l = u_l[0] * (left - s_l)
    mass_r = u_r[0] * (right - s_r)
    middle = (p_r - p_l + mass_l * s_l - mass_r * s_r) / (mass_l - mass_r)
    take = (left >= 0.0) | (middle >= 0.0)
    u = [jnp.where(take, x, y) for x, y in zip(u_l, u_r)]
    p = jnp.where(take, p_l, p_r)
    s = jnp.where(take, s_l, s_r)
    mass = jnp.where(take, mass_l, mass_r)
    wave = jnp.where(take, left, right)
    use_star = jnp.where(take, -left, right) > 0.0
    a = jnp.where(use_star, wave * (middle - s) / (wave - middle), 0.0)
    speed = s + a
    push = a * mass
    lift = p + push
    return [
        u[0] * speed,
        u[1] * speed + lift * n[0],
        u[2] * speed + lift * n[1],
        u[3] * speed + lift * n[2],
        (u[4] + p) * speed + push * middle,
        u[5] * speed,
    ]


def two_halves(low, first, second):
    return jnp.where(low, first, swap(second)), jnp.where(low, swap(first), second)


def local_kernel(
    state_ref, mat_ref, metric_ref, count_ref, near_ref, face_ref, deriv_ref, info_ref, proj_ref, code_ref,
    mine_ref, even_ref, odd_ref, base_ref, local_ref, sub_ref, own_ref, scale_ref, hot_ref, back_ref,
):
    info = info_ref[...]
    element, face, sub, orient = (info[i : i + 1] for i in range(4))
    slot = lax.broadcasted_iota(jnp.int32, (1, SLOTS), 1)
    odd = jnp.bitwise_and(lax.axis_index("elem"), 1)
    side = jnp.bitwise_xor(jnp.bitwise_and(lax.shift_right_logical(slot, 5), 1), odd)
    group = jnp.where(slot < 64, lax.shift_right_logical(slot, 3), 8 + side)
    position = jnp.where(slot < 64, jnp.bitwise_and(slot, 7), jnp.bitwise_and(slot, 31))
    limit = jnp.zeros((1, SLOTS), jnp.int32)
    for n in range(10):
        limit = jnp.where(group == n, count_ref[n], limit)
    alive = jnp.where(position < limit, 1.0, 0.0)
    sign = jnp.where(jnp.bitwise_and(face, 1) == 1, 1.0, -1.0)
    axis = lax.shift_right_logical(face, 1)
    codes = code_rows(
        [sub.astype(f32), alive] + [jnp.where(axis == d, sign, 0.0) for d in range(3)]
    )
    spread = dot(codes, code_ref[...], 0, 0)
    sub_ref[...] = spread[:, 0:128]
    index = 48 * orient + 8 * face + element
    row = lax.broadcasted_iota(jnp.int32, (384, SLOTS), 0)
    beta = jnp.where(sub == 0, 1.0, 0.25)
    hot = jnp.where(row == index, beta, 0.0).astype(bf16)
    hot_ref[:, 0:128] = hot
    hot_ref[:, 128:256] = hot
    b_hi, b_lo = split2(jnp.concatenate(project_blocks(proj_ref), axis=1))
    back_ref[0:128, :] = b_hi
    back_ref[128:256, :] = b_hi
    back_ref[256:384, :] = b_lo
    heat = 1.4 + 0.27 * by_element(mat_ref, (8, 512))
    u = [state_ref[v] for v in range(6)]
    inv = 1.0 / u[0]
    vel = [u[1] * inv, u[2] * inv, u[3] * inv]
    p = (heat - 1.0) * (u[4] - 0.5 * (u[1] * vel[0] + u[2] * vel[1] + u[3] * vel[2]))
    fluxes = []
    for d in range(3):
        s = vel[d]
        f = [u[0] * s, u[1] * s, u[2] * s, u[3] * s, (u[4] + p) * s, u[5] * s]
        f[1 + d] = f[1 + d] + p
        fluxes.append(f)
    rows = []
    for v in range(6):
        for t in range(4):
            r = slice(128 * t, 128 * t + 128)
            rows.append(jnp.concatenate([fluxes[1][v][:, r], fluxes[2][v][:, r]], axis=1))
    hi, lo = split2(jnp.concatenate(rows, axis=0))
    d_hi, d_lo = deriv_ref[:, 0:128], deriv_ref[:, 128:256]
    main = dot(jnp.concatenate([hi, lo], axis=0), d_hi)
    bc = main[0:192] + main[192:384] + dot(hi, d_lo)
    low = lane_low((8, 128))
    deriv = cheb_matrix()
    scale = STEP * by_element(metric_ref, (8, 128))
    for v in range(6):
        x = [fluxes[0][v][:, 128 * t : 128 * t + 128] for t in range(4)]
        xs = [swap(a) for a in x]
        for t in range(4):
            acc = bc[32 * v + 8 * t : 32 * v + 8 * t + 8]
            for k in range(4):
                same = jnp.where(low, float(deriv[2 * t, 2 * k]), float(deriv[2 * t + 1, 2 * k + 1]))
                cross = jnp.where(low, float(deriv[2 * t, 2 * k + 1]), float(deriv[2 * t + 1, 2 * k]))
                acc = acc + same * x[k] + cross * xs[k]
            r = slice(128 * t, 128 * t + 128)
            base_ref[v, :, r] = u[v][:, r] - scale * acc
    faces = face_ref[...]
    lane = lax.broadcasted_iota(jnp.int32, (8, 256), 1)
    hot, live = [], []
    for k in range(6):
        near = jnp.broadcast_to(near_ref[:, k : k + 1], (8, 256))
        live.append((near >= 0)[:, 0:128])
        target = 8 * (k ^ 1) + near
        hit = (jnp.bitwise_and(lane, 63) == target) & (near >= 0) & (lane < 192)
        hot.append(jnp.where(hit, 1.0, 0.0))
    hot = jnp.concatenate(hot, axis=0).astype(bf16)
    heat_rows = jnp.concatenate([heat[:, 0:128]] * 6, axis=0)
    table = jnp.concatenate([faces[0:48], faces[48:96], faces[96:144], heat_rows], axis=1)
    gap = jnp.zeros((16, 512), bf16)
    terms = []
    for term in split3(table):
        terms += [term, gap]
    terms.append(jnp.zeros((64, 512), bf16))
    theirs = dot(hot, jnp.concatenate(terms, axis=0))
    low = lane_low((48, 128))
    row = lax.broadcasted_iota(jnp.int32, (48, 128), 0)
    sign = jnp.where(jnp.bitwise_and(row, 8) != 0, 1.0, -1.0)
    normal = [jnp.where(lax.shift_right_logical(row, 4) == d, sign, 0.0) for d in range(3)]
    mine, other = [], []
    for j in range(3):
        x, y = faces[48 * j : 48 * j + 48], theirs[:, 128 * j : 128 * j + 128]
        mine += [x, swap(x)]
        other += [y, swap(y)]
    prim = primitives(mine, heat_rows, normal)
    flux = flux_of(mine, prim[0], prim[1], normal)
    through = hllc(mine, other, prim, primitives(other, theirs[:, 384:512], normal), normal)
    corr = [f - h for f, h in zip(flux, through)]
    for j in range(3):
        packed = join_pair(low, corr[2 * j], corr[2 * j + 1])
        for k in range(6):
            local_ref[48 * j + 8 * k : 48 * j + 8 * k + 8, :] = jnp.where(
                live[k], packed[8 * k : 8 * k + 8], 0.0
            )
    low = lane_low((64, 128))

    def rows(at):
        lanes = slice(at, at + 128)
        return (
            jnp.concatenate([mine_ref[g, :, lanes] for g in range(8)], axis=0),
            jnp.concatenate([even_ref[:, lanes], odd_ref[:, lanes]], axis=0),
        )

    states = []
    for j in range(3):
        states += two_halves(low, *rows(128 * j))
    g = jnp.where(low, *rows(384))
    slots = [
        jnp.where(low, spread[0:64, 128 * n : 128 * n + 128], spread[64:128, 128 * n : 128 * n + 128])
        for n in range(1, 5)
    ]
    prim = primitives(states, g, slots[1:])
    kept = [*states, *prim, *flux_of(states, prim[0], prim[1], slots[1:]), *slots]
    for n, x in enumerate(kept):
        own_ref[n] = x
    scale_ref[...] = (STEP * LIFT) * by_element(metric_ref, (8, 128))


def mortar_kernel(
    from_grp_ref, from_even_ref, from_late_ref, from_odd_ref, sel_ref, orient_ref,
    base_ref, local_ref, sub_ref, own_ref, scale_ref, hot_ref, back_ref, out_hbm, new_ref, sem,
):
    chunk = 16
    low = lane_low((chunk, 128))
    first, second = [[], [], []], [[], [], []]
    for at in range(0, 64, chunk):
        r = slice(at, at + chunk)

        def rows(lane):
            lanes = slice(lane, lane + 128)
            grp = jnp.concatenate([from_grp_ref[at // 8 + n, :, lanes] for n in range(chunk // 8)], axis=0)
            if at < 32:
                return grp, from_even_ref[r, lanes] + from_late_ref[r, lanes]
            return grp, from_odd_ref[at - 32 : at - 32 + chunk, lanes]

        theirs = []
        for j in range(3):
            theirs += two_halves(low, *rows(128 * j))
        g = jnp.where(low, *rows(384))
        mine = [own_ref[n, r] for n in range(6)]
        normal = [own_ref[n, r] for n in range(16, 19)]
        live = own_ref[15, r] > 0.5
        prim = tuple(own_ref[n, r] for n in range(6, 9))
        through = hllc(mine, theirs, prim, primitives(theirs, g, normal), normal)
        corr = [jnp.where(live, own_ref[9 + n, r] - through[n], 0.0) for n in range(6)]
        for j in range(3):
            x, y = two_halves(low, corr[2 * j], corr[2 * j + 1])
            first[j].append(x)
            second[j].append(y)
    corr = jnp.concatenate([x for j in range(3) for x in first[j] + second[j]], axis=0)
    hi, lo = split2(corr)
    wide = dot(jnp.concatenate([hi, lo, hi], axis=1), back_ref[...])
    sub_of = sub_ref[...].astype(jnp.int32)
    back = []
    for j in range(3):
        r = slice(128 * j, 128 * j + 128)
        y = corr[r]
        for s in range(4):
            y = jnp.where(sub_of == s + 1, wide[r, 128 * s : 128 * s + 128], y)
        back.append(y)
    hi, lo = split2(jnp.concatenate(back, axis=1))
    summed = dot(hot_ref[...], jnp.concatenate([hi, lo], axis=0))
    rows = []
    for j in range(3):
        lanes = slice(128 * j, 128 * j + 128)
        rows.append(jnp.concatenate([summed[48 * o : 48 * o + 48, lanes] for o in range(8)], axis=1))
    hi, lo = split2(jnp.concatenate(rows, axis=0))
    turned = dot(jnp.concatenate([hi, lo], axis=0), orient_ref[...], 1, 1)
    total = turned[0:144] + turned[144:288] + local_ref[...]
    low = lane_low((8, 128))
    lift = []
    for v in range(6):
        at = 48 * (v // 2)
        parts = []
        for d in range(3):
            first = total[at + 16 * d : at + 16 * d + 8]
            second = total[at + 16 * d + 8 : at + 16 * d + 16]
            if v % 2 == 0:
                parts.append(jnp.where(low, first, swap(second)))
            else:
                parts.append(jnp.where(low, swap(first), second))
        lift.append(parts)
    side = jnp.concatenate(
        [jnp.concatenate([lift[v][1] for v in range(6)], axis=0), jnp.concatenate([lift[v][2] for v in range(6)], axis=0)],
        axis=1,
    )
    hi, lo = split2(side)
    placed = dot(jnp.concatenate([hi, lo], axis=0), sel_ref[...], 1, 1)
    placed = placed[0:48] + placed[48:96]
    scale = scale_ref[...]
    stores = []
    for v in range(6):
        for t in range(4):
            lanes = slice(128 * t, 128 * t + 128)
            value = placed[8 * v : 8 * v + 8, lanes]
            if t == 0:
                value = value + jnp.where(low, lift[v][0], 0.0)
            if t == 3:
                value = value + jnp.where(low, 0.0, lift[v][0])
            new_ref[v, :, lanes] = base_ref[v, :, lanes] + scale * value
        if v % 2 == 1:
            pair = pl.ds(v - 1, 2)
            stores.append(pltpu.make_async_copy(new_ref.at[pair], out_hbm.at[pair], sem.at[v // 2]))
            stores[-1].start()
    for store in stores:
        store.wait()


SM = pl.BlockSpec(memory_space=pltpu.SMEM)
VM = pl.BlockSpec(memory_space=pltpu.VMEM)


def call(kernel, outs, scalars, args, free=()):
    outs = [s if isinstance(s[0], tuple) else (s, f32) for s in outs]
    held = [
        a if n in scalars else pltpu.with_memory_space_constraint(a, pltpu.VMEM)
        for n, a in enumerate(args)
    ]
    return pl.pallas_call(
        kernel,
        out_shape=[jax.ShapeDtypeStruct(*s) if n in free else pltpu.VMEM(*s) for n, s in enumerate(outs)],
        in_specs=[SM if n in scalars else VM for n in range(len(args))],
        out_specs=[VM] * len(outs),
        compiler_params=pltpu.CompilerParams(vmem_limit_bytes=16 << 20),
    )(*held)


def section(state, material, metric, mortar_proj, mortar_map, mortar_count, neighbours):
    groups = lax.axis_size("grp")
    n_elem = lax.axis_size("elem")
    elements = jnp.transpose(state, (1, 0, 2))
    info = mortar_map[0]
    counts = mortar_count[0]
    select = jnp.asarray(face_select(), bf16)
    orients = jnp.asarray(orient_table(), bf16)
    deriv = deriv_table()
    d_hi = deriv.astype(bf16)
    d_lo = (deriv - d_hi.astype(np.float32)).astype(bf16)
    derivs = jnp.asarray(np.concatenate([d_hi, d_lo], axis=1))
    codes_c = jnp.asarray(code_table([{n: 1} for n in range(5)]), bf16)

    far = pl.BlockSpec(memory_space=pl.ANY)
    grp, even, odd, faces, mine, kept = pl.pallas_call(
        trace_kernel,
        out_shape=[
            jax.ShapeDtypeStruct((groups, CAPG, 512), f32),
            pltpu.VMEM((CAPS, 512), f32),
            pltpu.VMEM((CAPS, 512), f32),
            pltpu.VMEM((144, 128), f32),
            pltpu.VMEM((groups, CAPG, 512), f32),
            pltpu.VMEM((8, SLOTS), jnp.int32),
        ],
        in_specs=[far] * 4,
        out_specs=[far] + [VM] * 5,
        scratch_shapes=[
            pltpu.VMEM((6, 8, 512), f32),
            pltpu.SMEM((8,), jnp.int32),
            pltpu.VMEM((4, SLOTS), jnp.int32),
            pltpu.VMEM((4, 64, 64), f32),
            pltpu.VMEM((512, 256), bf16),
            pltpu.VMEM((128, 1024), bf16),
            pltpu.SemaphoreType.DMA((4,)),
            pltpu.SemaphoreType.DMA((4,)),
        ],
        name="traces",
        compiler_params=pltpu.CompilerParams(vmem_limit_bytes=16 << 20),
    )(*(pltpu.with_memory_space_constraint(a, pltpu.HBM) for a in (elements, material, info, mortar_proj)))
    swaps = [
        [((i + n) * groups + g, (i + 1 - n) * groups + g) for i in range(first, n_elem - 1, 2) for g in range(groups) for n in range(2)]
        for first in range(2)
    ]
    late = [(0, groups), (groups, 0)]
    axes = ("elem", "grp")
    from_even = lax.ppermute(even, axes, [pair for pair in swaps[0] if pair not in late])
    arrived = lax.all_to_all(grp, "grp", split_axis=0, concat_axis=0, tiled=True)
    from_odd = lax.ppermute(odd, axes, swaps[1])
    from_late = lax.ppermute(even, axes, late)
    held = call(
        local_kernel,
        [
            (6, 8, 512), (144, 128), (SLOTS, 128), (19, 64, 128), (8, 128),
            ((384, 256), bf16), ((384, 512), bf16),
        ],
        {1, 2, 3},
        (
            elements, material, metric, counts, neighbours, faces, derivs, kept, mortar_proj, codes_c,
            mine, even, odd,
        ),
    )
    operands = (arrived, from_even, from_late, from_odd, select, orients, *held)
    new = pl.pallas_call(
        mortar_kernel,
        out_shape=jax.ShapeDtypeStruct((6, 8, 512), f32),
        in_specs=[VM] * len(operands),
        out_specs=far,
        scratch_shapes=[pltpu.VMEM((6, 8, 512), f32), pltpu.SemaphoreType.DMA((3,))],
        name="mortar",
        compiler_params=pltpu.CompilerParams(vmem_limit_bytes=16 << 20),
    )(*(pltpu.with_memory_space_constraint(a, pltpu.VMEM) for a in operands))
    return jnp.transpose(new, (1, 0, 2))


def solution(mesh):
    return jax.shard_map(
        section,
        mesh=mesh,
        in_specs=(
            P(("elem", "grp"), None, None),
            P(("elem", "grp")),
            P(("elem", "grp")),
            P(),
            P(("elem", "grp"), None, None),
            P(("elem", "grp"), None),
            P(("elem", "grp"), None),
        ),
        out_specs=P(("elem", "grp"), None, None),
        check_vma=False,
    )
```

```python
import jax
import jax.numpy as jnp
import numpy as np
from jax import lax
from jax.experimental import pallas as pl
from jax.experimental.pallas import tpu as pltpu
from jax.sharding import PartitionSpec as P


CAPG = 8
CAPS = 32
SLOTS = 128
ROWS = 25
STEP = 0.002
LIFT = 49.0

f32 = jnp.float32
bf16 = jnp.bfloat16


def cheb_matrix():
    points = -np.cos(np.pi * np.arange(8) / 7.0)
    factor = np.array([2.0, 1.0, 1.0, 1.0, 1.0, 1.0, 1.0, 2.0])
    alternating = np.where(np.arange(8) % 2 == 0, 1.0, -1.0)
    scaled = factor * alternating
    differ = points[:, None] - points[None, :] + np.eye(8)
    matrix = scaled[:, None] / scaled[None, :] / differ
    matrix = matrix * (1.0 - np.eye(8))
    return (matrix - np.eye(8) * matrix.sum(axis=1)[:, None]).astype(np.float32)


def face_select():
    grid = np.arange(512).reshape(8, 8, 8)
    planes = [grid[:, 0], grid[:, 7], grid[:, :, 0], grid[:, :, 7]]
    nodes = np.concatenate([p.reshape(64) for p in planes])
    return (np.arange(512)[:, None] == nodes[None, :]).astype(np.float32)


def deriv_table():
    d = cheb_matrix()
    along_b = np.kron(np.eye(2), np.kron(d, np.eye(8))).T
    along_c = np.kron(np.eye(16), d).T
    return np.concatenate([along_b, along_c], axis=0).astype(np.float32)


def code_table(rows):
    out = np.zeros((16, 128 * len(rows)), np.float32)
    for block, weights in enumerate(rows):
        for row, weight in weights.items():
            out[row, block * 128 : (block + 1) * 128] = weight
    return out


def dot(a, b, ca=1, cb=0):
    return lax.dot_general(a, b, (((ca,), (cb,)), ((), ())), preferred_element_type=f32)


def split2(x):
    hi = x.astype(bf16)
    return hi, (x - hi.astype(f32)).astype(bf16)


def split3(x):
    hi = x.astype(bf16)
    rest = x - hi.astype(f32)
    mid = rest.astype(bf16)
    return hi, mid, (rest - mid.astype(f32)).astype(bf16)


def lane_low(shape):
    return lax.broadcasted_iota(jnp.int32, shape, len(shape) - 1) % 128 < 64


def swap(x):
    return pltpu.roll(x, 64, 1)


def join_pair(low, a, b):
    return jnp.where(low, a, swap(b))


def by_element(ref, shape):
    row = lax.broadcasted_iota(jnp.int32, shape, 0)
    out = jnp.full(shape, ref[0], f32) if ref.dtype == f32 else jnp.full(shape, ref[0].astype(f32), f32)
    for e in range(1, 8):
        out = jnp.where(row == e, ref[e].astype(f32), out)
    return out


def project_blocks(proj_ref):
    zero = jnp.zeros((64, 64), f32)
    blocks = []
    for s in range(4):
        p = proj_ref[s]
        top = jnp.concatenate([p, zero], axis=1)
        bottom = jnp.concatenate([zero, p], axis=1)
        blocks.append(jnp.concatenate([top, bottom], axis=0))
    return blocks


def slot_material(mat_ref, element):
    out = jnp.zeros(element.shape, f32)
    for e in range(8):
        out = jnp.where(element == e, mat_ref[e].astype(f32), out)
    return out


def code_rows(rows):
    pad = [jnp.zeros((1, SLOTS), f32)] * (16 - len(rows))
    return jnp.concatenate(rows + pad, axis=0).astype(bf16)


def selection():
    lane = lax.broadcasted_iota(jnp.int32, (1, 256), 1)
    far = jnp.bitwise_and(lax.shift_right_logical(lane, 6), 1)
    p = jnp.bitwise_and(lax.shift_right_logical(lane, 3), 7)
    r = jnp.bitwise_and(lane, 7)
    node = 64 * p + jnp.where(lane < 128, r + 56 * far, 8 * r + 7 * far)
    row = lax.broadcasted_iota(jnp.int32, (512, 256), 0)
    return jnp.where(row == node, 1.0, 0.0).astype(bf16)


def lane_sources(orient, back):
    lane = lax.broadcasted_iota(jnp.int32, orient.shape, 1)
    p = jnp.bitwise_and(lax.shift_right_logical(lane, 3), 7)
    r = jnp.bitwise_and(lane, 7)
    turn = jnp.bitwise_and(orient, 4) != 0
    flip_p = jnp.bitwise_and(orient, 1) != 0
    flip_r = jnp.bitwise_and(orient, 2) != 0
    if not back:
        p, r = jnp.where(turn, r, p), jnp.where(turn, p, r)
    p = jnp.where(flip_p, 7 - p, p)
    r = jnp.where(flip_r, 7 - r, r)
    if back:
        p, r = jnp.where(turn, r, p), jnp.where(turn, p, r)
    return jnp.bitwise_and(lane, 64) + 8 * p + r


def reorder(x, source):
    return jnp.take_along_axis(x, source, axis=1, mode="promise_in_bounds")


def stacked(table):
    gap = jnp.zeros((16, table.shape[1]), bf16)
    terms = []
    for term in split3(table):
        terms += [term, gap]
    return jnp.concatenate(terms + [jnp.zeros((64, table.shape[1]), bf16)], axis=0)


def trace_kernel(
    state_hbm, mat_hbm, map_hbm, proj_hbm, grp_hbm, even_ref, odd_ref, face_ref, mine_ref, info_ref,
    state_ref, mat_ref, map_ref, proj_ref, sel_ref, pack_ref, in_sem, out_sem,
):
    def load(src, dst, n):
        copy = pltpu.make_async_copy(src, dst, in_sem.at[n])
        copy.start()
        return copy

    map_load = load(map_hbm, map_ref, 0)
    mat_load = load(mat_hbm, mat_ref, 1)
    state_load = load(state_hbm, state_ref, 2)
    proj_load = load(proj_hbm, proj_ref, 3)
    sel_ref[...] = selection()
    code_row = lax.broadcasted_iota(jnp.int32, (16, 128), 0)
    weights = jnp.where(code_row == 0, 1.0, jnp.where(code_row == 1, 8.0, 0.0))
    spreads = jnp.concatenate([weights] + [jnp.where(code_row == n, 1.0, 0.0) for n in range(2, 5)], axis=1)
    place = lax.broadcasted_iota(jnp.int32, (SLOTS, 128), 0)
    lane = lax.broadcasted_iota(jnp.int32, (SLOTS, 128), 1)
    fan = jnp.where(jnp.bitwise_and(place, 7) == lax.shift_right_logical(lane, 4), 1.0, 0.0).astype(bf16)
    map_load.wait()
    mat_load.wait()
    info = jnp.concatenate([map_ref[...]] * 2, axis=0)
    slot = lax.broadcasted_iota(jnp.int32, (8, SLOTS), 1)
    turned = jnp.where(slot < 96, pltpu.roll(info, 96, 1), pltpu.roll(info, 32, 1))
    odd = jnp.bitwise_and(lax.axis_index("elem"), 1) == 1
    info = jnp.where((slot >= 64) & odd, turned, info)
    info_ref[...] = info
    element, face, sub, orient = (info[i : i + 1] for i in range(4))
    material = slot_material(mat_ref, element)
    codes = code_rows([element.astype(f32), face.astype(f32), sub.astype(f32), orient.astype(f32), material])
    spread = dot(codes, spreads.astype(bf16), 0, 0)
    index = spread[:, 0:128].astype(jnp.int32)
    sub_of = spread[:, 128:256].astype(jnp.int32)
    source = lane_sources(spread[:, 256:384].astype(jnp.int32), False)
    hit = jnp.bitwise_and(lane, 63) == index
    one_hot = jnp.concatenate(
        [jnp.where(hit, 1.0, 0.0), jnp.where(hit & (lane < 64), 1.0, 0.0)], axis=1
    ).astype(bf16)
    heat = 1.4 + 0.27 * spread[:, 384:512]
    peer = lax.broadcasted_iota(jnp.int32, (8, 128), 0)
    by_peer = jnp.where(lax.shift_right_logical(slot, 3) == peer, material, 0.0)
    heat_rows = dot(by_peer.astype(bf16), fan)
    state_load.wait()
    low = lane_low((8, 128))
    flat = state_ref[...].reshape(48, 512)
    picked = dot(jnp.concatenate(split3(flat), axis=0), sel_ref[...])
    picked = picked[0:48] + picked[48:96] + picked[96:144]
    pairs = []
    for v in range(6):
        x = state_ref[v]
        pairs.append(
            [
                jnp.where(low, x[:, 0:128], x[:, 384:512]),
                picked[8 * v : 8 * v + 8, 0:128],
                picked[8 * v : 8 * v + 8, 128:256],
            ]
        )
    rows = []
    for j in range(3):
        for d in range(3):
            first, second = pairs[2 * j][d], pairs[2 * j + 1][d]
            rows.append(jnp.where(low, first, swap(second)))
            rows.append(jnp.where(low, swap(first), second))
    faces = jnp.concatenate(rows, axis=0)
    face_ref[...] = faces
    gathered = dot(one_hot, stacked(jnp.concatenate([faces[48 * j : 48 * j + 48] for j in range(3)], axis=1)))
    x = [reorder(gathered[:, 128 * j : 128 * j + 128], source) for j in range(3)]
    x = jnp.concatenate([x[j][at : at + 64] for at in (0, 64) for j in range(3)], axis=0)
    proj_load.wait()
    b_hi, b_lo = split2(jnp.concatenate(project_blocks(proj_ref), axis=0))
    hi, lo = split2(x)
    wide = dot(jnp.concatenate([hi, lo], axis=1), jnp.concatenate([b_hi, b_hi], axis=1), 1, 1) + dot(hi, b_lo, 1, 1)

    def projected(j, at):
        r = slice(64 * j + 3 * at, 64 * j + 3 * at + 64)
        w = x[r]
        for n in range(4):
            w = jnp.where(sub_of[at : at + 64] == n + 1, wide[r, 128 * n : 128 * n + 128], w)
        return w

    for j in range(3):
        w = projected(j, 0)
        for g in range(8):
            part = w[8 * g : 8 * g + 8]
            mine_ref[g, :, 128 * j : 128 * j + 128] = part
            pack_ref[ROWS * g + 8 * j : ROWS * g + 8 * j + 8, :] = part
    for g in range(8):
        pack_ref[ROWS * g + 24 : ROWS * g + 25, :] = heat_rows[g : g + 1]
    store = pltpu.make_async_copy(pack_ref, grp_hbm, out_sem.at[0])
    store.start()
    for j in range(3):
        w = projected(j, 64)
        even_ref[:, 128 * j : 128 * j + 128] = w[0:32]
        odd_ref[:, 128 * j : 128 * j + 128] = w[32:64]
    even_ref[:, 384:512] = heat[64:96]
    odd_ref[:, 384:512] = heat[96:128]
    store.wait()


def primitives(u, g, n):
    inv = 1.0 / u[0]
    p = (g - 1.0) * (u[4] - 0.5 * inv * (u[1] * u[1] + u[2] * u[2] + u[3] * u[3]))
    s = (n[0] * u[1] + n[1] * u[2] + n[2] * u[3]) * inv
    return p, s, jnp.sqrt(g * p * inv)


def flux_of(u, p, s, n):
    return [u[0] * s, u[1] * s + p * n[0], u[2] * s + p * n[1], u[3] * s + p * n[2], (u[4] + p) * s, u[5] * s]


def hllc(u_l, u_r, prim_l, prim_r, n):
    (p_l, s_l, c_l), (p_r, s_r, c_r) = prim_l, prim_r
    left = jnp.minimum(s_l - c_l, s_r - c_r)
    right = jnp.maximum(s_l + c_l, s_r + c_r)
    mass_l = u_l[0] * (left - s_l)
    mass_r = u_r[0] * (right - s_r)
    middle = (p_r - p_l + mass_l * s_l - mass_r * s_r) / (mass_l - mass_r)
    take = (left >= 0.0) | (middle >= 0.0)
    u = [jnp.where(take, x, y) for x, y in zip(u_l, u_r)]
    p = jnp.where(take, p_l, p_r)
    s = jnp.where(take, s_l, s_r)
    mass = jnp.where(take, mass_l, mass_r)
    wave = jnp.where(take, left, right)
    use_star = jnp.where(take, -left, right) > 0.0
    a = jnp.where(use_star, wave * (middle - s) / (wave - middle), 0.0)
    speed = s + a
    push = a * mass
    lift = p + push
    return [
        u[0] * speed,
        u[1] * speed + lift * n[0],
        u[2] * speed + lift * n[1],
        u[3] * speed + lift * n[2],
        (u[4] + p) * speed + push * middle,
        u[5] * speed,
    ]


def two_halves(low, first, second):
    return jnp.where(low, first, swap(second)), jnp.where(low, swap(first), second)


def local_kernel(
    state_ref, mat_ref, metric_ref, count_ref, near_ref, face_ref, deriv_ref, info_ref, proj_ref, code_ref,
    mine_ref, even_ref, odd_ref, base_ref, local_ref, sub_ref, own_ref, scale_ref, hot_ref, back_ref, turn_ref,
):
    info = info_ref[...]
    element, face, sub, orient = (info[i : i + 1] for i in range(4))
    slot = lax.broadcasted_iota(jnp.int32, (1, SLOTS), 1)
    odd = jnp.bitwise_and(lax.axis_index("elem"), 1)
    side = jnp.bitwise_xor(jnp.bitwise_and(lax.shift_right_logical(slot, 5), 1), odd)
    group = jnp.where(slot < 64, lax.shift_right_logical(slot, 3), 8 + side)
    position = jnp.where(slot < 64, jnp.bitwise_and(slot, 7), jnp.bitwise_and(slot, 31))
    limit = jnp.zeros((1, SLOTS), jnp.int32)
    for n in range(10):
        limit = jnp.where(group == n, count_ref[n], limit)
    alive = jnp.where(position < limit, 1.0, 0.0)
    sign = jnp.where(jnp.bitwise_and(face, 1) == 1, 1.0, -1.0)
    axis = lax.shift_right_logical(face, 1)
    codes = code_rows(
        [sub.astype(f32), alive]
        + [jnp.where(axis == d, sign, 0.0) for d in range(3)]
        + [orient.astype(f32), slot_material(mat_ref, element)]
    )
    spread = dot(codes, code_ref[...], 0, 0)
    sub_ref[...] = spread[:, 0:128]
    turn_ref[...] = lane_sources(spread[:, 640:768].astype(jnp.int32), True)
    row = lax.broadcasted_iota(jnp.int32, (48, SLOTS), 0)
    beta = jnp.where(sub == 0, 1.0, 0.25)
    hot = jnp.where(row == 8 * face + element, beta, 0.0).astype(bf16)
    hot_ref[:, 0:128] = hot
    hot_ref[:, 128:256] = hot
    b_hi, b_lo = split2(jnp.concatenate(project_blocks(proj_ref), axis=1))
    back_ref[0:128, :] = b_hi
    back_ref[128:256, :] = b_hi
    back_ref[256:384, :] = b_lo
    heat = 1.4 + 0.27 * by_element(mat_ref, (8, 512))
    u = [state_ref[v] for v in range(6)]
    inv = 1.0 / u[0]
    vel = [u[1] * inv, u[2] * inv, u[3] * inv]
    p = (heat - 1.0) * (u[4] - 0.5 * (u[1] * vel[0] + u[2] * vel[1] + u[3] * vel[2]))
    fluxes = []
    for d in range(3):
        s = vel[d]
        f = [u[0] * s, u[1] * s, u[2] * s, u[3] * s, (u[4] + p) * s, u[5] * s]
        f[1 + d] = f[1 + d] + p
        fluxes.append(f)
    rows = []
    for v in range(6):
        for t in range(4):
            r = slice(128 * t, 128 * t + 128)
            rows.append(jnp.concatenate([fluxes[1][v][:, r], fluxes[2][v][:, r]], axis=1))
    hi, lo = split2(jnp.concatenate(rows, axis=0))
    d_hi, d_lo = deriv_ref[:, 0:128], deriv_ref[:, 128:256]
    main = dot(jnp.concatenate([hi, lo], axis=0), d_hi)
    bc = main[0:192] + main[192:384] + dot(hi, d_lo)
    low = lane_low((8, 128))
    deriv = cheb_matrix()
    scale = STEP * by_element(metric_ref, (8, 128))
    for v in range(6):
        x = [fluxes[0][v][:, 128 * t : 128 * t + 128] for t in range(4)]
        xs = [swap(a) for a in x]
        for t in range(4):
            acc = bc[32 * v + 8 * t : 32 * v + 8 * t + 8]
            for k in range(4):
                same = jnp.where(low, float(deriv[2 * t, 2 * k]), float(deriv[2 * t + 1, 2 * k + 1]))
                cross = jnp.where(low, float(deriv[2 * t, 2 * k + 1]), float(deriv[2 * t + 1, 2 * k]))
                acc = acc + same * x[k] + cross * xs[k]
            r = slice(128 * t, 128 * t + 128)
            base_ref[v, :, r] = u[v][:, r] - scale * acc
    faces = face_ref[...]
    lane = lax.broadcasted_iota(jnp.int32, (8, 256), 1)
    hot, live = [], []
    for k in range(6):
        near = jnp.broadcast_to(near_ref[:, k : k + 1], (8, 256))
        live.append((near >= 0)[:, 0:128])
        target = 8 * (k ^ 1) + near
        hit = (jnp.bitwise_and(lane, 63) == target) & (near >= 0) & (lane < 192)
        hot.append(jnp.where(hit, 1.0, 0.0))
    hot = jnp.concatenate(hot, axis=0).astype(bf16)
    heat_rows = jnp.concatenate([heat[:, 0:128]] * 6, axis=0)
    table = jnp.concatenate([faces[0:48], faces[48:96], faces[96:144], heat_rows], axis=1)
    theirs = dot(hot, stacked(table))
    low = lane_low((48, 128))
    row = lax.broadcasted_iota(jnp.int32, (48, 128), 0)
    sign = jnp.where(jnp.bitwise_and(row, 8) != 0, 1.0, -1.0)
    normal = [jnp.where(lax.shift_right_logical(row, 4) == d, sign, 0.0) for d in range(3)]
    mine, other = [], []
    for j in range(3):
        x, y = faces[48 * j : 48 * j + 48], theirs[:, 128 * j : 128 * j + 128]
        mine += [x, swap(x)]
        other += [y, swap(y)]
    prim = primitives(mine, heat_rows, normal)
    flux = flux_of(mine, prim[0], prim[1], normal)
    through = hllc(mine, other, prim, primitives(other, theirs[:, 384:512], normal), normal)
    corr = [f - h for f, h in zip(flux, through)]
    for j in range(3):
        packed = join_pair(low, corr[2 * j], corr[2 * j + 1])
        for k in range(6):
            local_ref[48 * j + 8 * k : 48 * j + 8 * k + 8, :] = jnp.where(
                live[k], packed[8 * k : 8 * k + 8], 0.0
            )
    low = lane_low((64, 128))

    def rows(at):
        lanes = slice(at, at + 128)
        return (
            jnp.concatenate([mine_ref[g, :, lanes] for g in range(8)], axis=0),
            jnp.concatenate([even_ref[:, lanes], odd_ref[:, lanes]], axis=0),
        )

    states = []
    for j in range(3):
        states += two_halves(low, *rows(128 * j))
    heat = 1.4 + 0.27 * spread[:, 768:896]
    g = jnp.where(low, heat[0:64], heat[64:128])
    slots = [
        jnp.where(low, spread[0:64, 128 * n : 128 * n + 128], spread[64:128, 128 * n : 128 * n + 128])
        for n in range(1, 5)
    ]
    prim = primitives(states, g, slots[1:])
    kept = [*states, *prim, *flux_of(states, prim[0], prim[1], slots[1:]), *slots]
    for n, x in enumerate(kept):
        own_ref[n] = x
    scale_ref[...] = (STEP * LIFT) * by_element(metric_ref, (8, 128))


def mortar_kernel(
    from_grp_ref, from_even_ref, from_late_ref, from_odd_ref, sel_ref,
    base_ref, local_ref, sub_ref, own_ref, scale_ref, hot_ref, back_ref, turn_ref, out_hbm, new_ref, sem,
):
    chunk = 16
    low = lane_low((chunk, 128))
    first, second = [[], [], []], [[], [], []]
    spread = jnp.concatenate(
        [jnp.broadcast_to(from_grp_ref[ROWS * n + 24 : ROWS * n + 25, :], (8, 128)) for n in range(8)], axis=0
    )
    row = lax.broadcasted_iota(jnp.int32, (64, 128), 0)
    lane = lax.broadcasted_iota(jnp.int32, (64, 128), 1)
    spread = jnp.where(lane == 16 * jnp.bitwise_and(row, 7), spread, 0.0).astype(bf16)
    grp_heat = 1.4 + 0.27 * dot(spread, jnp.ones((128, 128), bf16))
    for at in range(0, 64, chunk):
        r = slice(at, at + chunk)

        def from_elem(lanes):
            if at < 32:
                return from_even_ref[r, lanes] + from_late_ref[r, lanes]
            return from_odd_ref[at - 32 : at - 32 + chunk, lanes]

        theirs = []
        for j in range(3):
            starts = [ROWS * (at // 8 + n) + 8 * j for n in range(chunk // 8)]
            grp = jnp.concatenate([from_grp_ref[x : x + 8, :] for x in starts], axis=0)
            theirs += two_halves(low, grp, from_elem(slice(128 * j, 128 * j + 128)))
        g = jnp.where(low, grp_heat[r], from_elem(slice(384, 512)))
        mine = [own_ref[n, r] for n in range(6)]
        normal = [own_ref[n, r] for n in range(16, 19)]
        live = own_ref[15, r] > 0.5
        prim = tuple(own_ref[n, r] for n in range(6, 9))
        through = hllc(mine, theirs, prim, primitives(theirs, g, normal), normal)
        corr = [jnp.where(live, own_ref[9 + n, r] - through[n], 0.0) for n in range(6)]
        for j in range(3):
            x, y = two_halves(low, corr[2 * j], corr[2 * j + 1])
            first[j].append(x)
            second[j].append(y)
    corr = jnp.concatenate([x for j in range(3) for x in first[j] + second[j]], axis=0)
    hi, lo = split2(corr)
    wide = dot(jnp.concatenate([hi, lo, hi], axis=1), back_ref[...])
    sub_of = sub_ref[...].astype(jnp.int32)
    turn = turn_ref[...]
    back = []
    for j in range(3):
        r = slice(128 * j, 128 * j + 128)
        y = corr[r]
        for s in range(4):
            y = jnp.where(sub_of == s + 1, wide[r, 128 * s : 128 * s + 128], y)
        back.append(reorder(y, turn))
    hi, lo = split2(jnp.concatenate(back, axis=1))
    summed = dot(hot_ref[...], jnp.concatenate([hi, lo], axis=0))
    total = jnp.concatenate([summed[:, 128 * j : 128 * j + 128] for j in range(3)], axis=0) + local_ref[...]
    low = lane_low((8, 128))
    lift = []
    for v in range(6):
        at = 48 * (v // 2)
        parts = []
        for d in range(3):
            first = total[at + 16 * d : at + 16 * d + 8]
            second = total[at + 16 * d + 8 : at + 16 * d + 16]
            if v % 2 == 0:
                parts.append(jnp.where(low, first, swap(second)))
            else:
                parts.append(jnp.where(low, swap(first), second))
        lift.append(parts)
    side = jnp.concatenate(
        [jnp.concatenate([lift[v][1] for v in range(6)], axis=0), jnp.concatenate([lift[v][2] for v in range(6)], axis=0)],
        axis=1,
    )
    hi, lo = split2(side)
    placed = dot(jnp.concatenate([hi, lo], axis=0), sel_ref[...], 1, 1)
    placed = placed[0:48] + placed[48:96]
    scale = scale_ref[...]
    stores = []
    for v in range(6):
        for t in range(4):
            lanes = slice(128 * t, 128 * t + 128)
            value = placed[8 * v : 8 * v + 8, lanes]
            if t == 0:
                value = value + jnp.where(low, lift[v][0], 0.0)
            if t == 3:
                value = value + jnp.where(low, 0.0, lift[v][0])
            new_ref[v, :, lanes] = base_ref[v, :, lanes] + scale * value
        if v % 2 == 1:
            pair = pl.ds(v - 1, 2)
            stores.append(pltpu.make_async_copy(new_ref.at[pair], out_hbm.at[pair], sem.at[v // 2]))
            stores[-1].start()
    for store in stores:
        store.wait()


SM = pl.BlockSpec(memory_space=pltpu.SMEM)
VM = pl.BlockSpec(memory_space=pltpu.VMEM)


def call(kernel, outs, scalars, args, free=()):
    outs = [s if isinstance(s[0], tuple) else (s, f32) for s in outs]
    held = [
        a if n in scalars else pltpu.with_memory_space_constraint(a, pltpu.VMEM)
        for n, a in enumerate(args)
    ]
    return pl.pallas_call(
        kernel,
        out_shape=[jax.ShapeDtypeStruct(*s) if n in free else pltpu.VMEM(*s) for n, s in enumerate(outs)],
        in_specs=[SM if n in scalars else VM for n in range(len(args))],
        out_specs=[VM] * len(outs),
        compiler_params=pltpu.CompilerParams(vmem_limit_bytes=16 << 20),
    )(*held)


def section(state, material, metric, mortar_proj, mortar_map, mortar_count, neighbours):
    groups = lax.axis_size("grp")
    n_elem = lax.axis_size("elem")
    elements = jnp.transpose(state, (1, 0, 2))
    info = mortar_map[0]
    counts = mortar_count[0]
    select = jnp.asarray(face_select(), bf16)
    deriv = deriv_table()
    d_hi = deriv.astype(bf16)
    d_lo = (deriv - d_hi.astype(np.float32)).astype(bf16)
    derivs = jnp.asarray(np.concatenate([d_hi, d_lo], axis=1))
    codes_c = jnp.asarray(code_table([{n: 1} for n in range(7)]), bf16)

    far = pl.BlockSpec(memory_space=pl.ANY)
    grp, even, odd, faces, mine, kept = pl.pallas_call(
        trace_kernel,
        out_shape=[
            jax.ShapeDtypeStruct((groups * ROWS, 128), f32),
            pltpu.VMEM((CAPS, 512), f32),
            pltpu.VMEM((CAPS, 512), f32),
            pltpu.VMEM((144, 128), f32),
            pltpu.VMEM((groups, CAPG, 384), f32),
            pltpu.VMEM((8, SLOTS), jnp.int32),
        ],
        in_specs=[far] * 4,
        out_specs=[far] + [VM] * 5,
        scratch_shapes=[
            pltpu.VMEM((6, 8, 512), f32),
            pltpu.SMEM((8,), jnp.int32),
            pltpu.VMEM((4, SLOTS), jnp.int32),
            pltpu.VMEM((4, 64, 64), f32),
            pltpu.VMEM((512, 256), bf16),
            pltpu.VMEM((groups * ROWS, 128), f32),
            pltpu.SemaphoreType.DMA((4,)),
            pltpu.SemaphoreType.DMA((1,)),
        ],
        name="traces",
        compiler_params=pltpu.CompilerParams(vmem_limit_bytes=16 << 20),
    )(*(pltpu.with_memory_space_constraint(a, pltpu.HBM) for a in (elements, material, info, mortar_proj)))
    swaps = [
        [((i + n) * groups + g, (i + 1 - n) * groups + g) for i in range(first, n_elem - 1, 2) for g in range(groups) for n in range(2)]
        for first in range(2)
    ]
    late = [(0, groups), (groups, 0)]
    axes = ("elem", "grp")
    from_even = lax.ppermute(even, axes, [pair for pair in swaps[0] if pair not in late])
    blocks = grp.reshape(groups, ROWS, 1, 128)
    arrived = lax.all_to_all(blocks, "grp", split_axis=0, concat_axis=0, tiled=True).reshape(groups * ROWS, 128)
    from_odd = lax.ppermute(odd, axes, swaps[1])
    from_late = lax.ppermute(even, axes, late)
    held = call(
        local_kernel,
        [
            (6, 8, 512), (144, 128), (SLOTS, 128), (19, 64, 128), (8, 128),
            ((48, 256), bf16), ((384, 512), bf16), ((SLOTS, 128), jnp.int32),
        ],
        {1, 2, 3},
        (
            elements, material, metric, counts, neighbours, faces, derivs, kept, mortar_proj, codes_c,
            mine, even, odd,
        ),
    )
    operands = (arrived, from_even, from_late, from_odd, select, *held)
    new = pl.pallas_call(
        mortar_kernel,
        out_shape=jax.ShapeDtypeStruct((6, 8, 512), f32),
        in_specs=[VM] * len(operands),
        out_specs=far,
        scratch_shapes=[pltpu.VMEM((6, 8, 512), f32), pltpu.SemaphoreType.DMA((3,))],
        name="mortar",
        compiler_params=pltpu.CompilerParams(vmem_limit_bytes=16 << 20),
    )(*(pltpu.with_memory_space_constraint(a, pltpu.VMEM) for a in operands))
    return jnp.transpose(new, (1, 0, 2))


def solution(mesh):
    return jax.shard_map(
        section,
        mesh=mesh,
        in_specs=(
            P(("elem", "grp"), None, None),
            P(("elem", "grp")),
            P(("elem", "grp")),
            P(),
            P(("elem", "grp"), None, None),
            P(("elem", "grp"), None),
            P(("elem", "grp"), None),
        ),
        out_specs=P(("elem", "grp"), None, None),
        check_vma=False,
    )
```

```python
import jax
import jax.numpy as jnp
import numpy as np
from jax import lax
from jax.experimental import pallas as pl
from jax.experimental.pallas import tpu as pltpu
from jax.sharding import PartitionSpec as P


CAPG = 8
CAPS = 32
SLOTS = 128
ROWS = 25
STEP = 0.002
LIFT = 49.0

f32 = jnp.float32
bf16 = jnp.bfloat16


def cheb_matrix():
    points = -np.cos(np.pi * np.arange(8) / 7.0)
    factor = np.array([2.0, 1.0, 1.0, 1.0, 1.0, 1.0, 1.0, 2.0])
    alternating = np.where(np.arange(8) % 2 == 0, 1.0, -1.0)
    scaled = factor * alternating
    differ = points[:, None] - points[None, :] + np.eye(8)
    matrix = scaled[:, None] / scaled[None, :] / differ
    matrix = matrix * (1.0 - np.eye(8))
    return (matrix - np.eye(8) * matrix.sum(axis=1)[:, None]).astype(np.float32)


def face_select():
    grid = np.arange(512).reshape(8, 8, 8)
    planes = [grid[:, 0], grid[:, 7], grid[:, :, 0], grid[:, :, 7]]
    nodes = np.concatenate([p.reshape(64) for p in planes])
    return (np.arange(512)[:, None] == nodes[None, :]).astype(np.float32)


def deriv_table():
    d = cheb_matrix()
    along_b = np.kron(np.eye(2), np.kron(d, np.eye(8))).T
    along_c = np.kron(np.eye(16), d).T
    return np.concatenate([along_b, along_c], axis=0).astype(np.float32)


def code_table(rows):
    out = np.zeros((16, 128 * len(rows)), np.float32)
    for block, weights in enumerate(rows):
        for row, weight in weights.items():
            out[row, block * 128 : (block + 1) * 128] = weight
    return out


def dot(a, b, ca=1, cb=0):
    return lax.dot_general(a, b, (((ca,), (cb,)), ((), ())), preferred_element_type=f32)


def split2(x):
    hi = x.astype(bf16)
    return hi, (x - hi.astype(f32)).astype(bf16)


def split3(x):
    hi = x.astype(bf16)
    rest = x - hi.astype(f32)
    mid = rest.astype(bf16)
    return hi, mid, (rest - mid.astype(f32)).astype(bf16)


def lane_low(shape):
    return lax.broadcasted_iota(jnp.int32, shape, len(shape) - 1) % 128 < 64


def swap(x):
    return pltpu.roll(x, 64, 1)


def join_pair(low, a, b):
    return jnp.where(low, a, swap(b))


def by_element(ref, shape):
    row = lax.broadcasted_iota(jnp.int32, shape, 0)
    out = jnp.full(shape, ref[0], f32) if ref.dtype == f32 else jnp.full(shape, ref[0].astype(f32), f32)
    for e in range(1, 8):
        out = jnp.where(row == e, ref[e].astype(f32), out)
    return out


def project_blocks(proj_ref):
    zero = jnp.zeros((64, 64), f32)
    blocks = []
    for s in range(4):
        p = proj_ref[s]
        top = jnp.concatenate([p, zero], axis=1)
        bottom = jnp.concatenate([zero, p], axis=1)
        blocks.append(jnp.concatenate([top, bottom], axis=0))
    return blocks


def slot_material(mat_ref, element):
    out = jnp.zeros(element.shape, f32)
    for e in range(8):
        out = jnp.where(element == e, mat_ref[e].astype(f32), out)
    return out


def code_rows(rows):
    pad = [jnp.zeros((1, SLOTS), f32)] * (16 - len(rows))
    return jnp.concatenate(rows + pad, axis=0).astype(bf16)


def selection():
    lane = lax.broadcasted_iota(jnp.int32, (1, 512), 1)
    far = jnp.bitwise_and(lax.shift_right_logical(lane, 7), 1)
    p = jnp.bitwise_and(lax.shift_right_logical(lane, 3), 7)
    r = jnp.bitwise_and(lane, 7)
    node = 64 * p + jnp.where(lane < 256, r + 56 * far, 8 * r + 7 * far)
    row = lax.broadcasted_iota(jnp.int32, (512, 512), 0)
    return jnp.where(row == node, 1.0, 0.0).astype(bf16)


def lane_sources(orient, back):
    lane = lax.broadcasted_iota(jnp.int32, orient.shape, 1)
    p = jnp.bitwise_and(lax.shift_right_logical(lane, 3), 7)
    r = jnp.bitwise_and(lane, 7)
    turn = jnp.bitwise_and(orient, 4) != 0
    flip_p = jnp.bitwise_and(orient, 1) != 0
    flip_r = jnp.bitwise_and(orient, 2) != 0
    if not back:
        p, r = jnp.where(turn, r, p), jnp.where(turn, p, r)
    p = jnp.where(flip_p, 7 - p, p)
    r = jnp.where(flip_r, 7 - r, r)
    if back:
        p, r = jnp.where(turn, r, p), jnp.where(turn, p, r)
    return jnp.bitwise_and(lane, 64) + 8 * p + r


def reorder(x, source):
    return jnp.take_along_axis(x, source, axis=1, mode="promise_in_bounds")


def stacked(table):
    gap = jnp.zeros((16, table.shape[1]), bf16)
    terms = []
    for term in split3(table):
        terms += [term, gap]
    return jnp.concatenate(terms + [jnp.zeros((64, table.shape[1]), bf16)], axis=0)


def trace_kernel(
    state_hbm, mat_hbm, map_hbm, proj_hbm, grp_hbm, even_ref, odd_ref, face_ref, mine_ref, info_ref,
    state_ref, mat_ref, map_ref, proj_ref, sel_ref, pack_ref, in_sem, out_sem,
):
    def load(src, dst, n):
        copy = pltpu.make_async_copy(src, dst, in_sem.at[n])
        copy.start()
        return copy

    map_load = load(map_hbm, map_ref, 0)
    mat_load = load(mat_hbm, mat_ref, 1)
    state_load = load(state_hbm, state_ref, 2)
    proj_load = load(proj_hbm, proj_ref, 3)
    sel_ref[...] = selection()
    code_row = lax.broadcasted_iota(jnp.int32, (16, 128), 0)
    weights = jnp.where(code_row == 0, 1.0, jnp.where(code_row == 1, 8.0, 0.0))
    spreads = jnp.concatenate([weights] + [jnp.where(code_row == n, 1.0, 0.0) for n in range(2, 5)], axis=1)
    place = lax.broadcasted_iota(jnp.int32, (SLOTS, 128), 0)
    lane = lax.broadcasted_iota(jnp.int32, (SLOTS, 128), 1)
    fan = jnp.where(jnp.bitwise_and(place, 7) == lax.shift_right_logical(lane, 4), 1.0, 0.0).astype(bf16)
    map_load.wait()
    mat_load.wait()
    state_load.wait()
    proj_load.wait()
    info = jnp.concatenate([map_ref[...]] * 2, axis=0)
    slot = lax.broadcasted_iota(jnp.int32, (8, SLOTS), 1)
    turned = jnp.where(slot < 96, pltpu.roll(info, 96, 1), pltpu.roll(info, 32, 1))
    odd = jnp.bitwise_and(lax.axis_index("elem"), 1) == 1
    info = jnp.where((slot >= 64) & odd, turned, info)
    info_ref[...] = info
    element, face, sub, orient = (info[i : i + 1] for i in range(4))
    material = slot_material(mat_ref, element)
    codes = code_rows([element.astype(f32), face.astype(f32), sub.astype(f32), orient.astype(f32), material])
    spread = dot(codes, spreads.astype(bf16), 0, 0)
    index = spread[:, 0:128].astype(jnp.int32)
    sub_of = spread[:, 128:256].astype(jnp.int32)
    source = lane_sources(spread[:, 256:384].astype(jnp.int32), False)
    hit = jnp.bitwise_and(lane, 63) == index
    one_hot = jnp.concatenate(
        [jnp.where(hit, 1.0, 0.0), jnp.where(hit & (lane < 64), 1.0, 0.0)], axis=1
    ).astype(bf16)
    heat = 1.4 + 0.27 * spread[:, 384:512]
    peer = lax.broadcasted_iota(jnp.int32, (8, 128), 0)
    by_peer = jnp.where(lax.shift_right_logical(slot, 3) == peer, material, 0.0)
    heat_rows = dot(by_peer.astype(bf16), fan)
    low = lane_low((8, 128))
    flat = state_ref[...].reshape(48, 512)
    picked = dot(jnp.concatenate(split3(flat), axis=0), sel_ref[...])
    picked = picked[0:48] + picked[48:96] + picked[96:144]
    rows = []
    for j in range(3):
        x, y = state_ref[2 * j], state_ref[2 * j + 1]
        rows.append(jnp.where(low, x[:, 0:128], swap(y[:, 0:128])))
        rows.append(jnp.where(low, swap(x[:, 384:512]), y[:, 384:512]))
        for k in range(4):
            lanes = slice(128 * k, 128 * k + 128)
            rows.append(jnp.where(low, picked[16 * j : 16 * j + 8, lanes], picked[16 * j + 8 : 16 * j + 16, lanes]))
    faces = jnp.concatenate(rows, axis=0)
    face_ref[...] = faces
    gathered = dot(one_hot, stacked(jnp.concatenate([faces[48 * j : 48 * j + 48] for j in range(3)], axis=1)))
    x = [reorder(gathered[:, 128 * j : 128 * j + 128], source) for j in range(3)]
    x = jnp.concatenate([x[j][at : at + 64] for at in (0, 64) for j in range(3)], axis=0)
    b_hi, b_lo = split2(jnp.concatenate(project_blocks(proj_ref), axis=0))
    hi, lo = split2(x)
    wide = dot(jnp.concatenate([hi, lo], axis=1), jnp.concatenate([b_hi, b_hi], axis=1), 1, 1) + dot(hi, b_lo, 1, 1)

    def projected(j, at):
        r = slice(64 * j + 3 * at, 64 * j + 3 * at + 64)
        w = x[r]
        for n in range(4):
            w = jnp.where(sub_of[at : at + 64] == n + 1, wide[r, 128 * n : 128 * n + 128], w)
        return w

    for j in range(3):
        w = projected(j, 0)
        for g in range(8):
            part = w[8 * g : 8 * g + 8]
            mine_ref[g, :, 128 * j : 128 * j + 128] = part
            pack_ref[ROWS * g + 8 * j : ROWS * g + 8 * j + 8, :] = part
    for g in range(8):
        pack_ref[ROWS * g + 24 : ROWS * g + 25, :] = heat_rows[g : g + 1]
    store = pltpu.make_async_copy(pack_ref, grp_hbm, out_sem.at[0])
    store.start()
    for j in range(3):
        w = projected(j, 64)
        even_ref[:, 128 * j : 128 * j + 128] = w[0:32]
        odd_ref[:, 128 * j : 128 * j + 128] = w[32:64]
    even_ref[:, 384:512] = heat[64:96]
    odd_ref[:, 384:512] = heat[96:128]
    store.wait()


def primitives(u, g, n):
    inv = 1.0 / u[0]
    p = (g - 1.0) * (u[4] - 0.5 * inv * (u[1] * u[1] + u[2] * u[2] + u[3] * u[3]))
    s = (n[0] * u[1] + n[1] * u[2] + n[2] * u[3]) * inv
    return p, s, jnp.sqrt(g * p * inv)


def flux_of(u, p, s, n):
    return [u[0] * s, u[1] * s + p * n[0], u[2] * s + p * n[1], u[3] * s + p * n[2], (u[4] + p) * s, u[5] * s]


def hllc(u_l, u_r, prim_l, prim_r, n):
    (p_l, s_l, c_l), (p_r, s_r, c_r) = prim_l, prim_r
    left = jnp.minimum(s_l - c_l, s_r - c_r)
    right = jnp.maximum(s_l + c_l, s_r + c_r)
    mass_l = u_l[0] * (left - s_l)
    mass_r = u_r[0] * (right - s_r)
    middle = (p_r - p_l + mass_l * s_l - mass_r * s_r) / (mass_l - mass_r)
    take = (left >= 0.0) | (middle >= 0.0)
    u = [jnp.where(take, x, y) for x, y in zip(u_l, u_r)]
    p = jnp.where(take, p_l, p_r)
    s = jnp.where(take, s_l, s_r)
    mass = jnp.where(take, mass_l, mass_r)
    wave = jnp.where(take, left, right)
    use_star = jnp.where(take, -left, right) > 0.0
    a = jnp.where(use_star, wave * (middle - s) / (wave - middle), 0.0)
    speed = s + a
    push = a * mass
    lift = p + push
    return [
        u[0] * speed,
        u[1] * speed + lift * n[0],
        u[2] * speed + lift * n[1],
        u[3] * speed + lift * n[2],
        (u[4] + p) * speed + push * middle,
        u[5] * speed,
    ]


def two_halves(low, first, second):
    return jnp.where(low, first, swap(second)), jnp.where(low, swap(first), second)


def local_kernel(
    state_ref, mat_ref, metric_ref, count_ref, near_ref, face_ref, deriv_ref, info_ref, proj_ref, code_ref,
    mine_ref, even_ref, odd_ref, base_ref, local_ref, sub_ref, own_ref, scale_ref, hot_ref, back_ref, turn_ref,
):
    info = info_ref[...]
    element, face, sub, orient = (info[i : i + 1] for i in range(4))
    slot = lax.broadcasted_iota(jnp.int32, (1, SLOTS), 1)
    odd = jnp.bitwise_and(lax.axis_index("elem"), 1)
    side = jnp.bitwise_xor(jnp.bitwise_and(lax.shift_right_logical(slot, 5), 1), odd)
    group = jnp.where(slot < 64, lax.shift_right_logical(slot, 3), 8 + side)
    position = jnp.where(slot < 64, jnp.bitwise_and(slot, 7), jnp.bitwise_and(slot, 31))
    limit = jnp.zeros((1, SLOTS), jnp.int32)
    for n in range(10):
        limit = jnp.where(group == n, count_ref[n], limit)
    alive = jnp.where(position < limit, 1.0, 0.0)
    sign = jnp.where(jnp.bitwise_and(face, 1) == 1, 1.0, -1.0)
    axis = lax.shift_right_logical(face, 1)
    codes = code_rows(
        [sub.astype(f32), alive]
        + [jnp.where(axis == d, sign, 0.0) for d in range(3)]
        + [orient.astype(f32), slot_material(mat_ref, element)]
    )
    spread = dot(codes, code_ref[...], 0, 0)
    sub_ref[...] = spread[:, 0:128]
    turn_ref[...] = lane_sources(spread[:, 640:768].astype(jnp.int32), True)
    row = lax.broadcasted_iota(jnp.int32, (48, SLOTS), 0)
    beta = jnp.where(sub == 0, 1.0, 0.25)
    hot = jnp.where(row == 8 * face + element, beta, 0.0).astype(bf16)
    hot_ref[:, 0:128] = hot
    hot_ref[:, 128:256] = hot
    b_hi, b_lo = split2(jnp.concatenate(project_blocks(proj_ref), axis=1))
    back_ref[0:128, :] = b_hi
    back_ref[128:256, :] = b_hi
    back_ref[256:384, :] = b_lo
    heat = 1.4 + 0.27 * by_element(mat_ref, (8, 512))
    u = [state_ref[v] for v in range(6)]
    inv = 1.0 / u[0]
    vel = [u[1] * inv, u[2] * inv, u[3] * inv]
    p = (heat - 1.0) * (u[4] - 0.5 * (u[1] * vel[0] + u[2] * vel[1] + u[3] * vel[2]))
    fluxes = []
    for d in range(3):
        s = vel[d]
        f = [u[0] * s, u[1] * s, u[2] * s, u[3] * s, (u[4] + p) * s, u[5] * s]
        f[1 + d] = f[1 + d] + p
        fluxes.append(f)
    rows = []
    for v in range(6):
        for t in range(4):
            r = slice(128 * t, 128 * t + 128)
            rows.append(jnp.concatenate([fluxes[1][v][:, r], fluxes[2][v][:, r]], axis=1))
    hi, lo = split2(jnp.concatenate(rows, axis=0))
    d_hi, d_lo = deriv_ref[:, 0:128], deriv_ref[:, 128:256]
    main = dot(jnp.concatenate([hi, lo], axis=0), d_hi)
    bc = main[0:192] + main[192:384] + dot(hi, d_lo)
    low = lane_low((8, 128))
    deriv = cheb_matrix()
    scale = STEP * by_element(metric_ref, (8, 128))
    for v in range(6):
        x = [fluxes[0][v][:, 128 * t : 128 * t + 128] for t in range(4)]
        xs = [swap(a) for a in x]
        for t in range(4):
            acc = bc[32 * v + 8 * t : 32 * v + 8 * t + 8]
            for k in range(4):
                same = jnp.where(low, float(deriv[2 * t, 2 * k]), float(deriv[2 * t + 1, 2 * k + 1]))
                cross = jnp.where(low, float(deriv[2 * t, 2 * k + 1]), float(deriv[2 * t + 1, 2 * k]))
                acc = acc + same * x[k] + cross * xs[k]
            r = slice(128 * t, 128 * t + 128)
            base_ref[v, :, r] = u[v][:, r] - scale * acc
    faces = face_ref[...]
    lane = lax.broadcasted_iota(jnp.int32, (8, 256), 1)
    hot, live = [], []
    for k in range(6):
        near = jnp.broadcast_to(near_ref[:, k : k + 1], (8, 256))
        live.append((near >= 0)[:, 0:128])
        target = 8 * (k ^ 1) + near
        hit = (jnp.bitwise_and(lane, 63) == target) & (near >= 0) & (lane < 192)
        hot.append(jnp.where(hit, 1.0, 0.0))
    hot = jnp.concatenate(hot, axis=0).astype(bf16)
    heat_rows = jnp.concatenate([heat[:, 0:128]] * 6, axis=0)
    table = jnp.concatenate([faces[0:48], faces[48:96], faces[96:144], heat_rows], axis=1)
    theirs = dot(hot, stacked(table))
    low = lane_low((48, 128))
    row = lax.broadcasted_iota(jnp.int32, (48, 128), 0)
    sign = jnp.where(jnp.bitwise_and(row, 8) != 0, 1.0, -1.0)
    normal = [jnp.where(lax.shift_right_logical(row, 4) == d, sign, 0.0) for d in range(3)]
    mine, other = [], []
    for j in range(3):
        x, y = faces[48 * j : 48 * j + 48], theirs[:, 128 * j : 128 * j + 128]
        mine += [x, swap(x)]
        other += [y, swap(y)]
    prim = primitives(mine, heat_rows, normal)
    flux = flux_of(mine, prim[0], prim[1], normal)
    through = hllc(mine, other, prim, primitives(other, theirs[:, 384:512], normal), normal)
    corr = [f - h for f, h in zip(flux, through)]
    for j in range(3):
        packed = join_pair(low, corr[2 * j], corr[2 * j + 1])
        for k in range(6):
            local_ref[48 * j + 8 * k : 48 * j + 8 * k + 8, :] = jnp.where(
                live[k], packed[8 * k : 8 * k + 8], 0.0
            )
    low = lane_low((64, 128))

    def rows(at):
        lanes = slice(at, at + 128)
        return (
            jnp.concatenate([mine_ref[g, :, lanes] for g in range(8)], axis=0),
            jnp.concatenate([even_ref[:, lanes], odd_ref[:, lanes]], axis=0),
        )

    states = []
    for j in range(3):
        states += two_halves(low, *rows(128 * j))
    heat = 1.4 + 0.27 * spread[:, 768:896]
    g = jnp.where(low, heat[0:64], heat[64:128])
    slots = [
        jnp.where(low, spread[0:64, 128 * n : 128 * n + 128], spread[64:128, 128 * n : 128 * n + 128])
        for n in range(1, 5)
    ]
    prim = primitives(states, g, slots[1:])
    kept = [*states, *prim, *flux_of(states, prim[0], prim[1], slots[1:]), *slots]
    for n, x in enumerate(kept):
        own_ref[n] = x
    scale_ref[...] = (STEP * LIFT) * by_element(metric_ref, (8, 128))


def mortar_kernel(
    from_grp_ref, from_even_ref, from_late_ref, from_odd_ref, sel_ref,
    base_ref, local_ref, sub_ref, own_ref, scale_ref, hot_ref, back_ref, turn_ref, out_hbm, new_ref, sem,
):
    chunk = 16
    low = lane_low((chunk, 128))
    first, second = [[], [], []], [[], [], []]
    spread = jnp.concatenate(
        [jnp.broadcast_to(from_grp_ref[ROWS * n + 24 : ROWS * n + 25, :], (8, 128)) for n in range(8)], axis=0
    )
    row = lax.broadcasted_iota(jnp.int32, (64, 128), 0)
    lane = lax.broadcasted_iota(jnp.int32, (64, 128), 1)
    spread = jnp.where(lane == 16 * jnp.bitwise_and(row, 7), spread, 0.0).astype(bf16)
    grp_heat = 1.4 + 0.27 * dot(spread, jnp.ones((128, 128), bf16))
    for at in range(0, 64, chunk):
        r = slice(at, at + chunk)

        def from_elem(lanes):
            if at < 32:
                return from_even_ref[r, lanes] + from_late_ref[r, lanes]
            return from_odd_ref[at - 32 : at - 32 + chunk, lanes]

        theirs = []
        for j in range(3):
            starts = [ROWS * (at // 8 + n) + 8 * j for n in range(chunk // 8)]
            grp = jnp.concatenate([from_grp_ref[x : x + 8, :] for x in starts], axis=0)
            theirs += two_halves(low, grp, from_elem(slice(128 * j, 128 * j + 128)))
        g = jnp.where(low, grp_heat[r], from_elem(slice(384, 512)))
        mine = [own_ref[n, r] for n in range(6)]
        normal = [own_ref[n, r] for n in range(16, 19)]
        live = own_ref[15, r] > 0.5
        prim = tuple(own_ref[n, r] for n in range(6, 9))
        through = hllc(mine, theirs, prim, primitives(theirs, g, normal), normal)
        corr = [jnp.where(live, own_ref[9 + n, r] - through[n], 0.0) for n in range(6)]
        for j in range(3):
            x, y = two_halves(low, corr[2 * j], corr[2 * j + 1])
            first[j].append(x)
            second[j].append(y)
    corr = jnp.concatenate([x for j in range(3) for x in first[j] + second[j]], axis=0)
    hi, lo = split2(corr)
    wide = dot(jnp.concatenate([hi, lo, hi], axis=1), back_ref[...])
    sub_of = sub_ref[...].astype(jnp.int32)
    turn = turn_ref[...]
    back = []
    for j in range(3):
        r = slice(128 * j, 128 * j + 128)
        y = corr[r]
        for s in range(4):
            y = jnp.where(sub_of == s + 1, wide[r, 128 * s : 128 * s + 128], y)
        back.append(reorder(y, turn))
    hi, lo = split2(jnp.concatenate(back, axis=1))
    summed = dot(hot_ref[...], jnp.concatenate([hi, lo], axis=0))
    total = jnp.concatenate([summed[:, 128 * j : 128 * j + 128] for j in range(3)], axis=0) + local_ref[...]
    low = lane_low((8, 128))
    lift = []
    for v in range(6):
        at = 48 * (v // 2)
        parts = []
        for d in range(3):
            first = total[at + 16 * d : at + 16 * d + 8]
            second = total[at + 16 * d + 8 : at + 16 * d + 16]
            if v % 2 == 0:
                parts.append(jnp.where(low, first, swap(second)))
            else:
                parts.append(jnp.where(low, swap(first), second))
        lift.append(parts)
    side = jnp.concatenate(
        [jnp.concatenate([lift[v][1] for v in range(6)], axis=0), jnp.concatenate([lift[v][2] for v in range(6)], axis=0)],
        axis=1,
    )
    hi, lo = split2(side)
    placed = dot(jnp.concatenate([hi, lo], axis=0), sel_ref[...], 1, 1)
    placed = placed[0:48] + placed[48:96]
    scale = scale_ref[...]
    stores = []
    for v in range(6):
        for t in range(4):
            lanes = slice(128 * t, 128 * t + 128)
            value = placed[8 * v : 8 * v + 8, lanes]
            if t == 0:
                value = value + jnp.where(low, lift[v][0], 0.0)
            if t == 3:
                value = value + jnp.where(low, 0.0, lift[v][0])
            new_ref[v, :, lanes] = base_ref[v, :, lanes] + scale * value
        if v % 2 == 1:
            pair = pl.ds(v - 1, 2)
            stores.append(pltpu.make_async_copy(new_ref.at[pair], out_hbm.at[pair], sem.at[v // 2]))
            stores[-1].start()
    for store in stores:
        store.wait()


SM = pl.BlockSpec(memory_space=pltpu.SMEM)
VM = pl.BlockSpec(memory_space=pltpu.VMEM)


def call(kernel, outs, scalars, args, free=()):
    outs = [s if isinstance(s[0], tuple) else (s, f32) for s in outs]
    held = [
        a if n in scalars else pltpu.with_memory_space_constraint(a, pltpu.VMEM)
        for n, a in enumerate(args)
    ]
    return pl.pallas_call(
        kernel,
        out_shape=[jax.ShapeDtypeStruct(*s) if n in free else pltpu.VMEM(*s) for n, s in enumerate(outs)],
        in_specs=[SM if n in scalars else VM for n in range(len(args))],
        out_specs=[VM] * len(outs),
        compiler_params=pltpu.CompilerParams(vmem_limit_bytes=16 << 20),
    )(*held)


def traces(groups, elements, material, info, mortar_proj):
    far = pl.BlockSpec(memory_space=pl.ANY)
    return pl.pallas_call(
        trace_kernel,
        out_shape=[
            jax.ShapeDtypeStruct((groups * ROWS, 128), f32),
            pltpu.VMEM((CAPS, 512), f32),
            pltpu.VMEM((CAPS, 512), f32),
            pltpu.VMEM((144, 128), f32),
            pltpu.VMEM((groups, CAPG, 384), f32),
            pltpu.VMEM((8, SLOTS), jnp.int32),
        ],
        in_specs=[far] * 4,
        out_specs=[far] + [VM] * 5,
        scratch_shapes=[
            pltpu.VMEM((6, 8, 512), f32),
            pltpu.SMEM((8,), jnp.int32),
            pltpu.VMEM((4, SLOTS), jnp.int32),
            pltpu.VMEM((4, 64, 64), f32),
            pltpu.VMEM((512, 512), bf16),
            pltpu.VMEM((groups * ROWS, 128), f32),
            pltpu.SemaphoreType.DMA((4,)),
            pltpu.SemaphoreType.DMA((1,)),
        ],
        name="traces",
        compiler_params=pltpu.CompilerParams(vmem_limit_bytes=16 << 20),
    )(*(pltpu.with_memory_space_constraint(a, pltpu.HBM) for a in (elements, material, info, mortar_proj)))


def section(state, material, metric, mortar_proj, mortar_map, mortar_count, neighbours):
    groups = lax.axis_size("grp")
    n_elem = lax.axis_size("elem")
    elements = jnp.transpose(state, (1, 0, 2))
    info = mortar_map[0]
    counts = mortar_count[0]
    select = jnp.asarray(face_select(), bf16)
    deriv = deriv_table()
    d_hi = deriv.astype(bf16)
    d_lo = (deriv - d_hi.astype(np.float32)).astype(bf16)
    derivs = jnp.asarray(np.concatenate([d_hi, d_lo], axis=1))
    codes_c = jnp.asarray(code_table([{n: 1} for n in range(7)]), bf16)

    grp, even, odd, faces, mine, kept = traces(groups, elements, material, info, mortar_proj)
    swaps = [
        [((i + n) * groups + g, (i + 1 - n) * groups + g) for i in range(first, n_elem - 1, 2) for g in range(groups) for n in range(2)]
        for first in range(2)
    ]
    late = [(0, groups), (groups, 0)]
    axes = ("elem", "grp")
    from_even = lax.ppermute(even, axes, [pair for pair in swaps[0] if pair not in late])
    blocks = grp.reshape(groups, ROWS, 1, 128)
    arrived = lax.all_to_all(blocks, "grp", split_axis=0, concat_axis=0, tiled=True).reshape(groups * ROWS, 128)
    from_odd = lax.ppermute(odd, axes, swaps[1])
    from_late = lax.ppermute(even, axes, late)
    held = call(
        local_kernel,
        [
            (6, 8, 512), (144, 128), (SLOTS, 128), (19, 64, 128), (8, 128),
            ((48, 256), bf16), ((384, 512), bf16), ((SLOTS, 128), jnp.int32),
        ],
        {1, 2, 3},
        (
            elements, material, metric, counts, neighbours, faces, derivs, kept, mortar_proj, codes_c,
            mine, even, odd,
        ),
    )
    operands = (arrived, from_even, from_late, from_odd, select, *held)
    new = pl.pallas_call(
        mortar_kernel,
        out_shape=jax.ShapeDtypeStruct((6, 8, 512), f32),
        in_specs=[VM] * len(operands),
        out_specs=pl.BlockSpec(memory_space=pl.ANY),
        scratch_shapes=[pltpu.VMEM((6, 8, 512), f32), pltpu.SemaphoreType.DMA((3,))],
        name="mortar",
        compiler_params=pltpu.CompilerParams(vmem_limit_bytes=16 << 20),
    )(*(pltpu.with_memory_space_constraint(a, pltpu.VMEM) for a in operands))
    return jnp.transpose(new, (1, 0, 2))


def solution(mesh):
    return jax.shard_map(
        section,
        mesh=mesh,
        in_specs=(
            P(("elem", "grp"), None, None),
            P(("elem", "grp")),
            P(("elem", "grp")),
            P(),
            P(("elem", "grp"), None, None),
            P(("elem", "grp"), None),
            P(("elem", "grp"), None),
        ),
        out_specs=P(("elem", "grp"), None, None),
        check_vma=False,
    )
```

```python
import jax
import jax.numpy as jnp
import numpy as np
from jax import lax
from jax.experimental import pallas as pl
from jax.experimental.pallas import tpu as pltpu
from jax.sharding import PartitionSpec as P


CAPG = 8
SLOTS = 128
ROWS = 25
STEP = 0.002
LIFT = 49.0

f32 = jnp.float32
bf16 = jnp.bfloat16


def cheb_matrix():
    points = -np.cos(np.pi * np.arange(8) / 7.0)
    factor = np.array([2.0, 1.0, 1.0, 1.0, 1.0, 1.0, 1.0, 2.0])
    alternating = np.where(np.arange(8) % 2 == 0, 1.0, -1.0)
    scaled = factor * alternating
    differ = points[:, None] - points[None, :] + np.eye(8)
    matrix = scaled[:, None] / scaled[None, :] / differ
    matrix = matrix * (1.0 - np.eye(8))
    return (matrix - np.eye(8) * matrix.sum(axis=1)[:, None]).astype(np.float32)


def face_select():
    grid = np.arange(512).reshape(8, 8, 8)
    planes = [grid[:, 0], grid[:, 7], grid[:, :, 0], grid[:, :, 7]]
    nodes = np.concatenate([p.reshape(64) for p in planes])
    return (np.arange(512)[:, None] == nodes[None, :]).astype(np.float32)


def deriv_table():
    d = cheb_matrix()
    along_b = np.kron(np.eye(2), np.kron(d, np.eye(8))).T
    along_c = np.kron(np.eye(16), d).T
    return np.concatenate([along_b, along_c], axis=0).astype(np.float32)


def code_table(rows):
    out = np.zeros((16, 128 * len(rows)), np.float32)
    for block, weights in enumerate(rows):
        for row, weight in weights.items():
            out[row, block * 128 : (block + 1) * 128] = weight
    return out


def dot(a, b, ca=1, cb=0):
    return lax.dot_general(a, b, (((ca,), (cb,)), ((), ())), preferred_element_type=f32)


def split2(x):
    hi = x.astype(bf16)
    return hi, (x - hi.astype(f32)).astype(bf16)


def split3(x):
    hi = x.astype(bf16)
    rest = x - hi.astype(f32)
    mid = rest.astype(bf16)
    return hi, mid, (rest - mid.astype(f32)).astype(bf16)


def lane_low(shape):
    return lax.broadcasted_iota(jnp.int32, shape, len(shape) - 1) % 128 < 64


def swap(x):
    return pltpu.roll(x, 64, 1)


def join_pair(low, a, b):
    return jnp.where(low, a, swap(b))


def by_element(ref, shape):
    row = lax.broadcasted_iota(jnp.int32, shape, 0)
    out = jnp.full(shape, ref[0], f32) if ref.dtype == f32 else jnp.full(shape, ref[0].astype(f32), f32)
    for e in range(1, 8):
        out = jnp.where(row == e, ref[e].astype(f32), out)
    return out


def project_blocks(proj_ref):
    zero = jnp.zeros((64, 64), f32)
    blocks = []
    for s in range(4):
        p = proj_ref[s]
        top = jnp.concatenate([p, zero], axis=1)
        bottom = jnp.concatenate([zero, p], axis=1)
        blocks.append(jnp.concatenate([top, bottom], axis=0))
    return blocks


def slot_material(mat_ref, element):
    out = jnp.zeros(element.shape, f32)
    for e in range(8):
        out = jnp.where(element == e, mat_ref[e].astype(f32), out)
    return out


def code_rows(rows):
    pad = [jnp.zeros((1, SLOTS), f32)] * (16 - len(rows))
    return jnp.concatenate(rows + pad, axis=0).astype(bf16)


def selection():
    lane = lax.broadcasted_iota(jnp.int32, (1, 512), 1)
    far = jnp.bitwise_and(lax.shift_right_logical(lane, 7), 1)
    p = jnp.bitwise_and(lax.shift_right_logical(lane, 3), 7)
    r = jnp.bitwise_and(lane, 7)
    node = 64 * p + jnp.where(lane < 256, r + 56 * far, 8 * r + 7 * far)
    row = lax.broadcasted_iota(jnp.int32, (512, 512), 0)
    return jnp.where(row == node, 1.0, 0.0).astype(bf16)


def lane_sources(orient, back):
    lane = lax.broadcasted_iota(jnp.int32, orient.shape, 1)
    p = jnp.bitwise_and(lax.shift_right_logical(lane, 3), 7)
    r = jnp.bitwise_and(lane, 7)
    turn = jnp.bitwise_and(orient, 4) != 0
    flip_p = jnp.bitwise_and(orient, 1) != 0
    flip_r = jnp.bitwise_and(orient, 2) != 0
    if not back:
        p, r = jnp.where(turn, r, p), jnp.where(turn, p, r)
    p = jnp.where(flip_p, 7 - p, p)
    r = jnp.where(flip_r, 7 - r, r)
    if back:
        p, r = jnp.where(turn, r, p), jnp.where(turn, p, r)
    return jnp.bitwise_and(lane, 64) + 8 * p + r


def reorder(x, source):
    return jnp.take_along_axis(x, source, axis=1, mode="promise_in_bounds")


def stacked(table):
    gap = jnp.zeros((16, table.shape[1]), bf16)
    terms = []
    for term in split3(table):
        terms += [term, gap]
    return jnp.concatenate(terms + [jnp.zeros((64, table.shape[1]), bf16)], axis=0)


def trace_kernel(
    state_hbm, mat_hbm, map_hbm, proj_hbm, grp_hbm, even_ref, odd_ref, face_ref, mine_ref, info_ref,
    state_ref, mat_ref, map_ref, proj_ref, sel_ref, pack_ref, in_sem, out_sem,
):
    def load(src, dst, n):
        copy = pltpu.make_async_copy(src, dst, in_sem.at[n])
        copy.start()
        return copy

    map_load = load(map_hbm, map_ref, 0)
    mat_load = load(mat_hbm, mat_ref, 1)
    state_load = load(state_hbm, state_ref, 2)
    proj_load = load(proj_hbm, proj_ref, 3)
    sel_ref[...] = selection()
    code_row = lax.broadcasted_iota(jnp.int32, (16, 128), 0)
    weights = jnp.where(code_row == 0, 1.0, jnp.where(code_row == 1, 8.0, 0.0))
    spreads = jnp.concatenate([weights] + [jnp.where(code_row == n, 1.0, 0.0) for n in range(2, 5)], axis=1)
    place = lax.broadcasted_iota(jnp.int32, (SLOTS, 128), 0)
    lane = lax.broadcasted_iota(jnp.int32, (SLOTS, 128), 1)
    fan = jnp.where(jnp.bitwise_and(place, 7) == lax.shift_right_logical(lane, 4), 1.0, 0.0).astype(bf16)
    map_load.wait()
    mat_load.wait()
    state_load.wait()
    proj_load.wait()
    info = jnp.concatenate([map_ref[...]] * 2, axis=0)
    slot = lax.broadcasted_iota(jnp.int32, (8, SLOTS), 1)
    turned = jnp.where(slot < 96, pltpu.roll(info, 96, 1), pltpu.roll(info, 32, 1))
    odd = jnp.bitwise_and(lax.axis_index("elem"), 1) == 1
    info = jnp.where((slot >= 64) & odd, turned, info)
    info_ref[...] = info
    element, face, sub, orient = (info[i : i + 1] for i in range(4))
    material = slot_material(mat_ref, element)
    codes = code_rows([element.astype(f32), face.astype(f32), sub.astype(f32), orient.astype(f32), material])
    spread = dot(codes, spreads.astype(bf16), 0, 0)
    index = spread[:, 0:128].astype(jnp.int32)
    sub_of = spread[:, 128:256].astype(jnp.int32)
    source = lane_sources(spread[:, 256:384].astype(jnp.int32), False)
    hit = jnp.bitwise_and(lane, 63) == index
    one_hot = jnp.concatenate(
        [jnp.where(hit, 1.0, 0.0), jnp.where(hit & (lane < 64), 1.0, 0.0)], axis=1
    ).astype(bf16)
    heat = 1.4 + 0.27 * spread[:, 384:512]
    peer = lax.broadcasted_iota(jnp.int32, (8, 128), 0)
    by_peer = jnp.where(lax.shift_right_logical(slot, 3) == peer, material, 0.0)
    heat_rows = dot(by_peer.astype(bf16), fan)
    low = lane_low((8, 128))
    flat = state_ref[...].reshape(48, 512)
    picked = dot(jnp.concatenate(split3(flat), axis=0), sel_ref[...])
    picked = picked[0:48] + picked[48:96] + picked[96:144]
    rows = []
    for j in range(3):
        x, y = state_ref[2 * j], state_ref[2 * j + 1]
        rows.append(jnp.where(low, x[:, 0:128], swap(y[:, 0:128])))
        rows.append(jnp.where(low, swap(x[:, 384:512]), y[:, 384:512]))
        for k in range(4):
            lanes = slice(128 * k, 128 * k + 128)
            rows.append(jnp.where(low, picked[16 * j : 16 * j + 8, lanes], picked[16 * j + 8 : 16 * j + 16, lanes]))
    faces = jnp.concatenate(rows, axis=0)
    face_ref[...] = faces
    gathered = dot(one_hot, stacked(jnp.concatenate([faces[48 * j : 48 * j + 48] for j in range(3)], axis=1)))
    x = [reorder(gathered[:, 128 * j : 128 * j + 128], source) for j in range(3)]
    x = jnp.concatenate([x[j][at : at + 64] for at in (0, 64) for j in range(3)], axis=0)
    b_hi, b_lo = split2(jnp.concatenate(project_blocks(proj_ref), axis=0))
    hi, lo = split2(x)
    wide = dot(jnp.concatenate([hi, lo], axis=1), jnp.concatenate([b_hi, b_hi], axis=1), 1, 1) + dot(hi, b_lo, 1, 1)

    def projected(j, at):
        r = slice(64 * j + 3 * at, 64 * j + 3 * at + 64)
        w = x[r]
        for n in range(4):
            w = jnp.where(sub_of[at : at + 64] == n + 1, wide[r, 128 * n : 128 * n + 128], w)
        return w

    for j in range(3):
        w = projected(j, 0)
        for g in range(8):
            part = w[8 * g : 8 * g + 8]
            mine_ref[g, :, 128 * j : 128 * j + 128] = part
            pack_ref[ROWS * g + 8 * j : ROWS * g + 8 * j + 8, :] = part
    for g in range(8):
        pack_ref[ROWS * g + 24 : ROWS * g + 25, :] = heat_rows[g : g + 1]
    store = pltpu.make_async_copy(pack_ref, grp_hbm, out_sem.at[0])
    store.start()
    for j in range(3):
        w = projected(j, 64)
        for t in range(4):
            even_ref[24 * t + 8 * j : 24 * t + 8 * j + 8, :] = w[8 * t : 8 * t + 8]
            odd_ref[24 * t + 8 * j : 24 * t + 8 * j + 8, :] = w[32 + 8 * t : 40 + 8 * t]
    quarter = lax.shift_right_logical(lax.broadcasted_iota(jnp.int32, (8, 128), 1), 5)
    for ref, at in ((even_ref, 64), (odd_ref, 96)):
        tile = heat[at : at + 8]
        for t in range(1, 4):
            tile = jnp.where(quarter == t, heat[at + 8 * t : at + 8 * t + 8], tile)
        ref[96:104, :] = tile
    store.wait()


def primitives(u, g, n):
    inv = 1.0 / u[0]
    p = (g - 1.0) * (u[4] - 0.5 * inv * (u[1] * u[1] + u[2] * u[2] + u[3] * u[3]))
    s = (n[0] * u[1] + n[1] * u[2] + n[2] * u[3]) * inv
    return p, s, jnp.sqrt(g * p * inv)


def flux_of(u, p, s, n):
    return [u[0] * s, u[1] * s + p * n[0], u[2] * s + p * n[1], u[3] * s + p * n[2], (u[4] + p) * s, u[5] * s]


def hllc(u_l, u_r, prim_l, prim_r, n):
    (p_l, s_l, c_l), (p_r, s_r, c_r) = prim_l, prim_r
    left = jnp.minimum(s_l - c_l, s_r - c_r)
    right = jnp.maximum(s_l + c_l, s_r + c_r)
    mass_l = u_l[0] * (left - s_l)
    mass_r = u_r[0] * (right - s_r)
    middle = (p_r - p_l + mass_l * s_l - mass_r * s_r) / (mass_l - mass_r)
    take = (left >= 0.0) | (middle >= 0.0)
    u = [jnp.where(take, x, y) for x, y in zip(u_l, u_r)]
    p = jnp.where(take, p_l, p_r)
    s = jnp.where(take, s_l, s_r)
    mass = jnp.where(take, mass_l, mass_r)
    wave = jnp.where(take, left, right)
    use_star = jnp.where(take, -left, right) > 0.0
    a = jnp.where(use_star, wave * (middle - s) / (wave - middle), 0.0)
    speed = s + a
    push = a * mass
    lift = p + push
    return [
        u[0] * speed,
        u[1] * speed + lift * n[0],
        u[2] * speed + lift * n[1],
        u[3] * speed + lift * n[2],
        (u[4] + p) * speed + push * middle,
        u[5] * speed,
    ]


def two_halves(low, first, second):
    return jnp.where(low, first, swap(second)), jnp.where(low, swap(first), second)


def local_kernel(
    state_ref, mat_ref, metric_ref, count_ref, near_ref, face_ref, deriv_ref, info_ref, proj_ref, code_ref,
    mine_ref, even_ref, odd_ref, base_ref, local_ref, sub_ref, own_ref, scale_ref, hot_ref, back_ref, turn_ref,
):
    info = info_ref[...]
    element, face, sub, orient = (info[i : i + 1] for i in range(4))
    slot = lax.broadcasted_iota(jnp.int32, (1, SLOTS), 1)
    odd = jnp.bitwise_and(lax.axis_index("elem"), 1)
    side = jnp.bitwise_xor(jnp.bitwise_and(lax.shift_right_logical(slot, 5), 1), odd)
    group = jnp.where(slot < 64, lax.shift_right_logical(slot, 3), 8 + side)
    position = jnp.where(slot < 64, jnp.bitwise_and(slot, 7), jnp.bitwise_and(slot, 31))
    limit = jnp.zeros((1, SLOTS), jnp.int32)
    for n in range(10):
        limit = jnp.where(group == n, count_ref[n], limit)
    alive = jnp.where(position < limit, 1.0, 0.0)
    sign = jnp.where(jnp.bitwise_and(face, 1) == 1, 1.0, -1.0)
    axis = lax.shift_right_logical(face, 1)
    codes = code_rows(
        [sub.astype(f32), alive]
        + [jnp.where(axis == d, sign, 0.0) for d in range(3)]
        + [orient.astype(f32), slot_material(mat_ref, element)]
    )
    spread = dot(codes, code_ref[...], 0, 0)
    sub_ref[...] = spread[:, 0:128]
    turn_ref[...] = lane_sources(spread[:, 640:768].astype(jnp.int32), True)
    row = lax.broadcasted_iota(jnp.int32, (48, SLOTS), 0)
    beta = jnp.where(sub == 0, 1.0, 0.25)
    hot = jnp.where(row == 8 * face + element, beta, 0.0).astype(bf16)
    hot_ref[:, 0:128] = hot
    hot_ref[:, 128:256] = hot
    b_hi, b_lo = split2(jnp.concatenate(project_blocks(proj_ref), axis=1))
    back_ref[0:128, :] = b_hi
    back_ref[128:256, :] = b_hi
    back_ref[256:384, :] = b_lo
    heat = 1.4 + 0.27 * by_element(mat_ref, (8, 512))
    u = [state_ref[v] for v in range(6)]
    inv = 1.0 / u[0]
    vel = [u[1] * inv, u[2] * inv, u[3] * inv]
    p = (heat - 1.0) * (u[4] - 0.5 * (u[1] * vel[0] + u[2] * vel[1] + u[3] * vel[2]))
    fluxes = []
    for d in range(3):
        s = vel[d]
        f = [u[0] * s, u[1] * s, u[2] * s, u[3] * s, (u[4] + p) * s, u[5] * s]
        f[1 + d] = f[1 + d] + p
        fluxes.append(f)
    rows = []
    for v in range(6):
        for t in range(4):
            r = slice(128 * t, 128 * t + 128)
            rows.append(jnp.concatenate([fluxes[1][v][:, r], fluxes[2][v][:, r]], axis=1))
    hi, lo = split2(jnp.concatenate(rows, axis=0))
    d_hi, d_lo = deriv_ref[:, 0:128], deriv_ref[:, 128:256]
    main = dot(jnp.concatenate([hi, lo], axis=0), d_hi)
    bc = main[0:192] + main[192:384] + dot(hi, d_lo)
    low = lane_low((8, 128))
    deriv = cheb_matrix()
    scale = STEP * by_element(metric_ref, (8, 128))
    for v in range(6):
        x = [fluxes[0][v][:, 128 * t : 128 * t + 128] for t in range(4)]
        xs = [swap(a) for a in x]
        for t in range(4):
            acc = bc[32 * v + 8 * t : 32 * v + 8 * t + 8]
            for k in range(4):
                same = jnp.where(low, float(deriv[2 * t, 2 * k]), float(deriv[2 * t + 1, 2 * k + 1]))
                cross = jnp.where(low, float(deriv[2 * t, 2 * k + 1]), float(deriv[2 * t + 1, 2 * k]))
                acc = acc + same * x[k] + cross * xs[k]
            r = slice(128 * t, 128 * t + 128)
            base_ref[v, :, r] = u[v][:, r] - scale * acc
    faces = face_ref[...]
    lane = lax.broadcasted_iota(jnp.int32, (8, 256), 1)
    hot, live = [], []
    for k in range(6):
        near = jnp.broadcast_to(near_ref[:, k : k + 1], (8, 256))
        live.append((near >= 0)[:, 0:128])
        target = 8 * (k ^ 1) + near
        hit = (jnp.bitwise_and(lane, 63) == target) & (near >= 0) & (lane < 192)
        hot.append(jnp.where(hit, 1.0, 0.0))
    hot = jnp.concatenate(hot, axis=0).astype(bf16)
    heat_rows = jnp.concatenate([heat[:, 0:128]] * 6, axis=0)
    table = jnp.concatenate([faces[0:48], faces[48:96], faces[96:144], heat_rows], axis=1)
    theirs = dot(hot, stacked(table))
    low = lane_low((48, 128))
    row = lax.broadcasted_iota(jnp.int32, (48, 128), 0)
    sign = jnp.where(jnp.bitwise_and(row, 8) != 0, 1.0, -1.0)
    normal = [jnp.where(lax.shift_right_logical(row, 4) == d, sign, 0.0) for d in range(3)]
    mine, other = [], []
    for j in range(3):
        x, y = faces[48 * j : 48 * j + 48], theirs[:, 128 * j : 128 * j + 128]
        mine += [x, swap(x)]
        other += [y, swap(y)]
    prim = primitives(mine, heat_rows, normal)
    flux = flux_of(mine, prim[0], prim[1], normal)
    through = hllc(mine, other, prim, primitives(other, theirs[:, 384:512], normal), normal)
    corr = [f - h for f, h in zip(flux, through)]
    for j in range(3):
        packed = join_pair(low, corr[2 * j], corr[2 * j + 1])
        for k in range(6):
            local_ref[48 * j + 8 * k : 48 * j + 8 * k + 8, :] = jnp.where(
                live[k], packed[8 * k : 8 * k + 8], 0.0
            )
    low = lane_low((64, 128))

    def rows(at):
        lanes = slice(at, at + 128)
        return (
            jnp.concatenate([mine_ref[g, :, lanes] for g in range(8)], axis=0),
            jnp.concatenate(
                [ref[24 * t + at // 16 : 24 * t + at // 16 + 8, :] for ref in (even_ref, odd_ref) for t in range(4)],
                axis=0,
            ),
        )

    states = []
    for j in range(3):
        states += two_halves(low, *rows(128 * j))
    heat = 1.4 + 0.27 * spread[:, 768:896]
    g = jnp.where(low, heat[0:64], heat[64:128])
    slots = [
        jnp.where(low, spread[0:64, 128 * n : 128 * n + 128], spread[64:128, 128 * n : 128 * n + 128])
        for n in range(1, 5)
    ]
    prim = primitives(states, g, slots[1:])
    kept = [*states, *prim, *flux_of(states, prim[0], prim[1], slots[1:]), *slots]
    for n, x in enumerate(kept):
        own_ref[n] = x
    scale_ref[...] = (STEP * LIFT) * by_element(metric_ref, (8, 128))


def mortar_kernel(
    from_grp_ref, from_even_ref, from_odd_ref, sel_ref,
    base_ref, local_ref, sub_ref, own_ref, scale_ref, hot_ref, back_ref, turn_ref, out_hbm, new_ref, sem,
):
    chunk = 16
    low = lane_low((chunk, 128))
    first, second = [[], [], []], [[], [], []]
    spread = jnp.concatenate(
        [jnp.broadcast_to(from_grp_ref[ROWS * n + 24 : ROWS * n + 25, :], (8, 128)) for n in range(8)], axis=0
    )
    row = lax.broadcasted_iota(jnp.int32, (64, 128), 0)
    lane = lax.broadcasted_iota(jnp.int32, (64, 128), 1)
    spread = jnp.where(lane == 16 * jnp.bitwise_and(row, 7), spread, 0.0).astype(bf16)
    grp_heat = 1.4 + 0.27 * dot(spread, jnp.ones((128, 128), bf16))
    for at in range(0, 64, chunk):
        r = slice(at, at + chunk)

        elem_ref = from_even_ref if at < 32 else from_odd_ref
        blocks = [(at % 32) // 8 + n for n in range(chunk // 8)]

        theirs = []
        for j in range(3):
            starts = [ROWS * (at // 8 + n) + 8 * j for n in range(chunk // 8)]
            grp = jnp.concatenate([from_grp_ref[x : x + 8, :] for x in starts], axis=0)
            elem = jnp.concatenate([elem_ref[24 * t + 8 * j : 24 * t + 8 * j + 8, :] for t in blocks], axis=0)
            theirs += two_halves(low, grp, elem)
        elem_heat = jnp.concatenate(
            [jnp.broadcast_to(elem_ref[96:104, 32 * t : 32 * t + 1], (8, 128)) for t in blocks], axis=0
        )
        g = jnp.where(low, grp_heat[r], elem_heat)
        mine = [own_ref[n, r] for n in range(6)]
        normal = [own_ref[n, r] for n in range(16, 19)]
        live = own_ref[15, r] > 0.5
        prim = tuple(own_ref[n, r] for n in range(6, 9))
        through = hllc(mine, theirs, prim, primitives(theirs, g, normal), normal)
        corr = [jnp.where(live, own_ref[9 + n, r] - through[n], 0.0) for n in range(6)]
        for j in range(3):
            x, y = two_halves(low, corr[2 * j], corr[2 * j + 1])
            first[j].append(x)
            second[j].append(y)
    corr = jnp.concatenate([x for j in range(3) for x in first[j] + second[j]], axis=0)
    hi, lo = split2(corr)
    wide = dot(jnp.concatenate([hi, lo, hi], axis=1), back_ref[...])
    sub_of = sub_ref[...].astype(jnp.int32)
    turn = turn_ref[...]
    back = []
    for j in range(3):
        r = slice(128 * j, 128 * j + 128)
        y = corr[r]
        for s in range(4):
            y = jnp.where(sub_of == s + 1, wide[r, 128 * s : 128 * s + 128], y)
        back.append(reorder(y, turn))
    hi, lo = split2(jnp.concatenate(back, axis=1))
    summed = dot(hot_ref[...], jnp.concatenate([hi, lo], axis=0))
    total = jnp.concatenate([summed[:, 128 * j : 128 * j + 128] for j in range(3)], axis=0) + local_ref[...]
    low = lane_low((8, 128))
    lift = []
    for v in range(6):
        at = 48 * (v // 2)
        parts = []
        for d in range(3):
            first = total[at + 16 * d : at + 16 * d + 8]
            second = total[at + 16 * d + 8 : at + 16 * d + 16]
            if v % 2 == 0:
                parts.append(jnp.where(low, first, swap(second)))
            else:
                parts.append(jnp.where(low, swap(first), second))
        lift.append(parts)
    side = jnp.concatenate(
        [jnp.concatenate([lift[v][1] for v in range(6)], axis=0), jnp.concatenate([lift[v][2] for v in range(6)], axis=0)],
        axis=1,
    )
    hi, lo = split2(side)
    placed = dot(jnp.concatenate([hi, lo], axis=0), sel_ref[...], 1, 1)
    placed = placed[0:48] + placed[48:96]
    scale = scale_ref[...]
    stores = []
    for v in range(6):
        for t in range(4):
            lanes = slice(128 * t, 128 * t + 128)
            value = placed[8 * v : 8 * v + 8, lanes]
            if t == 0:
                value = value + jnp.where(low, lift[v][0], 0.0)
            if t == 3:
                value = value + jnp.where(low, 0.0, lift[v][0])
            new_ref[v, :, lanes] = base_ref[v, :, lanes] + scale * value
        if v % 2 == 1:
            pair = pl.ds(v - 1, 2)
            stores.append(pltpu.make_async_copy(new_ref.at[pair], out_hbm.at[pair], sem.at[v // 2]))
            stores[-1].start()
    for store in stores:
        store.wait()


SM = pl.BlockSpec(memory_space=pltpu.SMEM)
VM = pl.BlockSpec(memory_space=pltpu.VMEM)


def call(kernel, outs, scalars, args, free=()):
    outs = [s if isinstance(s[0], tuple) else (s, f32) for s in outs]
    held = [
        a if n in scalars else pltpu.with_memory_space_constraint(a, pltpu.VMEM)
        for n, a in enumerate(args)
    ]
    return pl.pallas_call(
        kernel,
        out_shape=[jax.ShapeDtypeStruct(*s) if n in free else pltpu.VMEM(*s) for n, s in enumerate(outs)],
        in_specs=[SM if n in scalars else VM for n in range(len(args))],
        out_specs=[VM] * len(outs),
        compiler_params=pltpu.CompilerParams(vmem_limit_bytes=16 << 20),
    )(*held)


def traces(groups, elements, material, info, mortar_proj):
    far = pl.BlockSpec(memory_space=pl.ANY)
    return pl.pallas_call(
        trace_kernel,
        out_shape=[
            jax.ShapeDtypeStruct((groups * ROWS, 128), f32),
            pltpu.VMEM((104, 128), f32),
            pltpu.VMEM((104, 128), f32),
            pltpu.VMEM((144, 128), f32),
            pltpu.VMEM((groups, CAPG, 384), f32),
            pltpu.VMEM((8, SLOTS), jnp.int32),
        ],
        in_specs=[far] * 4,
        out_specs=[far] + [VM] * 5,
        scratch_shapes=[
            pltpu.VMEM((6, 8, 512), f32),
            pltpu.SMEM((8,), jnp.int32),
            pltpu.VMEM((4, SLOTS), jnp.int32),
            pltpu.VMEM((4, 64, 64), f32),
            pltpu.VMEM((512, 512), bf16),
            pltpu.VMEM((groups * ROWS, 128), f32),
            pltpu.SemaphoreType.DMA((4,)),
            pltpu.SemaphoreType.DMA((1,)),
        ],
        name="traces",
        compiler_params=pltpu.CompilerParams(vmem_limit_bytes=16 << 20),
    )(*(pltpu.with_memory_space_constraint(a, pltpu.HBM) for a in (elements, material, info, mortar_proj)))


def section(state, material, metric, mortar_proj, mortar_map, mortar_count, neighbours):
    groups = lax.axis_size("grp")
    n_elem = lax.axis_size("elem")
    elements = jnp.transpose(state, (1, 0, 2))
    info = mortar_map[0]
    counts = mortar_count[0]
    select = jnp.asarray(face_select(), bf16)
    deriv = deriv_table()
    d_hi = deriv.astype(bf16)
    d_lo = (deriv - d_hi.astype(np.float32)).astype(bf16)
    derivs = jnp.asarray(np.concatenate([d_hi, d_lo], axis=1))
    codes_c = jnp.asarray(code_table([{n: 1} for n in range(7)]), bf16)

    grp, even, odd, faces, mine, kept = traces(groups, elements, material, info, mortar_proj)
    swaps = [[(i + n, i + 1 - n) for i in range(first, n_elem - 1, 2) for n in range(2)] for first in range(2)]
    blocks = grp.reshape(groups, ROWS, 1, 128)
    arrived = lax.all_to_all(blocks, "grp", split_axis=0, concat_axis=0, tiled=True).reshape(groups * ROWS, 128)
    from_even = lax.ppermute(even, "elem", swaps[0])
    from_odd = lax.ppermute(odd, "elem", swaps[1])
    held = call(
        local_kernel,
        [
            (6, 8, 512), (144, 128), (SLOTS, 128), (19, 64, 128), (8, 128),
            ((48, 256), bf16), ((384, 512), bf16), ((SLOTS, 128), jnp.int32),
        ],
        {1, 2, 3},
        (
            elements, material, metric, counts, neighbours, faces, derivs, kept, mortar_proj, codes_c,
            mine, even, odd,
        ),
    )
    operands = (arrived, from_even, from_odd, select, *held)
    new = pl.pallas_call(
        mortar_kernel,
        out_shape=jax.ShapeDtypeStruct((6, 8, 512), f32),
        in_specs=[VM] * len(operands),
        out_specs=pl.BlockSpec(memory_space=pl.ANY),
        scratch_shapes=[pltpu.VMEM((6, 8, 512), f32), pltpu.SemaphoreType.DMA((3,))],
        name="mortar",
        compiler_params=pltpu.CompilerParams(vmem_limit_bytes=16 << 20),
    )(*(pltpu.with_memory_space_constraint(a, pltpu.VMEM) for a in operands))
    return jnp.transpose(new, (1, 0, 2))


def solution(mesh):
    return jax.shard_map(
        section,
        mesh=mesh,
        in_specs=(
            P(("elem", "grp"), None, None),
            P(("elem", "grp")),
            P(("elem", "grp")),
            P(),
            P(("elem", "grp"), None, None),
            P(("elem", "grp"), None),
            P(("elem", "grp"), None),
        ),
        out_specs=P(("elem", "grp"), None, None),
        check_vma=False,
    )
```

```python
import jax
import jax.numpy as jnp
import numpy as np
from jax import lax
from jax.experimental import pallas as pl
from jax.experimental.pallas import tpu as pltpu
from jax.sharding import PartitionSpec as P


CAPG = 8
SLOTS = 128
ROWS = 25
STEP = 0.002
LIFT = 49.0

f32 = jnp.float32
bf16 = jnp.bfloat16


def cheb_matrix():
    points = -np.cos(np.pi * np.arange(8) / 7.0)
    factor = np.array([2.0, 1.0, 1.0, 1.0, 1.0, 1.0, 1.0, 2.0])
    alternating = np.where(np.arange(8) % 2 == 0, 1.0, -1.0)
    scaled = factor * alternating
    differ = points[:, None] - points[None, :] + np.eye(8)
    matrix = scaled[:, None] / scaled[None, :] / differ
    matrix = matrix * (1.0 - np.eye(8))
    return (matrix - np.eye(8) * matrix.sum(axis=1)[:, None]).astype(np.float32)


def face_select():
    grid = np.arange(512).reshape(8, 8, 8)
    planes = [grid[:, 0], grid[:, 7], grid[:, :, 0], grid[:, :, 7]]
    nodes = np.concatenate([p.reshape(64) for p in planes])
    return (np.arange(512)[:, None] == nodes[None, :]).astype(np.float32)


def deriv_table():
    d = cheb_matrix()
    along_b = np.kron(np.eye(2), np.kron(d, np.eye(8))).T
    along_c = np.kron(np.eye(16), d).T
    return np.concatenate([along_b, along_c], axis=0).astype(np.float32)


def code_table(rows):
    out = np.zeros((16, 128 * len(rows)), np.float32)
    for block, weights in enumerate(rows):
        for row, weight in weights.items():
            out[row, block * 128 : (block + 1) * 128] = weight
    return out


def dot(a, b, ca=1, cb=0):
    return lax.dot_general(a, b, (((ca,), (cb,)), ((), ())), preferred_element_type=f32)


def split2(x):
    hi = x.astype(bf16)
    return hi, (x - hi.astype(f32)).astype(bf16)


def split3(x):
    hi = x.astype(bf16)
    rest = x - hi.astype(f32)
    mid = rest.astype(bf16)
    return hi, mid, (rest - mid.astype(f32)).astype(bf16)


def lane_low(shape):
    return lax.broadcasted_iota(jnp.int32, shape, len(shape) - 1) % 128 < 64


def swap(x):
    return pltpu.roll(x, 64, 1)


def join_pair(low, a, b):
    return jnp.where(low, a, swap(b))


def by_element(ref, shape):
    row = lax.broadcasted_iota(jnp.int32, shape, 0)
    out = jnp.full(shape, ref[0], f32) if ref.dtype == f32 else jnp.full(shape, ref[0].astype(f32), f32)
    for e in range(1, 8):
        out = jnp.where(row == e, ref[e].astype(f32), out)
    return out


def project_blocks(proj_ref):
    zero = jnp.zeros((64, 64), f32)
    blocks = []
    for s in range(4):
        p = proj_ref[s]
        top = jnp.concatenate([p, zero], axis=1)
        bottom = jnp.concatenate([zero, p], axis=1)
        blocks.append(jnp.concatenate([top, bottom], axis=0))
    return blocks


def slot_material(mat_ref, element):
    out = jnp.zeros(element.shape, f32)
    for e in range(8):
        out = jnp.where(element == e, mat_ref[e].astype(f32), out)
    return out


def code_rows(rows):
    pad = [jnp.zeros((1, SLOTS), f32)] * (16 - len(rows))
    return jnp.concatenate(rows + pad, axis=0).astype(bf16)


def selection():
    lane = lax.broadcasted_iota(jnp.int32, (1, 512), 1)
    far = jnp.bitwise_and(lax.shift_right_logical(lane, 7), 1)
    p = jnp.bitwise_and(lax.shift_right_logical(lane, 3), 7)
    r = jnp.bitwise_and(lane, 7)
    node = 64 * p + jnp.where(lane < 256, r + 56 * far, 8 * r + 7 * far)
    row = lax.broadcasted_iota(jnp.int32, (512, 512), 0)
    return jnp.where(row == node, 1.0, 0.0).astype(bf16)


def lane_sources(orient, back):
    lane = lax.broadcasted_iota(jnp.int32, orient.shape, 1)
    p = jnp.bitwise_and(lax.shift_right_logical(lane, 3), 7)
    r = jnp.bitwise_and(lane, 7)
    turn = jnp.bitwise_and(orient, 4) != 0
    flip_p = jnp.bitwise_and(orient, 1) != 0
    flip_r = jnp.bitwise_and(orient, 2) != 0
    if not back:
        p, r = jnp.where(turn, r, p), jnp.where(turn, p, r)
    p = jnp.where(flip_p, 7 - p, p)
    r = jnp.where(flip_r, 7 - r, r)
    if back:
        p, r = jnp.where(turn, r, p), jnp.where(turn, p, r)
    return jnp.bitwise_and(lane, 64) + 8 * p + r


def reorder(x, source):
    return jnp.take_along_axis(x, source, axis=1, mode="promise_in_bounds")


def stacked(table):
    gap = jnp.zeros((16, table.shape[1]), bf16)
    terms = []
    for term in split3(table):
        terms += [term, gap]
    return jnp.concatenate(terms + [jnp.zeros((64, table.shape[1]), bf16)], axis=0)


def trace_kernel(
    state_hbm, mat_hbm, map_hbm, proj_hbm, grp_hbm, even_ref, odd_ref, face_ref, mine_ref, info_ref,
    state_ref, mat_ref, map_ref, proj_ref, sel_ref, pack_ref, in_sem, out_sem,
):
    def load(src, dst, n):
        copy = pltpu.make_async_copy(src, dst, in_sem.at[n])
        copy.start()
        return copy

    map_load = load(map_hbm, map_ref, 0)
    mat_load = load(mat_hbm, mat_ref, 1)
    state_load = load(state_hbm, state_ref, 2)
    proj_load = load(proj_hbm, proj_ref, 3)
    sel_ref[...] = selection()
    code_row = lax.broadcasted_iota(jnp.int32, (16, 128), 0)
    weights = jnp.where(code_row == 0, 1.0, jnp.where(code_row == 1, 8.0, 0.0))
    spreads = jnp.concatenate([weights] + [jnp.where(code_row == n, 1.0, 0.0) for n in range(2, 5)], axis=1)
    place = lax.broadcasted_iota(jnp.int32, (SLOTS, 128), 0)
    lane = lax.broadcasted_iota(jnp.int32, (SLOTS, 128), 1)
    fan = jnp.where(jnp.bitwise_and(place, 7) == lax.shift_right_logical(lane, 4), 1.0, 0.0).astype(bf16)
    map_load.wait()
    mat_load.wait()
    state_load.wait()
    proj_load.wait()
    info = jnp.concatenate([map_ref[...]] * 2, axis=0)
    slot = lax.broadcasted_iota(jnp.int32, (8, SLOTS), 1)
    turned = jnp.where(slot < 96, pltpu.roll(info, 96, 1), pltpu.roll(info, 32, 1))
    odd = jnp.bitwise_and(lax.axis_index("elem"), 1) == 1
    info = jnp.where((slot >= 64) & odd, turned, info)
    info_ref[...] = info
    element, face, sub, orient = (info[i : i + 1] for i in range(4))
    material = slot_material(mat_ref, element)
    codes = code_rows([element.astype(f32), face.astype(f32), sub.astype(f32), orient.astype(f32), material])
    spread = dot(codes, spreads.astype(bf16), 0, 0)
    index = spread[:, 0:128].astype(jnp.int32)
    sub_of = spread[:, 128:256].astype(jnp.int32)
    source = lane_sources(spread[:, 256:384].astype(jnp.int32), False)
    hit = jnp.bitwise_and(lane, 63) == index
    one_hot = jnp.concatenate(
        [jnp.where(hit, 1.0, 0.0), jnp.where(hit & (lane < 64), 1.0, 0.0)], axis=1
    ).astype(bf16)
    heat = 1.4 + 0.27 * spread[:, 384:512]
    peer = lax.broadcasted_iota(jnp.int32, (8, 128), 0)
    by_peer = jnp.where(lax.shift_right_logical(slot, 3) == peer, material, 0.0)
    heat_rows = dot(by_peer.astype(bf16), fan)
    low = lane_low((8, 128))
    flat = state_ref[...].reshape(48, 512)
    picked = dot(jnp.concatenate(split3(flat), axis=0), sel_ref[...])
    picked = picked[0:48] + picked[48:96] + picked[96:144]
    rows = []
    for j in range(3):
        x, y = state_ref[2 * j], state_ref[2 * j + 1]
        rows.append(jnp.where(low, x[:, 0:128], swap(y[:, 0:128])))
        rows.append(jnp.where(low, swap(x[:, 384:512]), y[:, 384:512]))
        for k in range(4):
            lanes = slice(128 * k, 128 * k + 128)
            rows.append(jnp.where(low, picked[16 * j : 16 * j + 8, lanes], picked[16 * j + 8 : 16 * j + 16, lanes]))
    faces = jnp.concatenate(rows, axis=0)
    face_ref[...] = faces
    gathered = dot(one_hot, stacked(jnp.concatenate([faces[48 * j : 48 * j + 48] for j in range(3)], axis=1)))
    x = [reorder(gathered[:, 128 * j : 128 * j + 128], source) for j in range(3)]
    x = jnp.concatenate([x[j][at : at + 64] for at in (0, 64) for j in range(3)], axis=0)
    b_hi, b_lo = split2(jnp.concatenate(project_blocks(proj_ref), axis=0))
    hi, lo = split2(x)
    wide = dot(jnp.concatenate([hi, lo], axis=1), jnp.concatenate([b_hi, b_hi], axis=1), 1, 1) + dot(hi, b_lo, 1, 1)

    def projected(j, at):
        r = slice(64 * j + 3 * at, 64 * j + 3 * at + 64)
        w = x[r]
        for n in range(4):
            w = jnp.where(sub_of[at : at + 64] == n + 1, wide[r, 128 * n : 128 * n + 128], w)
        return w

    for j in range(3):
        w = projected(j, 0)
        for g in range(8):
            part = w[8 * g : 8 * g + 8]
            mine_ref[g, :, 128 * j : 128 * j + 128] = part
            pack_ref[ROWS * g + 8 * j : ROWS * g + 8 * j + 8, :] = part
    for g in range(8):
        pack_ref[ROWS * g + 24 : ROWS * g + 25, :] = heat_rows[g : g + 1]
    store = pltpu.make_async_copy(pack_ref, grp_hbm, out_sem.at[0])
    store.start()
    for j in range(3):
        w = projected(j, 64)
        for t in range(4):
            even_ref[24 * t + 8 * j : 24 * t + 8 * j + 8, :] = w[8 * t : 8 * t + 8]
            odd_ref[24 * t + 8 * j : 24 * t + 8 * j + 8, :] = w[32 + 8 * t : 40 + 8 * t]
    quarter = lax.shift_right_logical(lax.broadcasted_iota(jnp.int32, (8, 128), 1), 5)
    for ref, at in ((even_ref, 64), (odd_ref, 96)):
        tile = heat[at : at + 8]
        for t in range(1, 4):
            tile = jnp.where(quarter == t, heat[at + 8 * t : at + 8 * t + 8], tile)
        ref[96:104, :] = tile
    store.wait()


def primitives(u, g, n):
    inv = 1.0 / u[0]
    p = (g - 1.0) * (u[4] - 0.5 * inv * (u[1] * u[1] + u[2] * u[2] + u[3] * u[3]))
    s = (n[0] * u[1] + n[1] * u[2] + n[2] * u[3]) * inv
    return p, s, jnp.sqrt(g * p * inv)


def flux_of(u, p, s, n):
    return [u[0] * s, u[1] * s + p * n[0], u[2] * s + p * n[1], u[3] * s + p * n[2], (u[4] + p) * s, u[5] * s]


def hllc(u_l, u_r, prim_l, prim_r, n):
    (p_l, s_l, c_l), (p_r, s_r, c_r) = prim_l, prim_r
    left = jnp.minimum(s_l - c_l, s_r - c_r)
    right = jnp.maximum(s_l + c_l, s_r + c_r)
    mass_l = u_l[0] * (left - s_l)
    mass_r = u_r[0] * (right - s_r)
    middle = (p_r - p_l + mass_l * s_l - mass_r * s_r) / (mass_l - mass_r)
    take = (left >= 0.0) | (middle >= 0.0)
    u = [jnp.where(take, x, y) for x, y in zip(u_l, u_r)]
    p = jnp.where(take, p_l, p_r)
    s = jnp.where(take, s_l, s_r)
    mass = jnp.where(take, mass_l, mass_r)
    wave = jnp.where(take, left, right)
    use_star = jnp.where(take, -left, right) > 0.0
    a = jnp.where(use_star, wave * (middle - s) / (wave - middle), 0.0)
    speed = s + a
    push = a * mass
    lift = p + push
    return [
        u[0] * speed,
        u[1] * speed + lift * n[0],
        u[2] * speed + lift * n[1],
        u[3] * speed + lift * n[2],
        (u[4] + p) * speed + push * middle,
        u[5] * speed,
    ]


def two_halves(low, first, second):
    return jnp.where(low, first, swap(second)), jnp.where(low, swap(first), second)


def local_kernel(
    state_ref, mat_ref, metric_ref, count_ref, near_ref, face_ref, deriv_ref, info_ref, proj_ref, code_ref,
    mine_ref, even_ref, odd_ref, base_ref, local_ref, sub_ref, own_ref, scale_ref, hot_ref, back_ref, turn_ref,
):
    info = info_ref[...]
    element, face, sub, orient = (info[i : i + 1] for i in range(4))
    slot = lax.broadcasted_iota(jnp.int32, (1, SLOTS), 1)
    odd = jnp.bitwise_and(lax.axis_index("elem"), 1)
    side = jnp.bitwise_xor(jnp.bitwise_and(lax.shift_right_logical(slot, 5), 1), odd)
    group = jnp.where(slot < 64, lax.shift_right_logical(slot, 3), 8 + side)
    position = jnp.where(slot < 64, jnp.bitwise_and(slot, 7), jnp.bitwise_and(slot, 31))
    limit = jnp.zeros((1, SLOTS), jnp.int32)
    for n in range(10):
        limit = jnp.where(group == n, count_ref[n], limit)
    alive = jnp.where(position < limit, 1.0, 0.0)
    sign = jnp.where(jnp.bitwise_and(face, 1) == 1, 1.0, -1.0)
    axis = lax.shift_right_logical(face, 1)
    codes = code_rows(
        [sub.astype(f32), alive]
        + [jnp.where(axis == d, sign, 0.0) for d in range(3)]
        + [orient.astype(f32), slot_material(mat_ref, element)]
    )
    spread = dot(codes, code_ref[...], 0, 0)
    sub_ref[...] = spread[:, 0:128]
    turn_ref[...] = lane_sources(spread[:, 640:768].astype(jnp.int32), True)
    row = lax.broadcasted_iota(jnp.int32, (48, SLOTS), 0)
    beta = jnp.where(sub == 0, 1.0, 0.25)
    hot = jnp.where(row == 8 * face + element, beta, 0.0).astype(bf16)
    hot_ref[:, 0:128] = hot
    hot_ref[:, 128:256] = hot
    b_hi, b_lo = split2(jnp.concatenate(project_blocks(proj_ref), axis=1))
    back_ref[0:128, :] = b_hi
    back_ref[128:256, :] = b_hi
    back_ref[256:384, :] = b_lo
    heat = 1.4 + 0.27 * by_element(mat_ref, (8, 512))
    u = [state_ref[v] for v in range(6)]
    inv = 1.0 / u[0]
    vel = [u[1] * inv, u[2] * inv, u[3] * inv]
    p = (heat - 1.0) * (u[4] - 0.5 * (u[1] * vel[0] + u[2] * vel[1] + u[3] * vel[2]))
    fluxes = []
    for d in range(3):
        s = vel[d]
        f = [u[0] * s, u[1] * s, u[2] * s, u[3] * s, (u[4] + p) * s, u[5] * s]
        f[1 + d] = f[1 + d] + p
        fluxes.append(f)
    rows = []
    for v in range(6):
        for t in range(4):
            r = slice(128 * t, 128 * t + 128)
            rows.append(jnp.concatenate([fluxes[1][v][:, r], fluxes[2][v][:, r]], axis=1))
    hi, lo = split2(jnp.concatenate(rows, axis=0))
    d_hi, d_lo = deriv_ref[:, 0:128], deriv_ref[:, 128:256]
    main = dot(jnp.concatenate([hi, lo], axis=0), d_hi)
    bc = main[0:192] + main[192:384] + dot(hi, d_lo)
    low = lane_low((8, 128))
    deriv = cheb_matrix()
    scale = STEP * by_element(metric_ref, (8, 128))
    for v in range(6):
        x = [fluxes[0][v][:, 128 * t : 128 * t + 128] for t in range(4)]
        xs = [swap(a) for a in x]
        for t in range(4):
            acc = bc[32 * v + 8 * t : 32 * v + 8 * t + 8]
            for k in range(4):
                same = jnp.where(low, float(deriv[2 * t, 2 * k]), float(deriv[2 * t + 1, 2 * k + 1]))
                cross = jnp.where(low, float(deriv[2 * t, 2 * k + 1]), float(deriv[2 * t + 1, 2 * k]))
                acc = acc + same * x[k] + cross * xs[k]
            r = slice(128 * t, 128 * t + 128)
            base_ref[v, :, r] = u[v][:, r] - scale * acc
    faces = face_ref[...]
    lane = lax.broadcasted_iota(jnp.int32, (8, 256), 1)
    hot, live = [], []
    for k in range(6):
        near = jnp.broadcast_to(near_ref[:, k : k + 1], (8, 256))
        live.append((near >= 0)[:, 0:128])
        target = 8 * (k ^ 1) + near
        hit = (jnp.bitwise_and(lane, 63) == target) & (near >= 0) & (lane < 192)
        hot.append(jnp.where(hit, 1.0, 0.0))
    hot = jnp.concatenate(hot, axis=0).astype(bf16)
    heat_rows = jnp.concatenate([heat[:, 0:128]] * 6, axis=0)
    table = jnp.concatenate([faces[0:48], faces[48:96], faces[96:144], heat_rows], axis=1)
    theirs = dot(hot, stacked(table))
    low = lane_low((48, 128))
    row = lax.broadcasted_iota(jnp.int32, (48, 128), 0)
    sign = jnp.where(jnp.bitwise_and(row, 8) != 0, 1.0, -1.0)
    normal = [jnp.where(lax.shift_right_logical(row, 4) == d, sign, 0.0) for d in range(3)]
    mine, other = [], []
    for j in range(3):
        x, y = faces[48 * j : 48 * j + 48], theirs[:, 128 * j : 128 * j + 128]
        mine += [x, swap(x)]
        other += [y, swap(y)]
    prim = primitives(mine, heat_rows, normal)
    flux = flux_of(mine, prim[0], prim[1], normal)
    through = hllc(mine, other, prim, primitives(other, theirs[:, 384:512], normal), normal)
    corr = [f - h for f, h in zip(flux, through)]
    for j in range(3):
        packed = join_pair(low, corr[2 * j], corr[2 * j + 1])
        for k in range(6):
            local_ref[48 * j + 8 * k : 48 * j + 8 * k + 8, :] = jnp.where(
                live[k], packed[8 * k : 8 * k + 8], 0.0
            )
    low = lane_low((64, 128))

    def rows(at):
        lanes = slice(at, at + 128)
        return (
            jnp.concatenate([mine_ref[g, :, lanes] for g in range(8)], axis=0),
            jnp.concatenate(
                [ref[24 * t + at // 16 : 24 * t + at // 16 + 8, :] for ref in (even_ref, odd_ref) for t in range(4)],
                axis=0,
            ),
        )

    states = []
    for j in range(3):
        states += two_halves(low, *rows(128 * j))
    heat = 1.4 + 0.27 * spread[:, 768:896]
    g = jnp.where(low, heat[0:64], heat[64:128])
    slots = [
        jnp.where(low, spread[0:64, 128 * n : 128 * n + 128], spread[64:128, 128 * n : 128 * n + 128])
        for n in range(1, 5)
    ]
    prim = primitives(states, g, slots[1:])
    kept = [*states, *prim, *flux_of(states, prim[0], prim[1], slots[1:]), *slots]
    for n, x in enumerate(kept):
        own_ref[n] = x
    scale_ref[...] = (STEP * LIFT) * by_element(metric_ref, (8, 128))


def mortar_kernel(
    from_grp_ref, from_even_ref, from_odd_ref, sel_ref,
    base_ref, local_ref, sub_ref, own_ref, scale_ref, hot_ref, back_ref, turn_ref, out_hbm, new_ref, sem,
):
    chunk = 32
    low = lane_low((chunk, 128))
    first, second = [[], [], []], [[], [], []]
    spread = jnp.concatenate(
        [jnp.broadcast_to(from_grp_ref[ROWS * n + 24 : ROWS * n + 25, :], (8, 128)) for n in range(8)], axis=0
    )
    row = lax.broadcasted_iota(jnp.int32, (64, 128), 0)
    lane = lax.broadcasted_iota(jnp.int32, (64, 128), 1)
    spread = jnp.where(lane == 16 * jnp.bitwise_and(row, 7), spread, 0.0).astype(bf16)
    grp_heat = 1.4 + 0.27 * dot(spread, jnp.ones((128, 128), bf16))
    for at in range(0, 64, chunk):
        r = slice(at, at + chunk)

        elem_ref = from_even_ref if at < 32 else from_odd_ref
        blocks = [(at % 32) // 8 + n for n in range(chunk // 8)]

        theirs = []
        for j in range(3):
            starts = [ROWS * (at // 8 + n) + 8 * j for n in range(chunk // 8)]
            grp = jnp.concatenate([from_grp_ref[x : x + 8, :] for x in starts], axis=0)
            elem = jnp.concatenate([elem_ref[24 * t + 8 * j : 24 * t + 8 * j + 8, :] for t in blocks], axis=0)
            theirs += two_halves(low, grp, elem)
        elem_heat = jnp.concatenate(
            [jnp.broadcast_to(elem_ref[96:104, 32 * t : 32 * t + 1], (8, 128)) for t in blocks], axis=0
        )
        g = jnp.where(low, grp_heat[r], elem_heat)
        mine = [own_ref[n, r] for n in range(6)]
        normal = [own_ref[n, r] for n in range(16, 19)]
        live = own_ref[15, r] > 0.5
        prim = tuple(own_ref[n, r] for n in range(6, 9))
        through = hllc(mine, theirs, prim, primitives(theirs, g, normal), normal)
        corr = [jnp.where(live, own_ref[9 + n, r] - through[n], 0.0) for n in range(6)]
        for j in range(3):
            x, y = two_halves(low, corr[2 * j], corr[2 * j + 1])
            first[j].append(x)
            second[j].append(y)
    corr = jnp.concatenate([x for j in range(3) for x in first[j] + second[j]], axis=0)
    hi, lo = split2(corr)
    wide = dot(jnp.concatenate([hi, lo, hi], axis=1), back_ref[...])
    sub_of = sub_ref[...].astype(jnp.int32)
    turn = turn_ref[...]
    back = []
    for j in range(3):
        r = slice(128 * j, 128 * j + 128)
        y = corr[r]
        for s in range(4):
            y = jnp.where(sub_of == s + 1, wide[r, 128 * s : 128 * s + 128], y)
        back.append(reorder(y, turn))
    hi, lo = split2(jnp.concatenate(back, axis=1))
    summed = dot(hot_ref[...], jnp.concatenate([hi, lo], axis=0))
    total = jnp.concatenate([summed[:, 128 * j : 128 * j + 128] for j in range(3)], axis=0) + local_ref[...]
    low = lane_low((8, 128))
    lift = []
    for v in range(6):
        at = 48 * (v // 2)
        parts = []
        for d in range(3):
            first = total[at + 16 * d : at + 16 * d + 8]
            second = total[at + 16 * d + 8 : at + 16 * d + 16]
            if v % 2 == 0:
                parts.append(jnp.where(low, first, swap(second)))
            else:
                parts.append(jnp.where(low, swap(first), second))
        lift.append(parts)
    side = jnp.concatenate(
        [jnp.concatenate([lift[v][1] for v in range(6)], axis=0), jnp.concatenate([lift[v][2] for v in range(6)], axis=0)],
        axis=1,
    )
    hi, lo = split2(side)
    placed = dot(jnp.concatenate([hi, lo], axis=0), sel_ref[...], 1, 1)
    placed = placed[0:48] + placed[48:96]
    scale = scale_ref[...]
    stores = []
    for v in range(6):
        for t in range(4):
            lanes = slice(128 * t, 128 * t + 128)
            value = placed[8 * v : 8 * v + 8, lanes]
            if t == 0:
                value = value + jnp.where(low, lift[v][0], 0.0)
            if t == 3:
                value = value + jnp.where(low, 0.0, lift[v][0])
            new_ref[v, :, lanes] = base_ref[v, :, lanes] + scale * value
        if v % 2 == 1:
            pair = pl.ds(v - 1, 2)
            stores.append(pltpu.make_async_copy(new_ref.at[pair], out_hbm.at[pair], sem.at[v // 2]))
            stores[-1].start()
    for store in stores:
        store.wait()


SM = pl.BlockSpec(memory_space=pltpu.SMEM)
VM = pl.BlockSpec(memory_space=pltpu.VMEM)


def call(kernel, outs, scalars, args, free=()):
    outs = [s if isinstance(s[0], tuple) else (s, f32) for s in outs]
    held = [
        a if n in scalars else pltpu.with_memory_space_constraint(a, pltpu.VMEM)
        for n, a in enumerate(args)
    ]
    return pl.pallas_call(
        kernel,
        out_shape=[jax.ShapeDtypeStruct(*s) if n in free else pltpu.VMEM(*s) for n, s in enumerate(outs)],
        in_specs=[SM if n in scalars else VM for n in range(len(args))],
        out_specs=[VM] * len(outs),
        compiler_params=pltpu.CompilerParams(vmem_limit_bytes=16 << 20),
    )(*held)


def traces(groups, elements, material, info, mortar_proj):
    far = pl.BlockSpec(memory_space=pl.ANY)
    return pl.pallas_call(
        trace_kernel,
        out_shape=[
            jax.ShapeDtypeStruct((groups * ROWS, 128), f32),
            pltpu.VMEM((104, 128), f32),
            pltpu.VMEM((104, 128), f32),
            pltpu.VMEM((144, 128), f32),
            pltpu.VMEM((groups, CAPG, 384), f32),
            pltpu.VMEM((8, SLOTS), jnp.int32),
        ],
        in_specs=[far] * 4,
        out_specs=[far] + [VM] * 5,
        scratch_shapes=[
            pltpu.VMEM((6, 8, 512), f32),
            pltpu.SMEM((8,), jnp.int32),
            pltpu.VMEM((4, SLOTS), jnp.int32),
            pltpu.VMEM((4, 64, 64), f32),
            pltpu.VMEM((512, 512), bf16),
            pltpu.VMEM((groups * ROWS, 128), f32),
            pltpu.SemaphoreType.DMA((4,)),
            pltpu.SemaphoreType.DMA((1,)),
        ],
        name="traces",
        compiler_params=pltpu.CompilerParams(vmem_limit_bytes=16 << 20),
    )(*(pltpu.with_memory_space_constraint(a, pltpu.HBM) for a in (elements, material, info, mortar_proj)))


def finish(*operands):
    return pl.pallas_call(
        mortar_kernel,
        out_shape=jax.ShapeDtypeStruct((6, 8, 512), f32),
        in_specs=[VM] * len(operands),
        out_specs=pl.BlockSpec(memory_space=pl.ANY),
        scratch_shapes=[pltpu.VMEM((6, 8, 512), f32), pltpu.SemaphoreType.DMA((3,))],
        name="mortar",
        compiler_params=pltpu.CompilerParams(vmem_limit_bytes=16 << 20),
    )(*(pltpu.with_memory_space_constraint(a, pltpu.VMEM) for a in operands))


def section(state, material, metric, mortar_proj, mortar_map, mortar_count, neighbours):
    groups = lax.axis_size("grp")
    n_elem = lax.axis_size("elem")
    elements = jnp.transpose(state, (1, 0, 2))
    info = mortar_map[0]
    counts = mortar_count[0]
    select = jnp.asarray(face_select(), bf16)
    deriv = deriv_table()
    d_hi = deriv.astype(bf16)
    d_lo = (deriv - d_hi.astype(np.float32)).astype(bf16)
    derivs = jnp.asarray(np.concatenate([d_hi, d_lo], axis=1))
    codes_c = jnp.asarray(code_table([{n: 1} for n in range(7)]), bf16)

    grp, even, odd, faces, mine, kept = traces(groups, elements, material, info, mortar_proj)
    swaps = [[(i + n, i + 1 - n) for i in range(first, n_elem - 1, 2) for n in range(2)] for first in range(2)]
    blocks = grp.reshape(groups, ROWS, 1, 128)
    arrived = lax.all_to_all(blocks, "grp", split_axis=0, concat_axis=0, tiled=True).reshape(groups * ROWS, 128)
    from_even = lax.ppermute(even, "elem", swaps[0])
    from_odd = lax.ppermute(odd, "elem", swaps[1])
    held = call(
        local_kernel,
        [
            (6, 8, 512), (144, 128), (SLOTS, 128), (19, 64, 128), (8, 128),
            ((48, 256), bf16), ((384, 512), bf16), ((SLOTS, 128), jnp.int32),
        ],
        {1, 2, 3},
        (
            elements, material, metric, counts, neighbours, faces, derivs, kept, mortar_proj, codes_c,
            mine, even, odd,
        ),
    )
    new = finish(arrived, from_even, from_odd, select, *held)
    return jnp.transpose(new, (1, 0, 2))


def solution(mesh):
    return jax.shard_map(
        section,
        mesh=mesh,
        in_specs=(
            P(("elem", "grp"), None, None),
            P(("elem", "grp")),
            P(("elem", "grp")),
            P(),
            P(("elem", "grp"), None, None),
            P(("elem", "grp"), None),
            P(("elem", "grp"), None),
        ),
        out_specs=P(("elem", "grp"), None, None),
        check_vma=False,
    )
```

```python
import jax
import jax.numpy as jnp
import numpy as np
from jax import lax
from jax.experimental import pallas as pl
from jax.experimental.pallas import tpu as pltpu
from jax.sharding import PartitionSpec as P


CAPG = 8
SLOTS = 128
ROWS = 25
STEP = 0.002
LIFT = 49.0

f32 = jnp.float32
bf16 = jnp.bfloat16


def cheb_matrix():
    points = -np.cos(np.pi * np.arange(8) / 7.0)
    factor = np.array([2.0, 1.0, 1.0, 1.0, 1.0, 1.0, 1.0, 2.0])
    alternating = np.where(np.arange(8) % 2 == 0, 1.0, -1.0)
    scaled = factor * alternating
    differ = points[:, None] - points[None, :] + np.eye(8)
    matrix = scaled[:, None] / scaled[None, :] / differ
    matrix = matrix * (1.0 - np.eye(8))
    return (matrix - np.eye(8) * matrix.sum(axis=1)[:, None]).astype(np.float32)


def face_select():
    grid = np.arange(512).reshape(8, 8, 8)
    planes = [grid[:, 0], grid[:, 7], grid[:, :, 0], grid[:, :, 7]]
    nodes = np.concatenate([p.reshape(64) for p in planes])
    return (np.arange(512)[:, None] == nodes[None, :]).astype(np.float32)


def deriv_table():
    d = cheb_matrix()
    along_b = np.kron(np.eye(2), np.kron(d, np.eye(8))).T
    along_c = np.kron(np.eye(16), d).T
    return np.concatenate([along_b, along_c], axis=0).astype(np.float32)


def code_table(rows):
    out = np.zeros((16, 128 * len(rows)), np.float32)
    for block, weights in enumerate(rows):
        for row, weight in weights.items():
            out[row, block * 128 : (block + 1) * 128] = weight
    return out


def dot(a, b, ca=1, cb=0):
    return lax.dot_general(a, b, (((ca,), (cb,)), ((), ())), preferred_element_type=f32)


def split2(x):
    hi = x.astype(bf16)
    return hi, (x - hi.astype(f32)).astype(bf16)


def split3(x):
    hi = x.astype(bf16)
    rest = x - hi.astype(f32)
    mid = rest.astype(bf16)
    return hi, mid, (rest - mid.astype(f32)).astype(bf16)


def lane_low(shape):
    return lax.broadcasted_iota(jnp.int32, shape, len(shape) - 1) % 128 < 64


def swap(x):
    return pltpu.roll(x, 64, 1)


def join_pair(low, a, b):
    return jnp.where(low, a, swap(b))


def by_element(ref, shape):
    row = lax.broadcasted_iota(jnp.int32, shape, 0)
    out = jnp.full(shape, ref[0], f32) if ref.dtype == f32 else jnp.full(shape, ref[0].astype(f32), f32)
    for e in range(1, 8):
        out = jnp.where(row == e, ref[e].astype(f32), out)
    return out


def project_blocks(proj_ref):
    zero = jnp.zeros((64, 64), f32)
    blocks = []
    for s in range(4):
        p = proj_ref[s]
        top = jnp.concatenate([p, zero], axis=1)
        bottom = jnp.concatenate([zero, p], axis=1)
        blocks.append(jnp.concatenate([top, bottom], axis=0))
    return blocks


def slot_material(mat_ref, element):
    out = jnp.zeros(element.shape, f32)
    for e in range(8):
        out = jnp.where(element == e, mat_ref[e].astype(f32), out)
    return out


def code_rows(rows):
    pad = [jnp.zeros((1, SLOTS), f32)] * (16 - len(rows))
    return jnp.concatenate(rows + pad, axis=0).astype(bf16)


def selection():
    lane = lax.broadcasted_iota(jnp.int32, (1, 512), 1)
    far = jnp.bitwise_and(lax.shift_right_logical(lane, 7), 1)
    p = jnp.bitwise_and(lax.shift_right_logical(lane, 3), 7)
    r = jnp.bitwise_and(lane, 7)
    node = 64 * p + jnp.where(lane < 256, r + 56 * far, 8 * r + 7 * far)
    row = lax.broadcasted_iota(jnp.int32, (512, 512), 0)
    return jnp.where(row == node, 1.0, 0.0).astype(bf16)


def lane_sources(orient, back):
    lane = lax.broadcasted_iota(jnp.int32, orient.shape, 1)
    p = jnp.bitwise_and(lax.shift_right_logical(lane, 3), 7)
    r = jnp.bitwise_and(lane, 7)
    turn = jnp.bitwise_and(orient, 4) != 0
    flip_p = jnp.bitwise_and(orient, 1) != 0
    flip_r = jnp.bitwise_and(orient, 2) != 0
    if not back:
        p, r = jnp.where(turn, r, p), jnp.where(turn, p, r)
    p = jnp.where(flip_p, 7 - p, p)
    r = jnp.where(flip_r, 7 - r, r)
    if back:
        p, r = jnp.where(turn, r, p), jnp.where(turn, p, r)
    return jnp.bitwise_and(lane, 64) + 8 * p + r


def reorder(x, source):
    return jnp.take_along_axis(x, source, axis=1, mode="promise_in_bounds")


def stacked(table):
    gap = jnp.zeros((16, table.shape[1]), bf16)
    terms = []
    for term in split3(table):
        terms += [term, gap]
    return jnp.concatenate(terms + [jnp.zeros((64, table.shape[1]), bf16)], axis=0)


def trace_kernel(
    state_hbm, mat_hbm, map_hbm, proj_hbm, grp_hbm, even_ref, odd_ref, face_ref, mine_ref, info_ref,
    state_ref, mat_ref, map_ref, proj_ref, sel_ref, pack_ref, in_sem, out_sem,
):
    def load(src, dst, n):
        copy = pltpu.make_async_copy(src, dst, in_sem.at[n])
        copy.start()
        return copy

    map_load = load(map_hbm, map_ref, 0)
    mat_load = load(mat_hbm, mat_ref, 1)
    state_load = load(state_hbm, state_ref, 2)
    proj_load = load(proj_hbm, proj_ref, 3)
    sel_ref[...] = selection()
    code_row = lax.broadcasted_iota(jnp.int32, (16, 128), 0)
    weights = jnp.where(code_row == 0, 1.0, jnp.where(code_row == 1, 8.0, 0.0))
    spreads = jnp.concatenate([weights] + [jnp.where(code_row == n, 1.0, 0.0) for n in range(2, 5)], axis=1)
    place = lax.broadcasted_iota(jnp.int32, (SLOTS, 128), 0)
    lane = lax.broadcasted_iota(jnp.int32, (SLOTS, 128), 1)
    fan = jnp.where(jnp.bitwise_and(place, 7) == lax.shift_right_logical(lane, 4), 1.0, 0.0).astype(bf16)
    map_load.wait()
    mat_load.wait()
    state_load.wait()
    proj_load.wait()
    info = jnp.concatenate([map_ref[...]] * 2, axis=0)
    slot = lax.broadcasted_iota(jnp.int32, (8, SLOTS), 1)
    turned = jnp.where(slot < 96, pltpu.roll(info, 96, 1), pltpu.roll(info, 32, 1))
    odd = jnp.bitwise_and(lax.axis_index("elem"), 1) == 1
    info = jnp.where((slot >= 64) & odd, turned, info)
    info_ref[...] = info
    element, face, sub, orient = (info[i : i + 1] for i in range(4))
    material = slot_material(mat_ref, element)
    codes = code_rows([element.astype(f32), face.astype(f32), sub.astype(f32), orient.astype(f32), material])
    spread = dot(codes, spreads.astype(bf16), 0, 0)
    index = spread[:, 0:128].astype(jnp.int32)
    sub_of = spread[:, 128:256].astype(jnp.int32)
    source = lane_sources(spread[:, 256:384].astype(jnp.int32), False)
    hit = jnp.bitwise_and(lane, 63) == index
    one_hot = jnp.concatenate(
        [jnp.where(hit, 1.0, 0.0), jnp.where(hit & (lane < 64), 1.0, 0.0)], axis=1
    ).astype(bf16)
    heat = 1.4 + 0.27 * spread[:, 384:512]
    peer = lax.broadcasted_iota(jnp.int32, (8, 128), 0)
    by_peer = jnp.where(lax.shift_right_logical(slot, 3) == peer, material, 0.0)
    heat_rows = dot(by_peer.astype(bf16), fan)
    low = lane_low((8, 128))
    flat = state_ref[...].reshape(48, 512)
    picked = dot(jnp.concatenate(split3(flat), axis=0), sel_ref[...])
    picked = picked[0:48] + picked[48:96] + picked[96:144]
    rows = []
    for j in range(3):
        x, y = state_ref[2 * j], state_ref[2 * j + 1]
        rows.append(jnp.where(low, x[:, 0:128], swap(y[:, 0:128])))
        rows.append(jnp.where(low, swap(x[:, 384:512]), y[:, 384:512]))
        for k in range(4):
            lanes = slice(128 * k, 128 * k + 128)
            rows.append(jnp.where(low, picked[16 * j : 16 * j + 8, lanes], picked[16 * j + 8 : 16 * j + 16, lanes]))
    faces = jnp.concatenate(rows, axis=0)
    face_ref[...] = faces
    gathered = dot(one_hot, stacked(jnp.concatenate([faces[48 * j : 48 * j + 48] for j in range(3)], axis=1)))
    x = [reorder(gathered[:, 128 * j : 128 * j + 128], source) for j in range(3)]
    x = jnp.concatenate([x[j][at : at + 64] for at in (0, 64) for j in range(3)], axis=0)
    b_hi, b_lo = split2(jnp.concatenate(project_blocks(proj_ref), axis=0))
    hi, lo = split2(x)
    wide = dot(jnp.concatenate([hi, lo], axis=1), jnp.concatenate([b_hi, b_hi], axis=1), 1, 1) + dot(hi, b_lo, 1, 1)

    def projected(j, at):
        r = slice(64 * j + 3 * at, 64 * j + 3 * at + 64)
        w = x[r]
        for n in range(4):
            w = jnp.where(sub_of[at : at + 64] == n + 1, wide[r, 128 * n : 128 * n + 128], w)
        return w

    for j in range(3):
        w = projected(j, 0)
        for g in range(8):
            part = w[8 * g : 8 * g + 8]
            mine_ref[g, :, 128 * j : 128 * j + 128] = part
            pack_ref[ROWS * g + 8 * j : ROWS * g + 8 * j + 8, :] = part
    for g in range(8):
        pack_ref[ROWS * g + 24 : ROWS * g + 25, :] = heat_rows[g : g + 1]
    store = pltpu.make_async_copy(pack_ref, grp_hbm, out_sem.at[0])
    store.start()
    for j in range(3):
        w = projected(j, 64)
        for t in range(4):
            even_ref[24 * t + 8 * j : 24 * t + 8 * j + 8, :] = w[8 * t : 8 * t + 8]
            odd_ref[24 * t + 8 * j : 24 * t + 8 * j + 8, :] = w[32 + 8 * t : 40 + 8 * t]
    quarter = lax.shift_right_logical(lax.broadcasted_iota(jnp.int32, (8, 128), 1), 5)
    for ref, at in ((even_ref, 64), (odd_ref, 96)):
        tile = heat[at : at + 8]
        for t in range(1, 4):
            tile = jnp.where(quarter == t, heat[at + 8 * t : at + 8 * t + 8], tile)
        ref[96:104, :] = tile
    store.wait()


def primitives(u, g, n):
    inv = 1.0 / u[0]
    p = (g - 1.0) * (u[4] - 0.5 * inv * (u[1] * u[1] + u[2] * u[2] + u[3] * u[3]))
    s = (n[0] * u[1] + n[1] * u[2] + n[2] * u[3]) * inv
    return p, s, jnp.sqrt(g * p * inv)


def flux_of(u, p, s, n):
    return [u[0] * s, u[1] * s + p * n[0], u[2] * s + p * n[1], u[3] * s + p * n[2], (u[4] + p) * s, u[5] * s]


def hllc(u_l, u_r, prim_l, prim_r, n):
    (p_l, s_l, c_l), (p_r, s_r, c_r) = prim_l, prim_r
    left = jnp.minimum(s_l - c_l, s_r - c_r)
    right = jnp.maximum(s_l + c_l, s_r + c_r)
    mass_l = u_l[0] * (left - s_l)
    mass_r = u_r[0] * (right - s_r)
    middle = (p_r - p_l + mass_l * s_l - mass_r * s_r) / (mass_l - mass_r)
    take = (left >= 0.0) | (middle >= 0.0)
    u = [jnp.where(take, x, y) for x, y in zip(u_l, u_r)]
    p = jnp.where(take, p_l, p_r)
    s = jnp.where(take, s_l, s_r)
    mass = jnp.where(take, mass_l, mass_r)
    wave = jnp.where(take, left, right)
    use_star = jnp.where(take, -left, right) > 0.0
    a = jnp.where(use_star, wave * (middle - s) / (wave - middle), 0.0)
    speed = s + a
    push = a * mass
    lift = p + push
    return [
        u[0] * speed,
        u[1] * speed + lift * n[0],
        u[2] * speed + lift * n[1],
        u[3] * speed + lift * n[2],
        (u[4] + p) * speed + push * middle,
        u[5] * speed,
    ]


def two_halves(low, first, second):
    return jnp.where(low, first, swap(second)), jnp.where(low, swap(first), second)


def local_kernel(
    state_ref, mat_ref, metric_ref, count_ref, near_ref, face_ref, deriv_ref, info_ref, proj_ref, code_ref,
    mine_ref, even_ref, odd_ref, base_ref, local_ref, sub_ref, own_ref, scale_ref, hot_ref, back_ref, turn_ref,
):
    info = info_ref[...]
    element, face, sub, orient = (info[i : i + 1] for i in range(4))
    slot = lax.broadcasted_iota(jnp.int32, (1, SLOTS), 1)
    odd = jnp.bitwise_and(lax.axis_index("elem"), 1)
    side = jnp.bitwise_xor(jnp.bitwise_and(lax.shift_right_logical(slot, 5), 1), odd)
    group = jnp.where(slot < 64, lax.shift_right_logical(slot, 3), 8 + side)
    position = jnp.where(slot < 64, jnp.bitwise_and(slot, 7), jnp.bitwise_and(slot, 31))
    limit = jnp.zeros((1, SLOTS), jnp.int32)
    for n in range(10):
        limit = jnp.where(group == n, count_ref[n], limit)
    alive = jnp.where(position < limit, 1.0, 0.0)
    sign = jnp.where(jnp.bitwise_and(face, 1) == 1, 1.0, -1.0)
    axis = lax.shift_right_logical(face, 1)
    codes = code_rows(
        [sub.astype(f32), alive]
        + [jnp.where(axis == d, sign, 0.0) for d in range(3)]
        + [orient.astype(f32), slot_material(mat_ref, element)]
    )
    spread = dot(codes, code_ref[...], 0, 0)
    sub_ref[...] = spread[:, 0:128]
    turn_ref[...] = lane_sources(spread[:, 640:768].astype(jnp.int32), True)
    row = lax.broadcasted_iota(jnp.int32, (48, SLOTS), 0)
    beta = jnp.where(sub == 0, 1.0, 0.25)
    hot = jnp.where(row == 8 * face + element, beta, 0.0).astype(bf16)
    hot_ref[:, 0:128] = hot
    hot_ref[:, 128:256] = hot
    b_hi, b_lo = split2(jnp.concatenate(project_blocks(proj_ref), axis=1))
    back_ref[0:128, :] = b_hi
    back_ref[128:256, :] = b_hi
    back_ref[256:384, :] = b_lo
    heat = 1.4 + 0.27 * by_element(mat_ref, (8, 512))
    u = [state_ref[v] for v in range(6)]
    inv = 1.0 / u[0]
    vel = [u[1] * inv, u[2] * inv, u[3] * inv]
    p = (heat - 1.0) * (u[4] - 0.5 * (u[1] * vel[0] + u[2] * vel[1] + u[3] * vel[2]))
    fluxes = []
    for d in range(3):
        s = vel[d]
        f = [u[0] * s, u[1] * s, u[2] * s, u[3] * s, (u[4] + p) * s, u[5] * s]
        f[1 + d] = f[1 + d] + p
        fluxes.append(f)
    rows = []
    for v in range(6):
        for t in range(4):
            r = slice(128 * t, 128 * t + 128)
            rows.append(jnp.concatenate([fluxes[1][v][:, r], fluxes[2][v][:, r]], axis=1))
    hi, lo = split2(jnp.concatenate(rows, axis=0))
    d_hi, d_lo = deriv_ref[:, 0:128], deriv_ref[:, 128:256]
    main = dot(jnp.concatenate([hi, lo], axis=0), d_hi)
    bc = main[0:192] + main[192:384] + dot(hi, d_lo)
    low = lane_low((8, 128))
    deriv = cheb_matrix()
    scale = STEP * by_element(metric_ref, (8, 128))
    for v in range(6):
        x = [fluxes[0][v][:, 128 * t : 128 * t + 128] for t in range(4)]
        xs = [swap(a) for a in x]
        for t in range(4):
            acc = bc[32 * v + 8 * t : 32 * v + 8 * t + 8]
            for k in range(4):
                same = jnp.where(low, float(deriv[2 * t, 2 * k]), float(deriv[2 * t + 1, 2 * k + 1]))
                cross = jnp.where(low, float(deriv[2 * t, 2 * k + 1]), float(deriv[2 * t + 1, 2 * k]))
                acc = acc + same * x[k] + cross * xs[k]
            r = slice(128 * t, 128 * t + 128)
            base_ref[v, :, r] = u[v][:, r] - scale * acc
    faces = face_ref[...]
    lane = lax.broadcasted_iota(jnp.int32, (8, 256), 1)
    hot, live = [], []
    for k in range(6):
        near = jnp.broadcast_to(near_ref[:, k : k + 1], (8, 256))
        live.append((near >= 0)[:, 0:128])
        target = 8 * (k ^ 1) + near
        hit = (jnp.bitwise_and(lane, 63) == target) & (near >= 0) & (lane < 192)
        hot.append(jnp.where(hit, 1.0, 0.0))
    hot = jnp.concatenate(hot, axis=0).astype(bf16)
    heat_rows = jnp.concatenate([heat[:, 0:128]] * 6, axis=0)
    table = jnp.concatenate([faces[0:48], faces[48:96], faces[96:144], heat_rows], axis=1)
    theirs = dot(hot, stacked(table))
    low = lane_low((48, 128))
    row = lax.broadcasted_iota(jnp.int32, (48, 128), 0)
    sign = jnp.where(jnp.bitwise_and(row, 8) != 0, 1.0, -1.0)
    normal = [jnp.where(lax.shift_right_logical(row, 4) == d, sign, 0.0) for d in range(3)]
    mine, other = [], []
    for j in range(3):
        x, y = faces[48 * j : 48 * j + 48], theirs[:, 128 * j : 128 * j + 128]
        mine += [x, swap(x)]
        other += [y, swap(y)]
    prim = primitives(mine, heat_rows, normal)
    flux = flux_of(mine, prim[0], prim[1], normal)
    through = hllc(mine, other, prim, primitives(other, theirs[:, 384:512], normal), normal)
    corr = [f - h for f, h in zip(flux, through)]
    for j in range(3):
        packed = join_pair(low, corr[2 * j], corr[2 * j + 1])
        for k in range(6):
            local_ref[48 * j + 8 * k : 48 * j + 8 * k + 8, :] = jnp.where(
                live[k], packed[8 * k : 8 * k + 8], 0.0
            )
    low = lane_low((64, 128))

    def rows(at):
        lanes = slice(at, at + 128)
        return (
            jnp.concatenate([mine_ref[g, :, lanes] for g in range(8)], axis=0),
            jnp.concatenate(
                [ref[24 * t + at // 16 : 24 * t + at // 16 + 8, :] for ref in (even_ref, odd_ref) for t in range(4)],
                axis=0,
            ),
        )

    states = []
    for j in range(3):
        states += two_halves(low, *rows(128 * j))
    heat = 1.4 + 0.27 * spread[:, 768:896]
    g = jnp.where(low, heat[0:64], heat[64:128])
    slots = [
        jnp.where(low, spread[0:64, 128 * n : 128 * n + 128], spread[64:128, 128 * n : 128 * n + 128])
        for n in range(1, 5)
    ]
    prim = primitives(states, g, slots[1:])
    kept = [*states, *prim, *flux_of(states, prim[0], prim[1], slots[1:]), *slots]
    for n, x in enumerate(kept):
        own_ref[n] = x
    scale_ref[...] = (STEP * LIFT) * by_element(metric_ref, (8, 128))


def mortar_kernel(
    from_grp_ref, from_even_ref, from_late_ref, from_odd_ref, sel_ref,
    base_ref, local_ref, sub_ref, own_ref, scale_ref, hot_ref, back_ref, turn_ref, out_hbm, new_ref, sem,
):
    chunk = 32
    low = lane_low((chunk, 128))
    first, second = [[], [], []], [[], [], []]
    spread = jnp.concatenate(
        [jnp.broadcast_to(from_grp_ref[ROWS * n + 24 : ROWS * n + 25, :], (8, 128)) for n in range(8)], axis=0
    )
    row = lax.broadcasted_iota(jnp.int32, (64, 128), 0)
    lane = lax.broadcasted_iota(jnp.int32, (64, 128), 1)
    spread = jnp.where(lane == 16 * jnp.bitwise_and(row, 7), spread, 0.0).astype(bf16)
    grp_heat = 1.4 + 0.27 * dot(spread, jnp.ones((128, 128), bf16))
    for at in range(0, 64, chunk):
        r = slice(at, at + chunk)


        def from_elem(x):
            if at < 32:
                return from_even_ref[x : x + 8, :] + from_late_ref[x : x + 8, :]
            return from_odd_ref[x : x + 8, :]

        blocks = [(at % 32) // 8 + n for n in range(chunk // 8)]

        theirs = []
        for j in range(3):
            starts = [ROWS * (at // 8 + n) + 8 * j for n in range(chunk // 8)]
            grp = jnp.concatenate([from_grp_ref[x : x + 8, :] for x in starts], axis=0)
            elem = jnp.concatenate([from_elem(24 * t + 8 * j) for t in blocks], axis=0)
            theirs += two_halves(low, grp, elem)
        heats = from_elem(96)
        elem_heat = jnp.concatenate(
            [jnp.broadcast_to(heats[:, 32 * t : 32 * t + 1], (8, 128)) for t in blocks], axis=0
        )
        g = jnp.where(low, grp_heat[r], elem_heat)
        mine = [own_ref[n, r] for n in range(6)]
        normal = [own_ref[n, r] for n in range(16, 19)]
        live = own_ref[15, r] > 0.5
        prim = tuple(own_ref[n, r] for n in range(6, 9))
        through = hllc(mine, theirs, prim, primitives(theirs, g, normal), normal)
        corr = [jnp.where(live, own_ref[9 + n, r] - through[n], 0.0) for n in range(6)]
        for j in range(3):
            x, y = two_halves(low, corr[2 * j], corr[2 * j + 1])
            first[j].append(x)
            second[j].append(y)
    corr = jnp.concatenate([x for j in range(3) for x in first[j] + second[j]], axis=0)
    hi, lo = split2(corr)
    wide = dot(jnp.concatenate([hi, lo, hi], axis=1), back_ref[...])
    sub_of = sub_ref[...].astype(jnp.int32)
    turn = turn_ref[...]
    back = []
    for j in range(3):
        r = slice(128 * j, 128 * j + 128)
        y = corr[r]
        for s in range(4):
            y = jnp.where(sub_of == s + 1, wide[r, 128 * s : 128 * s + 128], y)
        back.append(reorder(y, turn))
    hi, lo = split2(jnp.concatenate(back, axis=1))
    summed = dot(hot_ref[...], jnp.concatenate([hi, lo], axis=0))
    total = jnp.concatenate([summed[:, 128 * j : 128 * j + 128] for j in range(3)], axis=0) + local_ref[...]
    low = lane_low((8, 128))
    lift = []
    for v in range(6):
        at = 48 * (v // 2)
        parts = []
        for d in range(3):
            first = total[at + 16 * d : at + 16 * d + 8]
            second = total[at + 16 * d + 8 : at + 16 * d + 16]
            if v % 2 == 0:
                parts.append(jnp.where(low, first, swap(second)))
            else:
                parts.append(jnp.where(low, swap(first), second))
        lift.append(parts)
    side = jnp.concatenate(
        [jnp.concatenate([lift[v][1] for v in range(6)], axis=0), jnp.concatenate([lift[v][2] for v in range(6)], axis=0)],
        axis=1,
    )
    hi, lo = split2(side)
    placed = dot(jnp.concatenate([hi, lo], axis=0), sel_ref[...], 1, 1)
    placed = placed[0:48] + placed[48:96]
    scale = scale_ref[...]
    stores = []
    for v in range(6):
        for t in range(4):
            lanes = slice(128 * t, 128 * t + 128)
            value = placed[8 * v : 8 * v + 8, lanes]
            if t == 0:
                value = value + jnp.where(low, lift[v][0], 0.0)
            if t == 3:
                value = value + jnp.where(low, 0.0, lift[v][0])
            new_ref[v, :, lanes] = base_ref[v, :, lanes] + scale * value
        if v % 2 == 1:
            pair = pl.ds(v - 1, 2)
            stores.append(pltpu.make_async_copy(new_ref.at[pair], out_hbm.at[pair], sem.at[v // 2]))
            stores[-1].start()
    for store in stores:
        store.wait()


SM = pl.BlockSpec(memory_space=pltpu.SMEM)
VM = pl.BlockSpec(memory_space=pltpu.VMEM)


def call(kernel, outs, scalars, args, free=()):
    outs = [s if isinstance(s[0], tuple) else (s, f32) for s in outs]
    held = [
        a if n in scalars else pltpu.with_memory_space_constraint(a, pltpu.VMEM)
        for n, a in enumerate(args)
    ]
    return pl.pallas_call(
        kernel,
        out_shape=[jax.ShapeDtypeStruct(*s) if n in free else pltpu.VMEM(*s) for n, s in enumerate(outs)],
        in_specs=[SM if n in scalars else VM for n in range(len(args))],
        out_specs=[VM] * len(outs),
        compiler_params=pltpu.CompilerParams(vmem_limit_bytes=16 << 20),
    )(*held)


def traces(groups, elements, material, info, mortar_proj):
    far = pl.BlockSpec(memory_space=pl.ANY)
    return pl.pallas_call(
        trace_kernel,
        out_shape=[
            jax.ShapeDtypeStruct((groups * ROWS, 128), f32),
            pltpu.VMEM((104, 128), f32),
            pltpu.VMEM((104, 128), f32),
            pltpu.VMEM((144, 128), f32),
            pltpu.VMEM((groups, CAPG, 384), f32),
            pltpu.VMEM((8, SLOTS), jnp.int32),
        ],
        in_specs=[far] * 4,
        out_specs=[far] + [VM] * 5,
        scratch_shapes=[
            pltpu.VMEM((6, 8, 512), f32),
            pltpu.SMEM((8,), jnp.int32),
            pltpu.VMEM((4, SLOTS), jnp.int32),
            pltpu.VMEM((4, 64, 64), f32),
            pltpu.VMEM((512, 512), bf16),
            pltpu.VMEM((groups * ROWS, 128), f32),
            pltpu.SemaphoreType.DMA((4,)),
            pltpu.SemaphoreType.DMA((1,)),
        ],
        name="traces",
        compiler_params=pltpu.CompilerParams(vmem_limit_bytes=16 << 20),
    )(*(pltpu.with_memory_space_constraint(a, pltpu.HBM) for a in (elements, material, info, mortar_proj)))


def finish(*operands):
    return pl.pallas_call(
        mortar_kernel,
        out_shape=jax.ShapeDtypeStruct((6, 8, 512), f32),
        in_specs=[VM] * len(operands),
        out_specs=pl.BlockSpec(memory_space=pl.ANY),
        scratch_shapes=[pltpu.VMEM((6, 8, 512), f32), pltpu.SemaphoreType.DMA((3,))],
        name="mortar",
        compiler_params=pltpu.CompilerParams(vmem_limit_bytes=16 << 20),
    )(*(pltpu.with_memory_space_constraint(a, pltpu.VMEM) for a in operands))


def section(state, material, metric, mortar_proj, mortar_map, mortar_count, neighbours):
    groups = lax.axis_size("grp")
    n_elem = lax.axis_size("elem")
    elements = jnp.transpose(state, (1, 0, 2))
    info = mortar_map[0]
    counts = mortar_count[0]
    select = jnp.asarray(face_select(), bf16)
    deriv = deriv_table()
    d_hi = deriv.astype(bf16)
    d_lo = (deriv - d_hi.astype(np.float32)).astype(bf16)
    derivs = jnp.asarray(np.concatenate([d_hi, d_lo], axis=1))
    codes_c = jnp.asarray(code_table([{n: 1} for n in range(7)]), bf16)

    grp, even, odd, faces, mine, kept = traces(groups, elements, material, info, mortar_proj)
    swaps = [
        [((i + n) * groups + g, (i + 1 - n) * groups + g) for i in range(first, n_elem - 1, 2) for g in range(groups) for n in range(2)]
        for first in range(2)
    ]
    late = [(0, groups), (groups, 0)]
    axes = ("elem", "grp")
    from_even = lax.ppermute(even, axes, [pair for pair in swaps[0] if pair not in late])
    blocks = grp.reshape(groups, ROWS, 1, 128)
    arrived = lax.all_to_all(blocks, "grp", split_axis=0, concat_axis=0, tiled=True).reshape(groups * ROWS, 128)
    from_odd = lax.ppermute(odd, axes, swaps[1])
    from_late = lax.ppermute(even, axes, late)
    held = call(
        local_kernel,
        [
            (6, 8, 512), (144, 128), (SLOTS, 128), (19, 64, 128), (8, 128),
            ((48, 256), bf16), ((384, 512), bf16), ((SLOTS, 128), jnp.int32),
        ],
        {1, 2, 3},
        (
            elements, material, metric, counts, neighbours, faces, derivs, kept, mortar_proj, codes_c,
            mine, even, odd,
        ),
    )
    new = finish(arrived, from_even, from_late, from_odd, select, *held)
    return jnp.transpose(new, (1, 0, 2))


def solution(mesh):
    return jax.shard_map(
        section,
        mesh=mesh,
        in_specs=(
            P(("elem", "grp"), None, None),
            P(("elem", "grp")),
            P(("elem", "grp")),
            P(),
            P(("elem", "grp"), None, None),
            P(("elem", "grp"), None),
            P(("elem", "grp"), None),
        ),
        out_specs=P(("elem", "grp"), None, None),
        check_vma=False,
    )
```
